256 devices in a mesh: comp: 2 (over core), lat: 16 (over y, z_lo), lon: 8 (over z_hi, x).
Axes of the slice: x: 4, y: 4, z: 8 (z_hi: 2, z_lo: 4; z = z_hi * 4 + z_lo), core: 2. Of those that a mesh axis runs over, the one named last changes fastest.
Arguments:
- innovations: float32 [2, 3, 16384, 512], P('comp', None, ('lat', 'lon')), may hold values from -6 to 6
- obs_owner: int32 [2, 3, 16384, 1], P('comp', None, ('lat', 'lon')), may hold values from 0 to 127; in each aligned block of 128 rows (0 to 127, 128 to 255, ..., all dimensions but the last counted through in order) at most 2 rows name the same one
- obs_cell: int32 [2, 3, 16384], P('comp', None, ('lat', 'lon')), may hold values from 0 to 1023
- velocity: float32 [2, 3, 2, 128, 128, 1024], P('comp', None, None, None, 'lat', 'lon'), may hold values from -0.2 to 0.2
- diffusion: float32 [2, 3, 2, 128, 128, 1024], P('comp', None, None, None, 'lat', 'lon'), may hold values from 0.01 to 0.08
- mixing: float32 [2, 4, 4], P('comp'), may hold values from -0.15 to 0.15
- air_sea: float32 [4, 4], replicated, may hold values from -1 to 1
- sea_mask: int32 [128, 1024], P('lat', 'lon'), may hold values 0 or 1
Outputs:
- gradient: float32 [2, 4, 128, 128, 1024], P('comp', None, None, 'lat', 'lon')
The draws below stay inside these ranges and needn't reach their ends.
Inputs may be any that keep to these rules, and one draw needn't show every extreme that they name: `obs_owner`: among the 128 rows of one device for one section and timestep, no owner is named more than 2 times, a bound that some block reaches.
All inputs are finite; a program needn't handle non-finite values. No bound on the sum of `sea_mask` on one device may be relied on, other than what follows from the above.
Results may differ from the reference program's by a relative error of at most 0.0001.
Values sent between devices are 32-bit elements; how exact they have to be, the bound alone decides.
No kernel may reach another device: no remote copies, remote signals or barrier semaphores. Data moves between devices by JAX's collectives and lax.ppermute only.
A program may use at most 320 MiB of HBM per device.

```python
import math
import jax
import jax.numpy as jnp
import numpy as np
from jax import lax

FIELDS = 4
LEV = 128
STEPS = 3
CLAT = 8
CLON = 128
OBS_DEV = 128
CAP = 2
NLAT = 128
NLON = 1024
N_LAT = 16
N_LON = 8


def touch_ends(values, key, low, largest):
    extent = values.shape
    spot = [jax.random.randint(jax.random.fold_in(key, axis), (), 0, extent[axis]) for axis in range(len(extent))]
    values = values.at[tuple(spot)].set(low)
    longest = extent.index(max(extent))
    spot[longest] = (spot[longest] + 1) % extent[longest]
    return values.at[tuple(spot)].set(largest)


def block_levels(rng, shape, shards, least, largest):
    loudness = 1.0
    for dim, shards_of in shards:
        heights = jax.random.uniform(jax.random.fold_in(jax.random.fold_in(rng, 6), dim), (shards_of,), jnp.float32, least / len(shards), largest / len(shards))
        loudness = loudness * jnp.repeat(jnp.exp(heights), shape[dim] // shards_of).reshape((-1,) + (1,) * (len(shape) - 1 - dim))
    return loudness


def shared_out(stream_key, own, number, rows, count, top, most, lean):
    sequence = jax.random.permutation(stream_key, count)
    crowded, common = shares(count, rows * top, most, lean, True), shares(count, rows * top, most, lean, False)
    places = jnp.arange(count)

    def named(tallies, turn):
        used = int((tallies > 0).sum())
        fixed = max(1, used // 4)
        moved = fixed + (places - fixed + turn * (used - fixed)) % max(1, count - fixed)
        return jnp.zeros((count,), jnp.int32).at[sequence[jnp.where(places < fixed, places, moved)]].set(jnp.asarray(tallies, jnp.int32))

    tallies = jnp.where(number % 4 == 0, named(crowded, number // 4), named(common, number - number // 4 - 1))
    mixed = jax.random.permutation(jax.random.fold_in(own, 3), count)
    source_of, taker = mixed[0:count // 2 * 2:2], mixed[1:count // 2 * 2:2]
    slack = jnp.minimum(tallies[source_of] - 1, most - tallies[taker]) // 2
    slack = jnp.where((source_of == sequence[0]) | (taker == sequence[0]) | (tallies[taker] == 0), 0, jnp.maximum(slack, 0))
    moved = jax.random.randint(jax.random.fold_in(own, 4), (count // 2,), 0, 1 << 20) % (slack + 1)
    tallies = tallies.at[source_of].add(-moved).at[taker].add(moved)
    members = jnp.searchsorted(jnp.cumsum(tallies), jnp.arange(rows * top), side="right").astype(jnp.int32)
    listing = members.reshape(top, rows).T
    listing = listing[jax.random.permutation(jax.random.fold_in(own, 1), rows)]
    turn = jax.random.randint(jax.random.fold_in(own, 2), (rows, 1), 0, top)
    return jnp.take_along_axis(listing, (jnp.arange(top)[None, :] + turn) % top, axis=1)


def shares(count, total, limit, lean, full):
    weights = [(1 << 20) // math.isqrt(grade ** lean) + 1 for grade in range(1, count + 1)]
    largest = limit if full else min(limit, max(-(-total // count), total * weights[0] // sum(weights)))
    least = 1 if total - largest >= count - 1 else 0
    holding, rest = [largest] + [least] * (count - 1), total - largest - least * (count - 1)
    while rest > 0:
        candidates = [i for i in range(1, count) if holding[i] < largest] or [i for i in range(1, count) if holding[i] < limit]
        mass, left = sum([weights[i] for i in candidates]), rest
        for i in candidates:
            more = min(limit - holding[i], max(1, left * weights[i] // mass), rest)
            holding[i] = holding[i] + more
            rest = rest - more
    return np.array(holding)


def bell_draw(own_key, extent, deviation, limit, shards=(), kind=jnp.bfloat16):
    gain = block_levels(own_key, extent, shards, -0.22, 0.18) if shards else 1.0
    drawn = jax.random.normal(own_key, extent, jnp.float32) * deviation * gain
    return jnp.minimum(jnp.maximum(drawn, -limit), limit).astype(kind)


def setup_inputs(seed: int = 0) -> dict:
    keys = jax.random.split(jax.random.key(seed), 9)
    innovations = bell_draw(keys[0], (2, STEPS, N_LAT * N_LON * OBS_DEV, FIELDS * LEV), 1.0, 6.0, ((0, 2), (2, 128)), jnp.float32)
    obs_owner_keys = jax.random.split(jax.random.fold_in(keys[1], 1), 2 * STEPS * (N_LAT * N_LON * OBS_DEV) // OBS_DEV)
    obs_owner_turns = jax.random.permutation(jax.random.fold_in(keys[1], 3), 2 * STEPS * (N_LAT * N_LON * OBS_DEV) // OBS_DEV)
    obs_owner = jax.vmap(lambda own, number: shared_out(jax.random.fold_in(keys[1], 2), own, number, OBS_DEV, N_LAT * N_LON, 1, CAP, 2))(obs_owner_keys, obs_owner_turns).reshape((2, STEPS, N_LAT * N_LON * OBS_DEV, 1))
    obs_cell = touch_ends(jax.random.randint(keys[2], (2, STEPS, N_LAT * N_LON * OBS_DEV), 0, CLAT * CLON), jax.random.fold_in(keys[2], 1), 0, (CLAT * CLON) - 1).astype(jnp.int32)
    velocity = jnp.clip(jax.random.uniform(keys[3], (2, STEPS, 2, LEV, NLAT, NLON), jnp.float32, -0.2, 0.2) * block_levels(keys[3], (2, STEPS, 2, LEV, NLAT, NLON), ((0, 2), (4, 16), (5, 8)), -0.4, 0.0), -0.2, 0.2)
    diffusion = jnp.clip(jnp.exp(math.log(0.08) - 2.0794415 * jax.random.uniform(keys[4], (2, STEPS, 2, LEV, NLAT, NLON), jnp.float32) ** block_levels(keys[4], (2, STEPS, 2, LEV, NLAT, NLON), ((0, 2), (4, 16), (5, 8)), -0.2, 0.2)), 0.01, 0.08)
    mixing = jnp.clip(jax.random.uniform(keys[5], (2, FIELDS, FIELDS), jnp.float32, -0.15, 0.15) * block_levels(keys[5], (2, FIELDS, FIELDS), ((0, 2),), -0.4, 0.0), -0.15, 0.15)
    air_sea = jnp.clip(jax.random.uniform(keys[6], (FIELDS, FIELDS), jnp.float32, -1.0, 1.0), -1.0, 1.0)
    sea_mask = touch_ends((jax.random.randint(keys[7], (NLAT, NLON), 0, 3) < 2).astype(jnp.int32), jax.random.fold_in(keys[7], 1), 0, 1)
    return dict(innovations=innovations, obs_owner=obs_owner, obs_cell=obs_cell, velocity=velocity, diffusion=diffusion, mixing=mixing, air_sea=air_sea, sea_mask=sea_mask)


HIGH = lax.Precision.HIGHEST


def place_rows(rows, owner, cell):
    lat_block = owner // N_LON
    lon_block = owner % N_LON
    row_index = lat_block * CLAT + cell // CLON
    col_index = lon_block * CLON + cell % CLON
    flat_index = (row_index * NLON + col_index).astype(jnp.int32)
    total = jnp.zeros((NLAT * NLON, FIELDS * LEV), jnp.float32).at[flat_index].add(rows)
    return jnp.transpose(total.reshape(NLAT, NLON, FIELDS, LEV), (2, 3, 0, 1))


def adjoint_step(adjoint, speeds, diffuse, mixing, air_sea, sea_float):
    masked = jnp.stack([adjoint[0], adjoint[1] * sea_float])
    result = masked + jnp.einsum("sfg,sflyx->sglyx", mixing, masked, precision=HIGH)
    east_up = (jnp.maximum(speeds[:, 0], 0.0) + diffuse[:, 0])[:, None]
    east_down = (jnp.minimum(speeds[:, 0], 0.0) - diffuse[:, 0])[:, None]
    east_diff = jnp.roll(masked, -1, axis=4) - masked
    result = result + east_up * east_diff + jnp.roll(east_down * east_diff, 1, axis=4)
    open_rows = (jnp.arange(NLAT) < NLAT - 1).astype(jnp.float32)[:, None]
    north_up = ((jnp.maximum(speeds[:, 1], 0.0) + diffuse[:, 1]) * open_rows)[:, None]
    north_down = ((jnp.minimum(speeds[:, 1], 0.0) - diffuse[:, 1]) * open_rows)[:, None]
    north_next = jnp.concatenate([masked[:, :, :, 1:], jnp.zeros_like(masked[:, :, :, :1])], axis=3)
    north_diff = north_next - masked
    carried = north_down * north_diff
    shifted = jnp.concatenate([jnp.zeros_like(carried[:, :, :, :1]), carried[:, :, :, :-1]], axis=3)
    result = result + north_up * north_diff + shifted
    coupled = sea_float * jnp.einsum("fg,fyx->gyx", air_sea, masked[0, :, LEV - 1], precision=HIGH)
    return result.at[1, :, 0].add(coupled)


def reference(innovations, obs_owner, obs_cell, velocity, diffusion, mixing, air_sea, sea_mask):
    sea_float = sea_mask.astype(jnp.float32)
    adjoint = jnp.zeros((2, FIELDS, LEV, NLAT, NLON), jnp.float32)
    for step in reversed(range(STEPS)):
        forcing = jnp.stack([place_rows(innovations[section, step], obs_owner[section, step, :, 0], obs_cell[section, step]) for section in range(2)])
        adjoint = adjoint + forcing
        adjoint = adjoint_step(adjoint, velocity[:, step], diffusion[:, step], mixing, air_sea, sea_float)
    return adjoint
```

```python
import functools

import jax
import jax.numpy as jnp
from jax import lax
from jax.experimental import pallas as pl
from jax.experimental.pallas import tpu as pltpu
from jax.sharding import PartitionSpec as P

LANES = 128
SUBS = 8
VMEM_LIMIT = 40 * 1024 * 1024


def split3(x):
    hi = x.astype(jnp.bfloat16)
    rest = x - hi.astype(jnp.float32)
    mid = rest.astype(jnp.bfloat16)
    low = (rest - mid.astype(jnp.float32)).astype(jnp.bfloat16)
    return [hi, mid, low]


def pack_kernel(slots, rows_ref, owner_ref, cell_ref, out_ref):
    steps, count, width = rows_ref.shape
    owners = count
    parts = width // LANES
    stride = out_ref.shape[0] // owners
    dest = lax.broadcasted_iota(jnp.int32, (owners, count), 0)
    lane = lax.broadcasted_iota(jnp.int32, (owners, count), 1)
    before = (dest < lane).astype(jnp.bfloat16)
    cells = jnp.zeros((owners, LANES), jnp.float32)
    for step in range(steps):
        hits = owner_ref[step : step + 1, :] == dest
        hits_f = hits.astype(jnp.float32)
        prior = jnp.dot(hits_f.astype(jnp.bfloat16), before, preferred_element_type=jnp.float32)
        terms = jnp.concatenate(split3(rows_ref[step]), axis=0)
        marks = (cell_ref[step : step + 1, :] + 1).astype(jnp.float32)
        for k in range(slots):
            slot = step * slots + k
            pick = jnp.where(prior == float(k), hits_f, 0.0)
            pick_b = pick.astype(jnp.bfloat16)
            out = jnp.dot(
                jnp.concatenate([pick_b] * 3, axis=1), terms, preferred_element_type=jnp.float32
            )
            for part in range(parts):
                out_ref[pl.ds(slot * parts + part, owners, stride=stride), :] = out[
                    :, part * LANES : (part + 1) * LANES
                ]
            mark = jnp.sum(pick * marks, axis=1, keepdims=True)
            cells = jnp.where(lane == slot, mark, cells)
    out_ref[pl.ds(stride - 1, owners, stride=stride), :] = cells


def spread_rows(step, slots, got_ref, width):
    parts = width // LANES
    stride = parts * slots * 3 + 1
    sources = got_ref.shape[0] // stride
    marks = got_ref[pl.ds(stride - 1, sources, stride=stride), :]
    where_to = lax.broadcasted_iota(jnp.int32, (sources, SUBS * LANES), 1)
    terms, onehots = [], []
    for k in range(slots):
        slot = step * slots + k
        cols = []
        for part in range(parts):
            block = got_ref[pl.ds(slot * parts + part, sources, stride=stride), :]
            cols.append(block.T)
        turned = jnp.concatenate(cols, axis=0)
        terms += split3(turned)
        cell = marks[:, slot : slot + 1].astype(jnp.int32) - 1
        onehot = (cell == where_to).astype(jnp.float32).astype(jnp.bfloat16)
        onehots += [onehot] * 3
    return jnp.dot(
        jnp.concatenate(terms, axis=1),
        jnp.concatenate(onehots, axis=0),
        preferred_element_type=jnp.float32,
    )


def take_edges(m_ref, south_ref, north_ref, fields, levels):
    south_ref[...] = m_ref[pl.ds(0, fields * levels, stride=SUBS), :]
    north_ref[...] = m_ref[pl.ds(SUBS - 1, fields * levels, stride=SUBS), :]


def take_columns(m_ref, west_ref, east_ref, fields, levels):
    lane = lax.broadcasted_iota(jnp.int32, (SUBS, LANES), 1)
    for f in range(fields):

        def body(i, cols, f=f):
            west, east = cols
            for j in range(8):
                level = i * 8 + j
                plane = m_ref[pl.ds(pl.multiple_of((f * levels + level) * SUBS, SUBS), SUBS), :]
                west = jnp.where(lane == level, pltpu.roll(plane, level, 1), west)
                east = jnp.where(lane == level, pltpu.roll(plane, (level + 1) % LANES, 1), east)
            return west, east

        zero = jnp.zeros((SUBS, LANES), jnp.float32)
        west, east = lax.fori_loop(0, levels // 8, body, (zero, zero))
        west_ref[f * SUBS : (f + 1) * SUBS, :] = west
        east_ref[f * SUBS : (f + 1) * SUBS, :] = east


def first_kernel(step, slots, fields, levels, got_ref, mask_ref, m_ref, south_ref, north_ref, west_ref, east_ref):
    width = fields * levels
    out = spread_rows(step, slots, got_ref, width)
    for row in range(SUBS):
        m_ref[pl.ds(row, width, stride=SUBS), :] = (
            out[:, row * LANES : (row + 1) * LANES] * mask_ref[row : row + 1, :]
        )
    take_edges(m_ref, south_ref, north_ref, fields, levels)
    take_columns(m_ref, west_ref, east_ref, fields, levels)


def forcing_kernel(step, slots, width, got_ref, f_ref):
    out = spread_rows(step, slots, got_ref, width)
    for row in range(SUBS):
        f_ref[pl.ds(row, width, stride=SUBS), :] = out[:, row * LANES : (row + 1) * LANES]


def step_kernel(
    last,
    fields,
    levels,
    mix_ref,
    air_ref,
    m_ref,
    vel_ref,
    dif_ref,
    open_ref,
    sea_ref,
    mask_ref,
    from_south_ref,
    from_north_ref,
    from_west_ref,
    from_east_ref,
    low_ref,
    east_rim_ref,
    north_rim_ref,
    *rest,
):
    if last:
        (out_ref,) = rest
    else:
        f_ref, out_ref, south_ref, north_ref, west_ref, east_ref = rest
    lane = lax.broadcasted_iota(jnp.int32, (SUBS, LANES), 1)
    sub = lax.broadcasted_iota(jnp.int32, (SUBS, LANES), 0)
    at_west, at_east = lane == 0, lane == LANES - 1
    at_south, at_north = sub == 0, sub == SUBS - 1
    opened = open_ref[...]
    mask = mask_ref[...]
    mix = [[mix_ref[f, g] for g in range(fields)] for f in range(fields)]
    from_west = [from_west_ref[f * SUBS : (f + 1) * SUBS, :] for f in range(fields)]
    from_east = [from_east_ref[f * SUBS : (f + 1) * SUBS, :] for f in range(fields)]
    east_rim = east_rim_ref[...]

    def level_step(level):
        w_e, k_e, w_n, k_n = vel_ref[0, level], dif_ref[0, level], vel_ref[1, level], dif_ref[1, level]
        up_e = jnp.maximum(w_e, 0.0) + k_e
        down_e = jnp.minimum(w_e, 0.0) - k_e
        up_n = (jnp.maximum(w_n, 0.0) + k_n) * opened
        down_n = (jnp.minimum(w_n, 0.0) - k_n) * opened
        to_first = (LANES - level) % LANES
        to_last = LANES - 1 - level
        down_w = jnp.where(at_west, pltpu.roll(east_rim, to_first, 1), pltpu.roll(down_e, 1, 1))
        down_s = jnp.where(at_south, north_rim_ref[pl.ds(level, 1), :], pltpu.roll(down_n, 1, 0))
        planes = []
        for f in range(fields):
            at = pl.multiple_of((f * levels + level) * SUBS, SUBS)
            planes.append(m_ref[pl.ds(at, SUBS), :])
        for g in range(fields):
            m = planes[g]
            result = m
            for f in range(fields):
                result = result + mix[f][g] * planes[f]
            east = jnp.where(at_east, pltpu.roll(from_east[g], to_last, 1), pltpu.roll(m, LANES - 1, 1))
            west = jnp.where(at_west, pltpu.roll(from_west[g], to_first, 1), pltpu.roll(m, 1, 1))
            row = g * levels + level
            north = jnp.where(at_north, from_north_ref[pl.ds(row, 1), :], pltpu.roll(m, SUBS - 1, 0))
            south = jnp.where(at_south, from_south_ref[pl.ds(row, 1), :], pltpu.roll(m, 1, 0))
            result = result + up_e * (east - m) + down_w * (m - west)
            result = result + up_n * (north - m) + down_s * (m - south)
            at = pl.multiple_of(row * SUBS, SUBS)
            out_ref[pl.ds(at, SUBS), :] = result

    def body(i, carry):
        for j in range(4):
            level_step(i * 4 + j)
        return carry

    lax.fori_loop(0, levels // 4, body, 0)
    sea = sea_ref[...]
    for g in range(fields):
        coupled = jnp.zeros((SUBS, LANES), jnp.float32)
        for f in range(fields):
            coupled = coupled + air_ref[f, g] * low_ref[f * SUBS : (f + 1) * SUBS, :]
        at = g * levels * SUBS
        out_ref[at : at + SUBS, :] = out_ref[at : at + SUBS, :] + sea * coupled
    if not last:

        def add(i, carry):
            for j in range(8):
                at = pl.multiple_of((i * 8 + j) * SUBS, SUBS)
                out_ref[pl.ds(at, SUBS), :] = (
                    out_ref[pl.ds(at, SUBS), :] + f_ref[pl.ds(at, SUBS), :]
                ) * mask
            return carry

        lax.fori_loop(0, fields * levels // 8, add, 0)
        take_edges(out_ref, south_ref, north_ref, fields, levels)
        take_columns(out_ref, west_ref, east_ref, fields, levels)


def params():
    return pltpu.CompilerParams(vmem_limit_bytes=VMEM_LIMIT)


def ring(axis, by, closed):
    count = lax.axis_size(axis)
    return [(i, (i + by) % count) for i in range(count) if closed or 0 <= i + by < count]


def shards(innovations, obs_owner, obs_cell, velocity, diffusion, mixing, air_sea, sea_mask):
    lat_count = lax.axis_size("lat")
    lon_count = lax.axis_size("lon")
    owners = lat_count * lon_count
    steps, levels, lat_rows, lon_cols = (velocity.shape[i] for i in (1, 3, 4, 5))
    fields = mixing.shape[1]
    width = fields * levels
    count = innovations.shape[2]
    slots = 2
    assert (lat_rows, lon_cols, levels, count, owners, steps) == (SUBS, LANES, LANES, LANES, LANES, 3)
    f32 = functools.partial(jax.ShapeDtypeStruct, dtype=jnp.float32)
    stride = steps * slots * width // LANES + 1

    is_ocean = lax.axis_index("comp") == 1
    sea_float = sea_mask.astype(jnp.float32)
    mask = jnp.where(is_ocean, sea_float, jnp.ones_like(sea_float))
    global_rows = lax.axis_index("lat") * lat_rows + lax.broadcasted_iota(
        jnp.int32, (lat_rows, lon_cols), 0
    )
    opened = (global_rows < lat_count * lat_rows - 1).astype(jnp.float32)

    sent = pl.pallas_call(
        functools.partial(pack_kernel, slots),
        out_shape=f32((owners * stride, LANES)),
        compiler_params=params(),
        name="pack",
    )(innovations[0], obs_owner[0, :, :, 0], obs_cell[0])
    got = lax.all_to_all(
        sent.reshape(owners, 1, stride * LANES), ("lat", "lon"), split_axis=0, concat_axis=0, tiled=True
    ).reshape(owners * stride, LANES)

    speeds, diffuse = velocity[0], diffusion[0]
    last_col = jnp.minimum(speeds[:, 0, :, :, -1], 0.0) - diffuse[:, 0, :, :, -1]
    east_rims = lax.ppermute(
        jnp.swapaxes(last_col, 1, 2).reshape(steps * lat_rows, levels), "lon", ring("lon", 1, True)
    ).reshape(steps, lat_rows, levels)
    last_row = jnp.minimum(speeds[:, 1, :, -1, :], 0.0) - diffuse[:, 1, :, -1, :]
    north_rims = lax.ppermute(
        last_row.reshape(steps * levels, lon_cols), "lat", ring("lat", 1, False)
    ).reshape(steps, levels, lon_cols)

    edge_shapes = [
        f32((width * SUBS, LANES)),
        f32((width, LANES)),
        f32((width, LANES)),
        f32((fields * SUBS, LANES)),
        f32((fields * SUBS, LANES)),
    ]
    m, south, north, west, east = pl.pallas_call(
        functools.partial(first_kernel, steps - 1, slots, fields, levels),
        out_shape=edge_shapes,
        compiler_params=params(),
        name="first",
    )(got, mask)
    for step in reversed(range(steps)):
        low = lax.ppermute(
            m.reshape(fields, levels, SUBS, LANES)[:, -1].reshape(fields * SUBS, LANES), "comp", [(0, 1)]
        )
        from_south = lax.ppermute(north, "lat", ring("lat", 1, False))
        from_north = lax.ppermute(south, "lat", ring("lat", -1, False))
        from_west = lax.ppermute(east, "lon", ring("lon", 1, True))
        from_east = lax.ppermute(west, "lon", ring("lon", -1, True))
        last = step == 0
        operands = [
            mixing[0],
            air_sea,
            m,
            speeds[step],
            diffuse[step],
            opened,
            sea_float,
            mask,
            from_south,
            from_north,
            from_west,
            from_east,
            low,
            east_rims[step],
            north_rims[step],
        ]
        if not last:
            operands.append(
                pl.pallas_call(
                    functools.partial(forcing_kernel, step - 1, slots, width),
                    out_shape=f32((width * SUBS, LANES)),
                    compiler_params=params(),
                    cost_estimate=pl.CostEstimate(
                        flops=2 * 3 * width * 2 * LANES * SUBS * LANES,
                        bytes_accessed=4 * (owners * stride * LANES + width * SUBS * LANES),
                        transcendentals=0,
                    ),
                    name="forcing",
                )(got)
            )
        smem = pl.BlockSpec(memory_space=pltpu.SMEM)
        vmem = pl.BlockSpec(memory_space=pltpu.VMEM)
        result = pl.pallas_call(
            functools.partial(step_kernel, last, fields, levels),
            out_shape=edge_shapes[:1] if last else edge_shapes,
            in_specs=[smem, smem] + [vmem] * (len(operands) - 2),
            compiler_params=params(),
            name="step",
        )(*operands)
        if last:
            m = result[0]
        else:
            m, south, north, west, east = result
    return m.reshape(1, fields, levels, lat_rows, lon_cols)


def solution(mesh):
    return jax.shard_map(
        shards,
        mesh=mesh,
        in_specs=(
            P("comp", None, ("lat", "lon"), None),
            P("comp", None, ("lat", "lon"), None),
            P("comp", None, ("lat", "lon")),
            P("comp", None, None, None, "lat", "lon"),
            P("comp", None, None, None, "lat", "lon"),
            P("comp", None, None),
            P(),
            P("lat", "lon"),
        ),
        out_specs=P("comp", None, None, "lat", "lon"),
        check_vma=False,
    )
```

```python
import functools

import jax
import jax.numpy as jnp
from jax import lax
from jax.experimental import pallas as pl
from jax.experimental.pallas import tpu as pltpu
from jax.sharding import PartitionSpec as P

LANES = 128
SUBS = 8
VMEM_LIMIT = 40 * 1024 * 1024


def split3(x):
    hi = x.astype(jnp.bfloat16)
    rest = x - hi.astype(jnp.float32)
    mid = rest.astype(jnp.bfloat16)
    low = (rest - mid.astype(jnp.float32)).astype(jnp.bfloat16)
    return [hi, mid, low]


def pack_kernel(slots, rows_ref, owner_ref, cell_ref, out_ref):
    steps, count, width = rows_ref.shape
    owners = count
    parts = width // LANES
    stride = out_ref.shape[0] // owners
    dest = lax.broadcasted_iota(jnp.int32, (owners, count), 0)
    lane = lax.broadcasted_iota(jnp.int32, (owners, count), 1)
    before = (dest < lane).astype(jnp.bfloat16)
    cells = jnp.zeros((owners, LANES), jnp.float32)
    for step in range(steps):
        hits = owner_ref[step : step + 1, :] == dest
        hits_f = hits.astype(jnp.float32)
        prior = jnp.dot(hits_f.astype(jnp.bfloat16), before, preferred_element_type=jnp.float32)
        terms = jnp.concatenate(split3(rows_ref[step]), axis=0)
        marks = (cell_ref[step : step + 1, :] + 1).astype(jnp.float32)
        for k in range(slots):
            slot = step * slots + k
            pick = jnp.where(prior == float(k), hits_f, 0.0)
            pick_b = pick.astype(jnp.bfloat16)
            out = jnp.dot(
                jnp.concatenate([pick_b] * 3, axis=1), terms, preferred_element_type=jnp.float32
            )
            for part in range(parts):
                out_ref[pl.ds(slot * parts + part, owners, stride=stride), :] = out[
                    :, part * LANES : (part + 1) * LANES
                ]
            mark = jnp.sum(pick * marks, axis=1, keepdims=True)
            cells = jnp.where(lane == slot, mark, cells)
    out_ref[pl.ds(stride - 1, owners, stride=stride), :] = cells


def spread_rows(step, slots, got_ref, width):
    parts = width // LANES
    stride = parts * slots * 3 + 1
    sources = got_ref.shape[0] // stride
    marks = got_ref[pl.ds(stride - 1, sources, stride=stride), :]
    where_to = lax.broadcasted_iota(jnp.int32, (sources, SUBS * LANES), 1)
    terms, onehots = [], []
    for k in range(slots):
        slot = step * slots + k
        cols = []
        for part in range(parts):
            block = got_ref[pl.ds(slot * parts + part, sources, stride=stride), :]
            cols.append(block.T)
        turned = jnp.concatenate(cols, axis=0)
        terms += split3(turned)
        cell = marks[:, slot : slot + 1].astype(jnp.int32) - 1
        onehot = (cell == where_to).astype(jnp.float32).astype(jnp.bfloat16)
        onehots += [onehot] * 3
    return jnp.dot(
        jnp.concatenate(terms, axis=1),
        jnp.concatenate(onehots, axis=0),
        preferred_element_type=jnp.float32,
    )


def columns_start(fields):
    zero = jnp.zeros((SUBS, LANES), jnp.float32)
    return [zero] * (2 * fields)


def columns_insert(cols, f, y, plane):
    lane = lax.broadcasted_iota(jnp.int32, (SUBS, LANES), 1)
    turned = plane if y == 0 else pltpu.roll(plane, y, 1)
    here = (lane == y) | (lane == (y - 1) % LANES)
    at = 2 * f + y % 2
    cols[at] = jnp.where(here, turned, cols[at])


def columns_turn(cols):
    return [pltpu.roll(c, LANES - SUBS, 1) for c in cols]


def columns_store(cols, west_ref, east_ref, fields):
    even = lax.broadcasted_iota(jnp.int32, (SUBS, LANES), 1) % 2 == 0
    for f in range(fields):
        a, b = cols[2 * f], cols[2 * f + 1]
        west_ref[f * SUBS : (f + 1) * SUBS, :] = jnp.where(even, a, b)
        east_ref[f * SUBS : (f + 1) * SUBS, :] = jnp.where(even, b, a)


def columns_load(from_west_ref, from_east_ref, fields):
    even = lax.broadcasted_iota(jnp.int32, (SUBS, LANES), 1) % 2 == 0
    cols = []
    for f in range(fields):
        west = pltpu.roll(from_west_ref[f * SUBS : (f + 1) * SUBS, :], 1, 1)
        east = pltpu.roll(from_east_ref[f * SUBS : (f + 1) * SUBS, :], LANES - 1, 1)
        cols += [jnp.where(even, west, east), jnp.where(even, east, west)]
    return cols


def columns_take(cols, f, y):
    col = cols[2 * f + y % 2]
    return col if y == 0 else pltpu.roll(col, LANES - y, 1)


def rows_of(base, group):
    if isinstance(group, int):
        return pl.ds(base + group * SUBS, SUBS)
    return pl.ds(pl.multiple_of(base + group * SUBS, SUBS), SUBS)


def first_kernel(
    step, slots, fields, levels, got_ref, mask_ref, m_ref, south_ref, north_ref, west_ref, east_ref, low_ref
):
    width = fields * levels
    out = spread_rows(step, slots, got_ref, width)
    for y in range(SUBS):
        m_ref[y * width : (y + 1) * width, :] = out[:, y * LANES : (y + 1) * LANES] * mask_ref[y : y + 1, :]
    south_ref[...] = m_ref[:width, :]
    north_ref[...] = m_ref[(SUBS - 1) * width :, :]

    def body(group, cols):
        cols = list(cols)
        for f in range(fields):
            for y in range(SUBS):
                columns_insert(cols, f, y, m_ref[rows_of(y * width + f * levels, group), :])
        return tuple(columns_turn(cols))

    cols = lax.fori_loop(0, levels // SUBS, body, tuple(columns_start(fields)))
    columns_store(cols, west_ref, east_ref, fields)
    for f in range(fields):
        low_ref[f * SUBS : (f + 1) * SUBS, :] = m_ref[pl.ds(f * levels + levels - 1, SUBS, stride=width), :]


def forcing_kernel(step, slots, width, got_ref, f_ref):
    out = spread_rows(step, slots, got_ref, width)
    for y in range(SUBS):
        f_ref[y * width : (y + 1) * width, :] = out[:, y * LANES : (y + 1) * LANES]


def rim_kernel(vel_ref, dif_ref, rim_ref, vel_row, dif_row, sems):
    copies = [
        pltpu.make_async_copy(src.at[:, 1, :, SUBS - 1, :], dst, sems.at[i])
        for i, (src, dst) in enumerate(((vel_ref, vel_row), (dif_ref, dif_row)))
    ]
    for copy in copies:
        copy.start()
    for copy in copies:
        copy.wait()
    steps, levels, lanes = vel_row.shape
    rim_ref[...] = (jnp.minimum(vel_row[...], 0.0) - dif_row[...]).reshape(steps * levels, lanes)


def coefficient_kernel(steps, levels, vel_ref, dif_ref, open_ref, *outs):
    tables, rim_ref = outs[:-1], outs[-1]
    lane = lax.broadcasted_iota(jnp.int32, (SUBS, LANES), 1)
    for step in range(steps):
        up_e_ref, down_e_ref, up_n_ref, down_n_ref = tables[4 * step : 4 * step + 4]
        east, north = 2 * step * levels * SUBS, (2 * step + 1) * levels * SUBS
        for y in range(SUBS):
            rows = slice(y * levels, (y + 1) * levels)
            w = vel_ref[pl.ds(east + y, levels, stride=SUBS), :]
            k = dif_ref[pl.ds(east + y, levels, stride=SUBS), :]
            up_e_ref[rows, :] = jnp.maximum(w, 0.0) + k
            down_e_ref[rows, :] = jnp.minimum(w, 0.0) - k
            w = vel_ref[pl.ds(north + y, levels, stride=SUBS), :]
            k = dif_ref[pl.ds(north + y, levels, stride=SUBS), :]
            up = jnp.maximum(w, 0.0) + k
            up_n_ref[rows, :] = up * open_ref[...] if y == SUBS - 1 else up
            down_n_ref[rows, :] = jnp.minimum(w, 0.0) - k

        def body(group, rim, down_e_ref=down_e_ref):
            for y in range(SUBS):
                plane = down_e_ref[rows_of(y * levels, group), :]
                rim = jnp.where(lane == y, pltpu.roll(plane, y + 1, 1), rim)
            return pltpu.roll(rim, LANES - SUBS, 1)

        rim_ref[step * SUBS : (step + 1) * SUBS, :] = lax.fori_loop(
            0, levels // SUBS, body, jnp.zeros((SUBS, LANES), jnp.float32)
        )


def shift_kernel(steps, levels, rim_ref, *refs):
    lane = lax.broadcasted_iota(jnp.int32, (SUBS, LANES), 1)
    for step in range(steps):
        down_e_ref, down_w_ref = refs[step], refs[steps + step]

        def body(group, rim, down_e_ref=down_e_ref, down_w_ref=down_w_ref):
            for y in range(SUBS):
                plane = down_e_ref[rows_of(y * levels, group), :]
                col = rim if y == 0 else pltpu.roll(rim, LANES - y, 1)
                down_w_ref[rows_of(y * levels, group), :] = jnp.where(lane == 0, col, pltpu.roll(plane, 1, 1))
            return pltpu.roll(rim, LANES - SUBS, 1)

        lax.fori_loop(0, levels // SUBS, body, rim_ref[step * SUBS : (step + 1) * SUBS, :])


def step_kernel(
    last,
    fields,
    levels,
    mix_ref,
    air_ref,
    m_ref,
    up_e_ref,
    down_w_ref,
    up_n_ref,
    down_n_ref,
    north_rim_ref,
    sea_ref,
    mask_ref,
    from_south_ref,
    from_north_ref,
    from_west_ref,
    from_east_ref,
    from_low_ref,
    *rest,
):
    if last:
        (out_ref,) = rest
    else:
        f_ref, out_ref, south_ref, north_ref, west_ref, east_ref, low_ref = rest
    width = fields * levels
    lane = lax.broadcasted_iota(jnp.int32, (SUBS, LANES), 1)
    sub = lax.broadcasted_iota(jnp.int32, (SUBS, LANES), 0)
    at_west, at_east = lane == 0, lane == LANES - 1
    mix = [[mix_ref[f, g] for g in range(fields)] for f in range(fields)]
    sea = sea_ref[...]
    coupled = []
    for g in range(fields):
        total = jnp.zeros((SUBS, LANES), jnp.float32)
        for f in range(fields):
            total = total + air_ref[f, g] * from_low_ref[f * SUBS : (f + 1) * SUBS, :]
        coupled.append(sea * total)

    def group_step(group, halos, cols):
        cols = list(cols)
        for y in range(SUBS):
            up_e = up_e_ref[rows_of(y * levels, group), :]
            down_w = down_w_ref[rows_of(y * levels, group), :]
            up_n = up_n_ref[rows_of(y * levels, group), :]
            if y == 0:
                down_s = north_rim_ref[rows_of(0, group), :]
            else:
                down_s = down_n_ref[rows_of((y - 1) * levels, group), :]
            planes = [m_ref[rows_of(y * width + f * levels, group), :] for f in range(fields)]
            for g in range(fields):
                m = planes[g]
                if y == SUBS - 1:
                    north = from_north_ref[rows_of(g * levels, group), :]
                else:
                    north = m_ref[rows_of((y + 1) * width + g * levels, group), :]
                if y == 0:
                    south = from_south_ref[rows_of(g * levels, group), :]
                else:
                    south = m_ref[rows_of((y - 1) * width + g * levels, group), :]
                halo = columns_take(halos, g, y)
                east = jnp.where(at_east, halo, pltpu.roll(m, LANES - 1, 1))
                west = jnp.where(at_west, halo, pltpu.roll(m, 1, 1))
                result = m
                for f in range(fields):
                    result = result + mix[f][g] * planes[f]
                result = result + (up_e * (east - m) + down_w * (m - west))
                result = result + (up_n * (north - m) + down_s * (m - south))
                if isinstance(group, int):
                    result = result + jnp.where(sub == 0, coupled[g][y : y + 1, :], 0.0)
                if last:
                    at = g * levels * SUBS + y
                    if isinstance(group, int):
                        out_ref[pl.ds(at + group * SUBS * SUBS, SUBS, stride=SUBS), :] = result
                    else:
                        out_ref[pl.ds(at + group * (SUBS * SUBS), SUBS, stride=SUBS), :] = result
                    continue
                rows = rows_of(y * width + g * levels, group)
                result = (result + f_ref[rows, :]) * mask_ref[y : y + 1, :]
                out_ref[rows, :] = result
                if y == 0:
                    south_ref[rows_of(g * levels, group), :] = result
                if y == SUBS - 1:
                    north_ref[rows_of(g * levels, group), :] = result
                columns_insert(cols, g, y, result)
        if not last:
            cols = columns_turn(cols)
        return columns_turn(halos), cols

    halos, cols = group_step(0, columns_load(from_west_ref, from_east_ref, fields), [] if last else columns_start(fields))

    def body(group, carry):
        halos, cols = group_step(group, list(carry[0]), list(carry[1]))
        return tuple(halos), tuple(cols)

    halos, cols = lax.fori_loop(1, levels // SUBS, body, (tuple(halos), tuple(cols)))
    if not last:
        columns_store(cols, west_ref, east_ref, fields)
        for f in range(fields):
            low_ref[f * SUBS : (f + 1) * SUBS, :] = out_ref[pl.ds(f * levels + levels - 1, SUBS, stride=width), :]


def params():
    return pltpu.CompilerParams(vmem_limit_bytes=VMEM_LIMIT)


def ring(axis, by, closed):
    count = lax.axis_size(axis)
    return [(i, (i + by) % count) for i in range(count) if closed or 0 <= i + by < count]


def shards(innovations, obs_owner, obs_cell, velocity, diffusion, mixing, air_sea, sea_mask):
    lat_count = lax.axis_size("lat")
    lon_count = lax.axis_size("lon")
    owners = lat_count * lon_count
    steps, levels, lat_rows, lon_cols = (velocity.shape[i] for i in (1, 3, 4, 5))
    fields = mixing.shape[1]
    width = fields * levels
    count = innovations.shape[2]
    slots = 2
    assert (lat_rows, lon_cols, levels, count, owners, steps) == (SUBS, LANES, LANES, LANES, LANES, 3)
    f32 = functools.partial(jax.ShapeDtypeStruct, dtype=jnp.float32)
    stride = steps * slots * width // LANES + 1

    is_ocean = lax.axis_index("comp") == 1
    sea_float = sea_mask.astype(jnp.float32)
    mask = jnp.where(is_ocean, sea_float, jnp.ones_like(sea_float))
    opened = jnp.full((1, lon_cols), lax.axis_index("lat") < lat_count - 1, jnp.float32)
    smem = pl.BlockSpec(memory_space=pltpu.SMEM)
    vmem = pl.BlockSpec(memory_space=pltpu.VMEM)
    anywhere = pl.BlockSpec(memory_space=pl.ANY)
    speeds, diffuse = velocity[0], diffusion[0]

    north_rims = pl.pallas_call(
        rim_kernel,
        out_shape=f32((steps * levels, LANES)),
        in_specs=[anywhere] * 2,
        scratch_shapes=[pltpu.VMEM((steps, levels, LANES), jnp.float32)] * 2 + [pltpu.SemaphoreType.DMA((2,))],
        compiler_params=params(),
        name="rim",
    )(speeds, diffuse)
    north_rims = lax.ppermute(north_rims, "lat", ring("lat", 1, False)).reshape(steps, levels, LANES)

    sent = pl.pallas_call(
        functools.partial(pack_kernel, slots),
        out_shape=f32((owners * stride, LANES)),
        compiler_params=params(),
        name="pack",
    )(innovations[0], obs_owner[0, :, :, 0], obs_cell[0])
    got = lax.all_to_all(
        sent.reshape(owners, 1, stride * LANES), ("lat", "lon"), split_axis=0, concat_axis=0, tiled=True
    ).reshape(owners * stride, LANES)

    table = f32((levels * SUBS, LANES))
    *tables, east_rims = pl.pallas_call(
        functools.partial(coefficient_kernel, steps, levels),
        out_shape=[table] * (4 * steps) + [f32((steps * SUBS, LANES))],
        compiler_params=params(),
        cost_estimate=pl.CostEstimate(flops=1 << 22, bytes_accessed=1 << 23, transcendentals=0),
        name="coefficients",
    )(
        speeds.reshape(steps * 2 * levels * SUBS, LANES),
        diffuse.reshape(steps * 2 * levels * SUBS, LANES),
        opened,
    )
    east_rims = lax.ppermute(east_rims, "lon", ring("lon", 1, True))
    downs_w = pl.pallas_call(
        functools.partial(shift_kernel, steps, levels),
        out_shape=[table] * steps,
        compiler_params=params(),
        name="shift",
    )(east_rims, *tables[1::4])

    edge_shapes = [
        f32((width * SUBS, LANES)),
        f32((width, LANES)),
        f32((width, LANES)),
        f32((fields * SUBS, LANES)),
        f32((fields * SUBS, LANES)),
        f32((fields * SUBS, LANES)),
    ]
    m, south, north, west, east, low = pl.pallas_call(
        functools.partial(first_kernel, steps - 1, slots, fields, levels),
        out_shape=edge_shapes,
        compiler_params=params(),
        name="first",
    )(got, mask)
    for step in reversed(range(steps)):
        from_south = lax.ppermute(north, "lat", ring("lat", 1, False))
        from_north = lax.ppermute(south, "lat", ring("lat", -1, False))
        from_west = lax.ppermute(east, "lon", ring("lon", 1, True))
        from_east = lax.ppermute(west, "lon", ring("lon", -1, True))
        from_low = lax.ppermute(low, "comp", [(0, 1)])
        last = step == 0
        operands = [
            mixing[0],
            air_sea,
            m,
            tables[4 * step],
            downs_w[step],
            tables[4 * step + 2],
            tables[4 * step + 3],
            north_rims[step],
            sea_float,
            mask,
            from_south,
            from_north,
            from_west,
            from_east,
            from_low,
        ]
        if not last:
            operands.append(
                pl.pallas_call(
                    functools.partial(forcing_kernel, step - 1, slots, width),
                    out_shape=f32((width * SUBS, LANES)),
                    compiler_params=params(),
                    cost_estimate=pl.CostEstimate(
                        flops=2 * 3 * width * 2 * LANES * SUBS * LANES,
                        bytes_accessed=4 * (owners * stride * LANES + width * SUBS * LANES),
                        transcendentals=0,
                    ),
                    name="forcing",
                )(got)
            )
        result = pl.pallas_call(
            functools.partial(step_kernel, last, fields, levels),
            out_shape=edge_shapes[:1] if last else edge_shapes,
            in_specs=[smem, smem] + [vmem] * (len(operands) - 2),
            compiler_params=params(),
            name="step",
        )(*operands)
        if last:
            m = result[0]
        else:
            m, south, north, west, east, low = result
    return m.reshape(1, fields, levels, lat_rows, lon_cols)


def solution(mesh):
    return jax.shard_map(
        shards,
        mesh=mesh,
        in_specs=(
            P("comp", None, ("lat", "lon"), None),
            P("comp", None, ("lat", "lon"), None),
            P("comp", None, ("lat", "lon")),
            P("comp", None, None, None, "lat", "lon"),
            P("comp", None, None, None, "lat", "lon"),
            P("comp", None, None),
            P(),
            P("lat", "lon"),
        ),
        out_specs=P("comp", None, None, "lat", "lon"),
        check_vma=False,
    )
```

```python
import functools

import jax
import jax.numpy as jnp
from jax import lax
from jax.experimental import pallas as pl
from jax.experimental.pallas import tpu as pltpu
from jax.sharding import PartitionSpec as P

LANES = 128
SUBS = 8
VMEM_LIMIT = 20 * 1024 * 1024


def split3(x):
    hi = x.astype(jnp.bfloat16)
    rest = x - hi.astype(jnp.float32)
    mid = rest.astype(jnp.bfloat16)
    low = (rest - mid.astype(jnp.float32)).astype(jnp.bfloat16)
    return [hi, mid, low]


def pack_kernel(slots, rows_hbm, owner_hbm, cell_hbm, out_ref, rows_ref, owner_ref, cell_ref, sems):
    steps, count, width = rows_ref.shape
    owners = count
    parts = width // LANES
    stride = out_ref.shape[0] // owners
    small = [
        pltpu.make_async_copy(owner_hbm, owner_ref, sems.at[steps]),
        pltpu.make_async_copy(cell_hbm, cell_ref, sems.at[steps + 1]),
    ]
    large = [
        pltpu.make_async_copy(rows_hbm.at[step], rows_ref.at[step], sems.at[step]) for step in range(steps)
    ]
    for copy in small + large:
        copy.start()
    dest = lax.broadcasted_iota(jnp.int32, (owners, count), 0)
    lane = lax.broadcasted_iota(jnp.int32, (owners, count), 1)
    before = (dest < lane).astype(jnp.bfloat16)
    cells = jnp.zeros((owners, LANES), jnp.float32)
    for copy in small:
        copy.wait()
    for step in range(steps):
        hits = owner_ref[step : step + 1, :] == dest
        hits_f = hits.astype(jnp.float32)
        prior = jnp.dot(hits_f.astype(jnp.bfloat16), before, preferred_element_type=jnp.float32)
        large[step].wait()
        terms = jnp.concatenate(split3(rows_ref[step]), axis=0)
        marks = (cell_ref[step : step + 1, :] + 1).astype(jnp.float32)
        for k in range(slots):
            slot = step * slots + k
            pick = jnp.where(prior == float(k), hits_f, 0.0)
            pick_b = pick.astype(jnp.bfloat16)
            out = jnp.dot(
                jnp.concatenate([pick_b] * 3, axis=1), terms, preferred_element_type=jnp.float32
            )
            for part in range(parts):
                out_ref[pl.ds(slot * parts + part, owners, stride=stride), :] = out[
                    :, part * LANES : (part + 1) * LANES
                ]
            mark = jnp.sum(pick * marks, axis=1, keepdims=True)
            cells = jnp.where(lane == slot, mark, cells)
    out_ref[pl.ds(stride - 1, owners, stride=stride), :] = cells


def spread_rows(step, slots, got_ref, width):
    parts = width // LANES
    stride = parts * slots * 3 + 1
    sources = got_ref.shape[0] // stride
    marks = got_ref[pl.ds(stride - 1, sources, stride=stride), :]
    where_to = lax.broadcasted_iota(jnp.int32, (sources, SUBS * LANES), 1)
    terms, onehots = [], []
    for k in range(slots):
        slot = step * slots + k
        cols = []
        for part in range(parts):
            block = got_ref[pl.ds(slot * parts + part, sources, stride=stride), :]
            cols.append(block.T)
        turned = jnp.concatenate(cols, axis=0)
        terms += split3(turned)
        cell = marks[:, slot : slot + 1].astype(jnp.int32) - 1
        onehot = (cell == where_to).astype(jnp.float32).astype(jnp.bfloat16)
        onehots += [onehot] * 3
    return jnp.dot(
        jnp.concatenate(terms, axis=1),
        jnp.concatenate(onehots, axis=0),
        preferred_element_type=jnp.float32,
    )


def columns_start(fields):
    zero = jnp.zeros((SUBS, LANES), jnp.float32)
    return [zero] * (2 * fields)


def columns_insert(cols, f, at, plane):
    lane = lax.broadcasted_iota(jnp.int32, (SUBS, LANES), 1)
    turned = plane if at == 0 else pltpu.roll(plane, at, 1)
    here = (lane == at) | (lane == (at - 1) % LANES)
    half = 2 * f + at % 2
    cols[half] = jnp.where(here, turned, cols[half])


def columns_turn(cols, groups):
    return [pltpu.roll(c, LANES - groups * SUBS, 1) for c in cols]


def columns_store(cols, rim, column_ref, fields):
    even = lax.broadcasted_iota(jnp.int32, (SUBS, LANES), 1) % 2 == 0
    for f in range(fields):
        a, b = cols[2 * f], cols[2 * f + 1]
        column_ref[f * SUBS : (f + 1) * SUBS, :] = jnp.where(even, a, b)
        column_ref[(fields + f) * SUBS : (fields + f + 1) * SUBS, :] = jnp.where(even, b, a)
    column_ref[2 * fields * SUBS :, :] = rim


def columns_load(lon_even, first_ref, second_ref, fields):
    even = lax.broadcasted_iota(jnp.int32, (SUBS, LANES), 1) % 2 == 0

    def rows(i):
        one, two = first_ref[i * SUBS : (i + 1) * SUBS, :], second_ref[i * SUBS : (i + 1) * SUBS, :]
        return jnp.where(lon_even, one, two), jnp.where(lon_even, two, one)

    cols = []
    for f in range(fields):
        west = pltpu.roll(rows(fields + f)[0], 1, 1)
        east = pltpu.roll(rows(f)[1], LANES - 1, 1)
        cols += [jnp.where(even, west, east), jnp.where(even, east, west)]
    return cols + [pltpu.roll(rows(2 * fields)[0], 1, 1)]


def turn_to_first(col, at):
    return col if at == 0 else pltpu.roll(col, LANES - at, 1)


def rows_of(base, group):
    if isinstance(group, int):
        return pl.ds(base + group * SUBS, SUBS)
    return pl.ds(pl.multiple_of(base + group * SUBS, SUBS), SUBS)


def slabs_store(lat_even, m_ref, first_ref, second_ref, width):
    for i in range(width // SUBS):
        rows = slice(i * SUBS, (i + 1) * SUBS)
        south = m_ref[rows, :]
        north = m_ref[(SUBS - 1) * width + i * SUBS : (SUBS - 1) * width + (i + 1) * SUBS, :]
        first_ref[rows, :] = jnp.where(lat_even, north, south)
        second_ref[rows, :] = jnp.where(lat_even, south, north)


def parity(ref, i):
    return jnp.full((SUBS, LANES), ref[i], jnp.int32) == 0


def low_store(m_ref, low_ref, fields, levels):
    for f in range(fields):
        low_ref[f * SUBS : (f + 1) * SUBS, :] = m_ref[
            pl.ds(f * levels + levels - 1, SUBS, stride=fields * levels), :
        ]


def first_kernel(
    step, slots, fields, levels, odd_ref, got_ref, mask_ref, rim_ref, m_ref, slab1_ref, slab2_ref, column_ref, low_ref
):
    width = fields * levels
    out = spread_rows(step, slots, got_ref, width)
    for y in range(SUBS):
        m_ref[y * width : (y + 1) * width, :] = out[:, y * LANES : (y + 1) * LANES] * mask_ref[y : y + 1, :]
    slabs_store(parity(odd_ref, 0), m_ref, slab1_ref, slab2_ref, width)
    cols = columns_start(fields)
    for group in range(levels // SUBS):
        for f in range(fields):
            for y in range(SUBS):
                columns_insert(cols, f, group * SUBS + y, m_ref[rows_of(y * width + f * levels, group), :])
    columns_store(cols, rim_ref[step * SUBS : (step + 1) * SUBS, :], column_ref, fields)
    low_store(m_ref, low_ref, fields, levels)


def forcing_kernel(step, slots, width, got_ref, f_ref):
    out = spread_rows(step, slots, got_ref, width)
    for y in range(SUBS):
        f_ref[y * width : (y + 1) * width, :] = out[:, y * LANES : (y + 1) * LANES]


def rim_kernel(vel_ref, dif_ref, rim_ref, vel_row, dif_row, sems):
    copies = [
        pltpu.make_async_copy(src.at[:, 1, :, SUBS - 1, :], dst, sems.at[i])
        for i, (src, dst) in enumerate(((vel_ref, vel_row), (dif_ref, dif_row)))
    ]
    for copy in copies:
        copy.start()
    for copy in copies:
        copy.wait()
    steps, levels, lanes = vel_row.shape
    rim_ref[...] = (jnp.minimum(vel_row[...], 0.0) - dif_row[...]).reshape(steps * levels, lanes)


def coefficient_kernel(steps, levels, vel_ref, dif_ref, open_ref, *outs):
    tables, rim_ref = outs[:-1], outs[-1]
    lane = lax.broadcasted_iota(jnp.int32, (SUBS, LANES), 1)
    for step in range(steps):
        up_e_ref, down_w_ref, up_n_ref, down_n_ref = tables[4 * step : 4 * step + 4]
        east, north = 2 * step * levels * SUBS, (2 * step + 1) * levels * SUBS
        for y in range(SUBS):
            rows = slice(y * levels, (y + 1) * levels)
            w = vel_ref[pl.ds(east + y, levels, stride=SUBS), :]
            k = dif_ref[pl.ds(east + y, levels, stride=SUBS), :]
            up_e_ref[rows, :] = jnp.maximum(w, 0.0) + k
            down_w_ref[rows, :] = pltpu.roll(jnp.minimum(w, 0.0) - k, 1, 1)
            w = vel_ref[pl.ds(north + y, levels, stride=SUBS), :]
            k = dif_ref[pl.ds(north + y, levels, stride=SUBS), :]
            up = jnp.maximum(w, 0.0) + k
            up_n_ref[rows, :] = up * open_ref[...] if y == SUBS - 1 else up
            down_n_ref[rows, :] = jnp.minimum(w, 0.0) - k
        rim = jnp.zeros((SUBS, LANES), jnp.float32)
        for group in range(levels // SUBS):
            for y in range(SUBS):
                at = group * SUBS + y
                plane = down_w_ref[rows_of(y * levels, group), :]
                to = (at - 1) % LANES
                rim = jnp.where(lane == to, plane if to == 0 else pltpu.roll(plane, to, 1), rim)
        rim_ref[step * SUBS : (step + 1) * SUBS, :] = rim


def step_kernel(
    last,
    step,
    fields,
    levels,
    mix_ref,
    air_ref,
    odd_ref,
    m_ref,
    up_e_ref,
    down_w_ref,
    up_n_ref,
    down_n_ref,
    north_rim_ref,
    sea_ref,
    mask_ref,
    from_slab1_ref,
    from_slab2_ref,
    from_column1_ref,
    from_column2_ref,
    from_low_ref,
    *rest,
):
    if last:
        (out_ref,) = rest
    else:
        f_ref, rim_ref, out_ref, slab1_ref, slab2_ref, column_ref, low_ref = rest
    width = fields * levels
    batch = 4
    lane = lax.broadcasted_iota(jnp.int32, (SUBS, LANES), 1)
    sub = lax.broadcasted_iota(jnp.int32, (SUBS, LANES), 0)
    at_west, at_east = lane == 0, lane == LANES - 1
    mix = [[mix_ref[f, g] for g in range(fields)] for f in range(fields)]
    lat_even, lon_even = parity(odd_ref, 0), parity(odd_ref, 1)
    sea = sea_ref[...]
    coupled = []
    for g in range(fields):
        total = jnp.zeros((SUBS, LANES), jnp.float32)
        for f in range(fields):
            total = total + air_ref[f, g] * from_low_ref[f * SUBS : (f + 1) * SUBS, :]
        coupled.append(sea * total)

    def batch_step(group0, halos, cols):
        cols = list(cols)
        for u in range(batch):
            group = group0 + u
            for y in range(SUBS):
                at = u * SUBS + y
                up_e = up_e_ref[rows_of(y * levels, group), :]
                down_w = jnp.where(
                    at_west, turn_to_first(halos[2 * fields], at), down_w_ref[rows_of(y * levels, group), :]
                )
                up_n = up_n_ref[rows_of(y * levels, group), :]
                if y == 0:
                    down_s = north_rim_ref[rows_of(0, group), :]
                else:
                    down_s = down_n_ref[rows_of((y - 1) * levels, group), :]
                planes = [m_ref[rows_of(y * width + f * levels, group), :] for f in range(fields)]
                for g in range(fields):
                    m = planes[g]
                    if y == 0 or y == SUBS - 1:
                        one = from_slab1_ref[rows_of(g * levels, group), :]
                        two = from_slab2_ref[rows_of(g * levels, group), :]
                    if y == SUBS - 1:
                        north = jnp.where(lat_even, one, two)
                    else:
                        north = m_ref[rows_of((y + 1) * width + g * levels, group), :]
                    if y == 0:
                        south = jnp.where(lat_even, two, one)
                    else:
                        south = m_ref[rows_of((y - 1) * width + g * levels, group), :]
                    halo = turn_to_first(halos[2 * g + at % 2], at)
                    east = jnp.where(at_east, halo, pltpu.roll(m, LANES - 1, 1))
                    west = jnp.where(at_west, halo, pltpu.roll(m, 1, 1))
                    result = m
                    for f in range(fields):
                        result = result + mix[f][g] * planes[f]
                    result = result + (up_e * (east - m) + down_w * (m - west))
                    result = result + (up_n * (north - m) + down_s * (m - south))
                    if isinstance(group, int) and group == 0:
                        result = result + jnp.where(sub == 0, coupled[g][y : y + 1, :], 0.0)
                    if last:
                        out_ref[pl.ds(g * levels * SUBS + y + group * (SUBS * SUBS), SUBS, stride=SUBS), :] = result
                        continue
                    rows = rows_of(y * width + g * levels, group)
                    result = (result + f_ref[rows, :]) * mask_ref[y : y + 1, :]
                    out_ref[rows, :] = result
                    columns_insert(cols, g, at, result)
        return columns_turn(halos, batch), columns_turn(cols, batch)

    halos = columns_load(lon_even, from_column1_ref, from_column2_ref, fields)
    halos, cols = batch_step(0, halos, [] if last else columns_start(fields))

    def body(i, carry):
        halos, cols = batch_step(i * batch, list(carry[0]), list(carry[1]))
        return tuple(halos), tuple(cols)

    halos, cols = lax.fori_loop(1, levels // (SUBS * batch), body, (tuple(halos), tuple(cols)))
    if not last:
        columns_store(cols, rim_ref[(step - 1) * SUBS : step * SUBS, :], column_ref, fields)
        slabs_store(lat_even, out_ref, slab1_ref, slab2_ref, width)
        low_store(out_ref, low_ref, fields, levels)


def params():
    return pltpu.CompilerParams(vmem_limit_bytes=VMEM_LIMIT)


def swaps(axis, start, closed):
    count = lax.axis_size(axis)
    pairs = []
    for i in range(start, count if closed else count - 1, 2):
        j = (i + 1) % count
        pairs += [(i, j), (j, i)]
    return pairs


def shards(innovations, obs_owner, obs_cell, velocity, diffusion, mixing, air_sea, sea_mask):
    lat_count = lax.axis_size("lat")
    lon_count = lax.axis_size("lon")
    owners = lat_count * lon_count
    steps, levels, lat_rows, lon_cols = (velocity.shape[i] for i in (1, 3, 4, 5))
    fields = mixing.shape[1]
    width = fields * levels
    count = innovations.shape[2]
    slots = 2
    assert (lat_rows, lon_cols, levels, count, owners, steps) == (SUBS, LANES, LANES, LANES, LANES, 3)
    f32 = functools.partial(jax.ShapeDtypeStruct, dtype=jnp.float32)
    stride = steps * slots * width // LANES + 1

    is_ocean = lax.axis_index("comp") == 1
    sea_float = sea_mask.astype(jnp.float32)
    mask = jnp.where(is_ocean, sea_float, jnp.ones_like(sea_float))
    opened = jnp.full((1, lon_cols), lax.axis_index("lat") < lat_count - 1, jnp.float32)
    smem = pl.BlockSpec(memory_space=pltpu.SMEM)
    vmem = pl.BlockSpec(memory_space=pltpu.VMEM)
    anywhere = pl.BlockSpec(memory_space=pltpu.HBM)
    speeds, diffuse = velocity[0], diffusion[0]

    north_rims = pl.pallas_call(
        rim_kernel,
        out_shape=f32((steps * levels, LANES)),
        in_specs=[anywhere] * 2,
        scratch_shapes=[pltpu.VMEM((steps, levels, LANES), jnp.float32)] * 2 + [pltpu.SemaphoreType.DMA((2,))],
        compiler_params=params(),
        name="rim",
    )(speeds, diffuse)
    north_rims = lax.ppermute(
        north_rims, "lat", [(i, i + 1) for i in range(lat_count - 1)]
    ).reshape(steps, levels, LANES)

    sent = pl.pallas_call(
        functools.partial(pack_kernel, slots),
        out_shape=f32((owners * stride, LANES)),
        in_specs=[anywhere] * 3,
        scratch_shapes=[
            pltpu.VMEM((steps, count, width), jnp.float32),
            pltpu.VMEM((steps, count), jnp.int32),
            pltpu.VMEM((steps, count), jnp.int32),
            pltpu.SemaphoreType.DMA((steps + 2,)),
        ],
        compiler_params=params(),
        name="pack",
    )(innovations[0], obs_owner[0, :, :, 0], obs_cell[0])
    got = lax.all_to_all(
        sent.reshape(owners, 1, stride * LANES), ("lat", "lon"), split_axis=0, concat_axis=0, tiled=True
    ).reshape(owners * stride, LANES)

    table = f32((levels * SUBS, LANES))
    *tables, east_rims = pl.pallas_call(
        functools.partial(coefficient_kernel, steps, levels),
        out_shape=[table] * (4 * steps) + [f32((steps * SUBS, LANES))],
        compiler_params=params(),
        cost_estimate=pl.CostEstimate(flops=1 << 22, bytes_accessed=1 << 23, transcendentals=0),
        name="coefficients",
    )(
        speeds.reshape(steps * 2 * levels * SUBS, LANES),
        diffuse.reshape(steps * 2 * levels * SUBS, LANES),
        opened,
    )
    odd = jnp.stack([lax.axis_index("lat") % 2, lax.axis_index("lon") % 2]).astype(jnp.int32)
    edge_shapes = [
        f32((width * SUBS, LANES)),
        f32((width, LANES)),
        f32((width, LANES)),
        f32(((2 * fields + 1) * SUBS, LANES)),
        f32((fields * SUBS, LANES)),
    ]
    m, slab1, slab2, columns, low = pl.pallas_call(
        functools.partial(first_kernel, steps - 1, slots, fields, levels),
        out_shape=edge_shapes,
        in_specs=[smem] + [vmem] * 3,
        compiler_params=params(),
        name="first",
    )(odd, got, mask, east_rims)
    for step in reversed(range(steps)):
        last = step == 0
        operands = [
            mixing[0],
            air_sea,
            odd,
            m,
            *tables[4 * step : 4 * step + 4],
            north_rims[step],
            sea_float,
            mask,
            lax.ppermute(slab1, "lat", swaps("lat", 0, False)),
            lax.ppermute(slab2, "lat", swaps("lat", 1, False)),
            lax.ppermute(columns, "lon", swaps("lon", 1, True)),
            lax.ppermute(columns, "lon", swaps("lon", 0, True)),
            lax.ppermute(low, "comp", [(0, 1)]),
        ]
        if not last:
            operands.append(
                pl.pallas_call(
                    functools.partial(forcing_kernel, step - 1, slots, width),
                    out_shape=f32((width * SUBS, LANES)),
                    compiler_params=params(),
                    cost_estimate=pl.CostEstimate(
                        flops=2 * 3 * width * 2 * LANES * SUBS * LANES,
                        bytes_accessed=4 * (owners * stride * LANES + width * SUBS * LANES),
                        transcendentals=0,
                    ),
                    name="forcing",
                )(got)
            )
            operands.append(east_rims)
        result = pl.pallas_call(
            functools.partial(step_kernel, last, step, fields, levels),
            out_shape=edge_shapes[:1] if last else edge_shapes,
            in_specs=[smem] * 3 + [vmem] * (len(operands) - 3),
            compiler_params=params(),
            name="step",
        )(*operands)
        if last:
            m = result[0]
        else:
            m, slab1, slab2, columns, low = result
    return m.reshape(1, fields, levels, lat_rows, lon_cols)


def solution(mesh):
    return jax.shard_map(
        shards,
        mesh=mesh,
        in_specs=(
            P("comp", None, ("lat", "lon"), None),
            P("comp", None, ("lat", "lon"), None),
            P("comp", None, ("lat", "lon")),
            P("comp", None, None, None, "lat", "lon"),
            P("comp", None, None, None, "lat", "lon"),
            P("comp", None, None),
            P(),
            P("lat", "lon"),
        ),
        out_specs=P("comp", None, None, "lat", "lon"),
        check_vma=False,
    )
```

```python
import functools

import jax
import jax.numpy as jnp
from jax import lax
from jax.experimental import pallas as pl
from jax.experimental.pallas import tpu as pltpu
from jax.sharding import PartitionSpec as P

LANES = 128
SUBS = 8
VMEM_LIMIT = 20 * 1024 * 1024


def split3(x):
    hi = x.astype(jnp.bfloat16)
    rest = x - hi.astype(jnp.float32)
    mid = rest.astype(jnp.bfloat16)
    low = (rest - mid.astype(jnp.float32)).astype(jnp.bfloat16)
    return [hi, mid, low]


def pack_kernel(slots, rows_hbm, owner_hbm, cell_hbm, out_ref, rows_ref, owner_ref, cell_ref, sems):
    steps, count, width = rows_ref.shape
    owners = count
    parts = width // LANES
    stride = out_ref.shape[0] // owners
    small = [
        pltpu.make_async_copy(owner_hbm, owner_ref, sems.at[steps]),
        pltpu.make_async_copy(cell_hbm, cell_ref, sems.at[steps + 1]),
    ]
    large = [
        pltpu.make_async_copy(rows_hbm.at[step], rows_ref.at[step], sems.at[step]) for step in range(steps)
    ]
    for copy in small + large:
        copy.start()
    dest = lax.broadcasted_iota(jnp.int32, (owners, count), 0)
    lane = lax.broadcasted_iota(jnp.int32, (owners, count), 1)
    before = (dest < lane).astype(jnp.bfloat16)
    cells = jnp.zeros((owners, LANES), jnp.float32)
    for copy in small:
        copy.wait()
    for step in range(steps):
        hits = owner_ref[step : step + 1, :] == dest
        hits_f = hits.astype(jnp.float32)
        prior = jnp.dot(hits_f.astype(jnp.bfloat16), before, preferred_element_type=jnp.float32)
        large[step].wait()
        terms = jnp.concatenate(split3(rows_ref[step]), axis=0)
        marks = (cell_ref[step : step + 1, :] + 1).astype(jnp.float32)
        for k in range(slots):
            slot = step * slots + k
            pick = jnp.where(prior == float(k), hits_f, 0.0)
            pick_b = pick.astype(jnp.bfloat16)
            out = jnp.dot(
                jnp.concatenate([pick_b] * 3, axis=1), terms, preferred_element_type=jnp.float32
            )
            for part in range(parts):
                out_ref[pl.ds(slot * parts + part, owners, stride=stride), :] = out[
                    :, part * LANES : (part + 1) * LANES
                ]
            mark = jnp.sum(pick * marks, axis=1, keepdims=True)
            cells = jnp.where(lane == slot, mark, cells)
    out_ref[pl.ds(stride - 1, owners, stride=stride), :] = cells


def spread_rows(step, slots, got_ref, width):
    parts = width // LANES
    stride = parts * slots * 3 + 1
    sources = got_ref.shape[0] // stride
    marks = got_ref[pl.ds(stride - 1, sources, stride=stride), :]
    where_to = lax.broadcasted_iota(jnp.int32, (sources, SUBS * LANES), 1)
    terms, onehots = [], []
    for k in range(slots):
        slot = step * slots + k
        cols = []
        for part in range(parts):
            block = got_ref[pl.ds(slot * parts + part, sources, stride=stride), :]
            cols.append(block.T)
        turned = jnp.concatenate(cols, axis=0)
        terms += split3(turned)
        cell = marks[:, slot : slot + 1].astype(jnp.int32) - 1
        onehot = (cell == where_to).astype(jnp.float32).astype(jnp.bfloat16)
        onehots += [onehot] * 3
    return jnp.dot(
        jnp.concatenate(terms, axis=1),
        jnp.concatenate(onehots, axis=0),
        preferred_element_type=jnp.float32,
    )


def columns_store(m_ref, rim, column_ref, fields, levels):
    lane = lax.broadcasted_iota(jnp.int32, (SUBS, LANES), 1)
    even = lane % 2 == 0
    for f in range(fields):
        halves = [jnp.zeros((SUBS, LANES), jnp.float32)] * 2
        for group in range(levels // SUBS):
            for y in range(SUBS):
                at = group * SUBS + y
                plane = m_ref[rows_of((y * fields + f) * levels, group), :]
                turned = plane if at == 0 else pltpu.roll(plane, at, 1)
                here = (lane == at) | (lane == (at - 1) % LANES)
                halves[at % 2] = jnp.where(here, turned, halves[at % 2])
        column_ref[f * SUBS : (f + 1) * SUBS, :] = jnp.where(even, halves[0], halves[1])
        column_ref[(fields + f) * SUBS : (fields + f + 1) * SUBS, :] = jnp.where(even, halves[1], halves[0])
    column_ref[2 * fields * SUBS :, :] = rim


def columns_turn(cols, groups):
    return [pltpu.roll(c, LANES - groups * SUBS, 1) for c in cols]


def columns_load(lon_even, first_ref, second_ref, fields):
    even = lax.broadcasted_iota(jnp.int32, (SUBS, LANES), 1) % 2 == 0

    def rows(i):
        one, two = first_ref[i * SUBS : (i + 1) * SUBS, :], second_ref[i * SUBS : (i + 1) * SUBS, :]
        return jnp.where(lon_even, one, two), jnp.where(lon_even, two, one)

    cols = []
    for f in range(fields):
        west = pltpu.roll(rows(fields + f)[0], 1, 1)
        east = pltpu.roll(rows(f)[1], LANES - 1, 1)
        cols += [jnp.where(even, west, east), jnp.where(even, east, west)]
    return cols + [pltpu.roll(rows(2 * fields)[0], 1, 1)]


def turn_to_first(col, at):
    return col if at == 0 else pltpu.roll(col, LANES - at, 1)


def rows_of(base, group):
    if isinstance(group, int):
        return pl.ds(base + group * SUBS, SUBS)
    return pl.ds(pl.multiple_of(base + group * SUBS, SUBS), SUBS)


def slabs_store(lat_even, m_ref, first_ref, second_ref, width):
    for i in range(width // SUBS):
        rows = slice(i * SUBS, (i + 1) * SUBS)
        south = m_ref[rows, :]
        north = m_ref[(SUBS - 1) * width + i * SUBS : (SUBS - 1) * width + (i + 1) * SUBS, :]
        first_ref[rows, :] = jnp.where(lat_even, north, south)
        second_ref[rows, :] = jnp.where(lat_even, south, north)


def parity(ref, i):
    return jnp.full((SUBS, LANES), ref[i], jnp.int32) == 0


def low_store(m_ref, low_ref, fields, levels):
    for f in range(fields):
        low_ref[f * SUBS : (f + 1) * SUBS, :] = m_ref[
            pl.ds(f * levels + levels - 1, SUBS, stride=fields * levels), :
        ]


def first_kernel(
    step, slots, fields, levels, odd_ref, got_ref, mask_ref, rim_ref, m_ref, slab1_ref, slab2_ref, column_ref, low_ref
):
    width = fields * levels
    out = spread_rows(step, slots, got_ref, width)
    for y in range(SUBS):
        m_ref[y * width : (y + 1) * width, :] = out[:, y * LANES : (y + 1) * LANES] * mask_ref[y : y + 1, :]
    slabs_store(parity(odd_ref, 0), m_ref, slab1_ref, slab2_ref, width)
    columns_store(m_ref, rim_ref[step * SUBS : (step + 1) * SUBS, :], column_ref, fields, levels)
    low_store(m_ref, low_ref, fields, levels)


def forcing_kernel(step, slots, width, got_ref, f_ref):
    out = spread_rows(step, slots, got_ref, width)
    for y in range(SUBS):
        f_ref[y * width : (y + 1) * width, :] = out[:, y * LANES : (y + 1) * LANES]


def rim_kernel(vel_ref, dif_ref, rim_ref, vel_row, dif_row, sems):
    copies = [
        pltpu.make_async_copy(src.at[:, 1, :, SUBS - 1, :], dst, sems.at[i])
        for i, (src, dst) in enumerate(((vel_ref, vel_row), (dif_ref, dif_row)))
    ]
    for copy in copies:
        copy.start()
    for copy in copies:
        copy.wait()
    steps, levels, lanes = vel_row.shape
    rim_ref[...] = (jnp.minimum(vel_row[...], 0.0) - dif_row[...]).reshape(steps * levels, lanes)


def coefficient_kernel(steps, levels, vel_ref, dif_ref, open_ref, *outs):
    tables, rim_ref = outs[:-1], outs[-1]
    lane = lax.broadcasted_iota(jnp.int32, (SUBS, LANES), 1)
    for step in range(steps):
        up_e_ref, down_w_ref, up_n_ref, down_n_ref = tables[4 * step : 4 * step + 4]
        east, north = 2 * step * levels * SUBS, (2 * step + 1) * levels * SUBS
        for y in range(SUBS):
            rows = slice(y * levels, (y + 1) * levels)
            w = vel_ref[pl.ds(east + y, levels, stride=SUBS), :]
            k = dif_ref[pl.ds(east + y, levels, stride=SUBS), :]
            up_e_ref[rows, :] = jnp.maximum(w, 0.0) + k
            down_w_ref[rows, :] = pltpu.roll(jnp.minimum(w, 0.0) - k, 1, 1)
            w = vel_ref[pl.ds(north + y, levels, stride=SUBS), :]
            k = dif_ref[pl.ds(north + y, levels, stride=SUBS), :]
            up = jnp.maximum(w, 0.0) + k
            up_n_ref[rows, :] = up * open_ref[...] if y == SUBS - 1 else up
            down_n_ref[rows, :] = jnp.minimum(w, 0.0) - k
        rim = jnp.zeros((SUBS, LANES), jnp.float32)
        for group in range(levels // SUBS):
            for y in range(SUBS):
                at = group * SUBS + y
                plane = down_w_ref[rows_of(y * levels, group), :]
                to = (at - 1) % LANES
                rim = jnp.where(lane == to, plane if to == 0 else pltpu.roll(plane, to, 1), rim)
        rim_ref[step * SUBS : (step + 1) * SUBS, :] = rim


def step_kernel(
    last,
    step,
    fields,
    levels,
    mix_ref,
    air_ref,
    odd_ref,
    m_ref,
    up_e_ref,
    down_w_ref,
    up_n_ref,
    down_n_ref,
    north_rim_ref,
    sea_ref,
    mask_ref,
    from_slab1_ref,
    from_slab2_ref,
    from_column1_ref,
    from_column2_ref,
    from_low_ref,
    *rest,
):
    if last:
        (out_ref,) = rest
    else:
        f_ref, rim_ref, out_ref, slab1_ref, slab2_ref, column_ref, low_ref = rest
    width = fields * levels
    batch = 4
    lane = lax.broadcasted_iota(jnp.int32, (SUBS, LANES), 1)
    sub = lax.broadcasted_iota(jnp.int32, (SUBS, LANES), 0)
    at_west, at_east = lane == 0, lane == LANES - 1
    mix = [[mix_ref[f, g] for g in range(fields)] for f in range(fields)]
    lat_even, lon_even = parity(odd_ref, 0), parity(odd_ref, 1)
    sea = sea_ref[...]
    coupled = []
    for g in range(fields):
        total = jnp.zeros((SUBS, LANES), jnp.float32)
        for f in range(fields):
            total = total + air_ref[f, g] * from_low_ref[f * SUBS : (f + 1) * SUBS, :]
        coupled.append(sea * total)

    def batch_step(group0, halos):
        for u in range(batch):
            group = group0 + u
            for y in range(SUBS):
                at = u * SUBS + y
                up_e = up_e_ref[rows_of(y * levels, group), :]
                down_w = jnp.where(
                    at_west, turn_to_first(halos[2 * fields], at), down_w_ref[rows_of(y * levels, group), :]
                )
                up_n = up_n_ref[rows_of(y * levels, group), :]
                if y == 0:
                    down_s = north_rim_ref[rows_of(0, group), :]
                else:
                    down_s = down_n_ref[rows_of((y - 1) * levels, group), :]
                planes = [m_ref[rows_of(y * width + f * levels, group), :] for f in range(fields)]
                for g in range(fields):
                    m = planes[g]
                    if y == 0 or y == SUBS - 1:
                        one = from_slab1_ref[rows_of(g * levels, group), :]
                        two = from_slab2_ref[rows_of(g * levels, group), :]
                    if y == SUBS - 1:
                        north = jnp.where(lat_even, one, two)
                    else:
                        north = m_ref[rows_of((y + 1) * width + g * levels, group), :]
                    if y == 0:
                        south = jnp.where(lat_even, two, one)
                    else:
                        south = m_ref[rows_of((y - 1) * width + g * levels, group), :]
                    halo = turn_to_first(halos[2 * g + at % 2], at)
                    east = jnp.where(at_east, halo, pltpu.roll(m, LANES - 1, 1))
                    west = jnp.where(at_west, halo, pltpu.roll(m, 1, 1))
                    result = m
                    for f in range(fields):
                        result = result + mix[f][g] * planes[f]
                    result = result + (up_e * (east - m) + down_w * (m - west))
                    result = result + (up_n * (north - m) + down_s * (m - south))
                    if isinstance(group, int) and group == 0:
                        result = result + jnp.where(sub == 0, coupled[g][y : y + 1, :], 0.0)
                    if last:
                        out_ref[pl.ds(g * levels * SUBS + y + group * (SUBS * SUBS), SUBS, stride=SUBS), :] = result
                        continue
                    rows = rows_of(y * width + g * levels, group)
                    result = (result + f_ref[rows, :]) * mask_ref[y : y + 1, :]
                    out_ref[rows, :] = result
        return columns_turn(halos, batch)

    halos = columns_load(lon_even, from_column1_ref, from_column2_ref, fields)
    halos = batch_step(0, halos)

    def body(i, halos):
        return tuple(batch_step(i * batch, list(halos)))

    lax.fori_loop(1, levels // (SUBS * batch), body, tuple(halos))
    if not last:
        columns_store(out_ref, rim_ref[(step - 1) * SUBS : step * SUBS, :], column_ref, fields, levels)
        slabs_store(lat_even, out_ref, slab1_ref, slab2_ref, width)
        low_store(out_ref, low_ref, fields, levels)


def params():
    return pltpu.CompilerParams(vmem_limit_bytes=VMEM_LIMIT)


def swaps(axis, start, closed):
    count = lax.axis_size(axis)
    pairs = []
    for i in range(start, count if closed else count - 1, 2):
        j = (i + 1) % count
        pairs += [(i, j), (j, i)]
    return pairs


def shards(innovations, obs_owner, obs_cell, velocity, diffusion, mixing, air_sea, sea_mask):
    lat_count = lax.axis_size("lat")
    lon_count = lax.axis_size("lon")
    owners = lat_count * lon_count
    steps, levels, lat_rows, lon_cols = (velocity.shape[i] for i in (1, 3, 4, 5))
    fields = mixing.shape[1]
    width = fields * levels
    count = innovations.shape[2]
    slots = 2
    assert (lat_rows, lon_cols, levels, count, owners, steps) == (SUBS, LANES, LANES, LANES, LANES, 3)
    f32 = functools.partial(jax.ShapeDtypeStruct, dtype=jnp.float32)
    stride = steps * slots * width // LANES + 1

    is_ocean = lax.axis_index("comp") == 1
    sea_float = sea_mask.astype(jnp.float32)
    mask = jnp.where(is_ocean, sea_float, jnp.ones_like(sea_float))
    opened = jnp.full((1, lon_cols), lax.axis_index("lat") < lat_count - 1, jnp.float32)
    smem = pl.BlockSpec(memory_space=pltpu.SMEM)
    vmem = pl.BlockSpec(memory_space=pltpu.VMEM)
    anywhere = pl.BlockSpec(memory_space=pltpu.HBM)
    speeds, diffuse = velocity[0], diffusion[0]

    north_rims = pl.pallas_call(
        rim_kernel,
        out_shape=f32((steps * levels, LANES)),
        in_specs=[anywhere] * 2,
        scratch_shapes=[pltpu.VMEM((steps, levels, LANES), jnp.float32)] * 2 + [pltpu.SemaphoreType.DMA((2,))],
        compiler_params=params(),
        name="rim",
    )(speeds, diffuse)
    north_rims = lax.ppermute(
        north_rims, "lat", [(i, i + 1) for i in range(lat_count - 1)]
    ).reshape(steps, levels, LANES)

    sent = pl.pallas_call(
        functools.partial(pack_kernel, slots),
        out_shape=f32((owners * stride, LANES)),
        in_specs=[anywhere] * 3,
        scratch_shapes=[
            pltpu.VMEM((steps, count, width), jnp.float32),
            pltpu.VMEM((steps, count), jnp.int32),
            pltpu.VMEM((steps, count), jnp.int32),
            pltpu.SemaphoreType.DMA((steps + 2,)),
        ],
        compiler_params=params(),
        name="pack",
    )(innovations[0], obs_owner[0, :, :, 0], obs_cell[0])
    got = lax.all_to_all(
        sent.reshape(owners, 1, stride * LANES), ("lat", "lon"), split_axis=0, concat_axis=0, tiled=True
    ).reshape(owners * stride, LANES)

    table = f32((levels * SUBS, LANES))
    *tables, east_rims = pl.pallas_call(
        functools.partial(coefficient_kernel, steps, levels),
        out_shape=[table] * (4 * steps) + [f32((steps * SUBS, LANES))],
        compiler_params=params(),
        cost_estimate=pl.CostEstimate(flops=1 << 22, bytes_accessed=1 << 23, transcendentals=0),
        name="coefficients",
    )(
        speeds.reshape(steps * 2 * levels * SUBS, LANES),
        diffuse.reshape(steps * 2 * levels * SUBS, LANES),
        opened,
    )
    odd = jnp.stack([lax.axis_index("lat") % 2, lax.axis_index("lon") % 2]).astype(jnp.int32)
    edge_shapes = [
        f32((width * SUBS, LANES)),
        f32((width, LANES)),
        f32((width, LANES)),
        f32(((2 * fields + 1) * SUBS, LANES)),
        f32((fields * SUBS, LANES)),
    ]
    m, slab1, slab2, columns, low = pl.pallas_call(
        functools.partial(first_kernel, steps - 1, slots, fields, levels),
        out_shape=edge_shapes,
        in_specs=[smem] + [vmem] * 3,
        compiler_params=params(),
        name="first",
    )(odd, got, mask, east_rims)
    for step in reversed(range(steps)):
        last = step == 0
        operands = [
            mixing[0],
            air_sea,
            odd,
            m,
            *tables[4 * step : 4 * step + 4],
            north_rims[step],
            sea_float,
            mask,
            lax.ppermute(slab1, "lat", swaps("lat", 0, False)),
            lax.ppermute(slab2, "lat", swaps("lat", 1, False)),
            lax.ppermute(columns, "lon", swaps("lon", 1, True)),
            lax.ppermute(columns, "lon", swaps("lon", 0, True)),
            lax.ppermute(low, "comp", [(0, 1)]),
        ]
        if not last:
            operands.append(
                pl.pallas_call(
                    functools.partial(forcing_kernel, step - 1, slots, width),
                    out_shape=f32((width * SUBS, LANES)),
                    compiler_params=params(),
                    cost_estimate=pl.CostEstimate(
                        flops=2 * 3 * width * 2 * LANES * SUBS * LANES,
                        bytes_accessed=4 * (owners * stride * LANES + width * SUBS * LANES),
                        transcendentals=0,
                    ),
                    name="forcing",
                )(got)
            )
            operands.append(east_rims)
        result = pl.pallas_call(
            functools.partial(step_kernel, last, step, fields, levels),
            out_shape=edge_shapes[:1] if last else edge_shapes,
            in_specs=[smem] * 3 + [vmem] * (len(operands) - 3),
            compiler_params=params(),
            name="step",
        )(*operands)
        if last:
            m = result[0]
        else:
            m, slab1, slab2, columns, low = result
    return m.reshape(1, fields, levels, lat_rows, lon_cols)


def solution(mesh):
    return jax.shard_map(
        shards,
        mesh=mesh,
        in_specs=(
            P("comp", None, ("lat", "lon"), None),
            P("comp", None, ("lat", "lon"), None),
            P("comp", None, ("lat", "lon")),
            P("comp", None, None, None, "lat", "lon"),
            P("comp", None, None, None, "lat", "lon"),
            P("comp", None, None),
            P(),
            P("lat", "lon"),
        ),
        out_specs=P("comp", None, None, "lat", "lon"),
        check_vma=False,
    )
```

```python
import functools

import jax
import jax.numpy as jnp
from jax import lax
from jax.experimental import pallas as pl
from jax.experimental.pallas import tpu as pltpu
from jax.sharding import PartitionSpec as P

LANES = 128
SUBS = 8
BATCH = 4
VMEM_LIMIT = 20 * 1024 * 1024
VMEM_WHOLE = 58 * 1024 * 1024


def split3(x):
    hi = x.astype(jnp.bfloat16)
    rest = x - hi.astype(jnp.float32)
    mid = rest.astype(jnp.bfloat16)
    low = (rest - mid.astype(jnp.float32)).astype(jnp.bfloat16)
    return [hi, mid, low]


def pack_kernel(slots, rows_hbm, owner_hbm, cell_hbm, out_ref, rows_ref, owner_ref, cell_ref, sems):
    steps, count, width = rows_ref.shape
    owners = count
    parts = width // LANES
    stride = out_ref.shape[0] // owners
    small = [
        pltpu.make_async_copy(owner_hbm, owner_ref, sems.at[steps]),
        pltpu.make_async_copy(cell_hbm, cell_ref, sems.at[steps + 1]),
    ]
    large = [
        pltpu.make_async_copy(rows_hbm.at[step], rows_ref.at[step], sems.at[step]) for step in range(steps)
    ]
    for copy in small + large:
        copy.start()
    dest = lax.broadcasted_iota(jnp.int32, (owners, count), 0)
    lane = lax.broadcasted_iota(jnp.int32, (owners, count), 1)
    before = (dest < lane).astype(jnp.bfloat16)
    cells = jnp.zeros((owners, LANES), jnp.float32)
    for copy in small:
        copy.wait()
    for step in range(steps):
        hits = owner_ref[step] == dest
        hits_f = hits.astype(jnp.float32)
        prior = jnp.dot(hits_f.astype(jnp.bfloat16), before, preferred_element_type=jnp.float32)
        large[step].wait()
        terms = jnp.concatenate(split3(rows_ref[step]), axis=0)
        marks = (cell_ref[step] + 1).astype(jnp.float32)
        for k in range(slots):
            slot = step * slots + k
            pick = jnp.where(prior == float(k), hits_f, 0.0)
            pick_b = pick.astype(jnp.bfloat16)
            out = jnp.dot(
                jnp.concatenate([pick_b] * 3, axis=1), terms, preferred_element_type=jnp.float32
            )
            for part in range(parts):
                out_ref[pl.ds(slot * parts + part, owners, stride=stride), :] = out[
                    :, part * LANES : (part + 1) * LANES
                ]
            mark = jnp.sum(pick * marks, axis=1, keepdims=True)
            cells = jnp.where(lane == slot, mark, cells)
    out_ref[pl.ds(stride - 1, owners, stride=stride), :] = cells


def spread_rows(step, slots, got_ref, width):
    parts = width // LANES
    stride = parts * slots * 3 + 1
    sources = got_ref.shape[0] // stride
    marks = got_ref[pl.ds(stride - 1, sources, stride=stride), :]
    where_to = lax.broadcasted_iota(jnp.int32, (sources, SUBS * LANES), 1)
    terms, onehots = [], []
    for k in range(slots):
        slot = step * slots + k
        cols = []
        for part in range(parts):
            block = got_ref[pl.ds(slot * parts + part, sources, stride=stride), :]
            cols.append(block.T)
        turned = jnp.concatenate(cols, axis=0)
        terms += split3(turned)
        cell = marks[:, slot : slot + 1].astype(jnp.int32) - 1
        onehot = (cell == where_to).astype(jnp.float32).astype(jnp.bfloat16)
        onehots += [onehot] * 3
    return jnp.dot(
        jnp.concatenate(terms, axis=1),
        jnp.concatenate(onehots, axis=0),
        preferred_element_type=jnp.float32,
    )


def columns_store(m_ref, rim, column_ref, fields, levels):
    lane = lax.broadcasted_iota(jnp.int32, (SUBS, LANES), 1)
    even = lane % 2 == 0
    for f in range(fields):
        halves = [jnp.zeros((SUBS, LANES), jnp.float32)] * 2
        for group in range(levels // SUBS):
            for y in range(SUBS):
                at = group * SUBS + y
                plane = m_ref[rows_of((y * fields + f) * levels, group), :]
                turned = plane if at == 0 else pltpu.roll(plane, at, 1)
                here = (lane == at) | (lane == (at - 1) % LANES)
                halves[at % 2] = jnp.where(here, turned, halves[at % 2])
        column_ref[f * SUBS : (f + 1) * SUBS, :] = jnp.where(even, halves[0], halves[1])
        column_ref[(fields + f) * SUBS : (fields + f + 1) * SUBS, :] = jnp.where(even, halves[1], halves[0])
    column_ref[2 * fields * SUBS :, :] = rim


def columns_turn(cols, groups):
    return [pltpu.roll(c, LANES - groups * SUBS, 1) for c in cols]


def columns_load(lon_even, first_ref, second_ref, fields):
    even = lax.broadcasted_iota(jnp.int32, (SUBS, LANES), 1) % 2 == 0

    def rows(i):
        one, two = first_ref[i * SUBS : (i + 1) * SUBS, :], second_ref[i * SUBS : (i + 1) * SUBS, :]
        return jnp.where(lon_even, one, two), jnp.where(lon_even, two, one)

    cols = []
    for f in range(fields):
        west = pltpu.roll(rows(fields + f)[0], 1, 1)
        east = pltpu.roll(rows(f)[1], LANES - 1, 1)
        cols += [jnp.where(even, west, east), jnp.where(even, east, west)]
    return cols + [pltpu.roll(rows(2 * fields)[0], 1, 1)]


def turn_to_first(col, at):
    return col if at == 0 else pltpu.roll(col, LANES - at, 1)


def rows_of(base, group):
    if isinstance(group, int):
        return pl.ds(base + group * SUBS, SUBS)
    return pl.ds(pl.multiple_of(base + group * SUBS, SUBS), SUBS)


def slabs_store(lat_even, m_ref, first_ref, second_ref, width):
    for i in range(width // SUBS):
        rows = slice(i * SUBS, (i + 1) * SUBS)
        south = m_ref[rows, :]
        north = m_ref[(SUBS - 1) * width + i * SUBS : (SUBS - 1) * width + (i + 1) * SUBS, :]
        first_ref[rows, :] = jnp.where(lat_even, north, south)
        second_ref[rows, :] = jnp.where(lat_even, south, north)


def parity(ref, i):
    return jnp.full((SUBS, LANES), ref[i], jnp.int32) == 0


def low_store(m_ref, low_ref, fields, levels):
    for f in range(fields):
        low_ref[f * SUBS : (f + 1) * SUBS, :] = m_ref[
            pl.ds(f * levels + levels - 1, SUBS, stride=fields * levels), :
        ]


def first_kernel(
    step, slots, fields, levels, odd_ref, got_ref, mask_ref, rim_ref, m_ref, slab1_ref, slab2_ref, column_ref, low_ref
):
    width = fields * levels
    out = spread_rows(step, slots, got_ref, width)
    for y in range(SUBS):
        m_ref[y * width : (y + 1) * width, :] = out[:, y * LANES : (y + 1) * LANES] * mask_ref[y : y + 1, :]
    slabs_store(parity(odd_ref, 0), m_ref, slab1_ref, slab2_ref, width)
    columns_store(m_ref, rim_ref[step * SUBS : (step + 1) * SUBS, :], column_ref, fields, levels)
    low_store(m_ref, low_ref, fields, levels)


def forcing_kernel(step, slots, width, got_ref, f_ref):
    out = spread_rows(step, slots, got_ref, width)
    for y in range(SUBS):
        f_ref[y * width : (y + 1) * width, :] = out[:, y * LANES : (y + 1) * LANES]


def rim_kernel(vel_ref, dif_ref, rim_ref, vel_row, dif_row, sems):
    copies = [
        pltpu.make_async_copy(src.at[:, 1, :, SUBS - 1, :], dst, sems.at[i])
        for i, (src, dst) in enumerate(((vel_ref, vel_row), (dif_ref, dif_row)))
    ]
    for copy in copies:
        copy.start()
    for copy in copies:
        copy.wait()
    steps, levels, lanes = vel_row.shape
    rim_ref[...] = (jnp.minimum(vel_row[...], 0.0) - dif_row[...]).reshape(steps * levels, lanes)


def coefficient_kernel(steps, levels, vel_ref, dif_ref, open_ref, *outs):
    tables, rim_ref = outs[:-1], outs[-1]
    lane = lax.broadcasted_iota(jnp.int32, (SUBS, LANES), 1)
    for step in range(steps):
        up_e_ref, down_w_ref, up_n_ref, down_n_ref = tables[4 * step : 4 * step + 4]
        east, north = 2 * step * levels * SUBS, (2 * step + 1) * levels * SUBS
        for y in range(SUBS):
            rows = slice(y * levels, (y + 1) * levels)
            w = vel_ref[pl.ds(east + y, levels, stride=SUBS), :]
            k = dif_ref[pl.ds(east + y, levels, stride=SUBS), :]
            up_e_ref[rows, :] = jnp.maximum(w, 0.0) + k
            down_w_ref[rows, :] = pltpu.roll(jnp.minimum(w, 0.0) - k, 1, 1)
            w = vel_ref[pl.ds(north + y, levels, stride=SUBS), :]
            k = dif_ref[pl.ds(north + y, levels, stride=SUBS), :]
            up = jnp.maximum(w, 0.0) + k
            up_n_ref[rows, :] = up * open_ref[...] if y == SUBS - 1 else up
            down_n_ref[rows, :] = jnp.minimum(w, 0.0) - k
        rim = jnp.zeros((SUBS, LANES), jnp.float32)
        for group in range(levels // SUBS):
            for y in range(SUBS):
                at = group * SUBS + y
                plane = down_w_ref[rows_of(y * levels, group), :]
                to = (at - 1) % LANES
                rim = jnp.where(lane == to, plane if to == 0 else pltpu.roll(plane, to, 1), rim)
        rim_ref[step * SUBS : (step + 1) * SUBS, :] = rim


def step_kernel(
    last,
    step,
    fields,
    levels,
    mix_ref,
    air_ref,
    odd_ref,
    m_ref,
    up_e_ref,
    down_w_ref,
    up_n_ref,
    down_n_ref,
    north_rim_ref,
    sea_ref,
    mask_ref,
    from_slab1_ref,
    from_slab2_ref,
    from_column1_ref,
    from_column2_ref,
    from_low_ref,
    *rest,
):
    if last:
        sent_ref, out_ref, sems = rest
    else:
        f_ref, rim_ref, out_ref, slab1_ref, slab2_ref, column_ref, low_ref = rest
    width = fields * levels
    batch = BATCH
    lane = lax.broadcasted_iota(jnp.int32, (SUBS, LANES), 1)
    sub = lax.broadcasted_iota(jnp.int32, (SUBS, LANES), 0)
    at_west, at_east = lane == 0, lane == LANES - 1
    mix = [[mix_ref[f, g] for g in range(fields)] for f in range(fields)]
    lat_even, lon_even = parity(odd_ref, 0), parity(odd_ref, 1)
    sea = sea_ref[...]
    coupled = []
    for g in range(fields):
        total = jnp.zeros((SUBS, LANES), jnp.float32)
        for f in range(fields):
            total = total + air_ref[f, g] * from_low_ref[f * SUBS : (f + 1) * SUBS, :]
        coupled.append(sea * total)

    def batch_step(group0, halos):
        for u in range(batch):
            group = group0 + u
            for y in range(SUBS):
                at = u * SUBS + y
                up_e = up_e_ref[rows_of(y * levels, group), :]
                down_w = jnp.where(
                    at_west, turn_to_first(halos[2 * fields], at), down_w_ref[rows_of(y * levels, group), :]
                )
                up_n = up_n_ref[rows_of(y * levels, group), :]
                if y == 0:
                    down_s = north_rim_ref[rows_of(step * levels, group), :]
                else:
                    down_s = down_n_ref[rows_of((y - 1) * levels, group), :]
                planes = [m_ref[rows_of(y * width + f * levels, group), :] for f in range(fields)]
                for g in range(fields):
                    m = planes[g]
                    if y == 0 or y == SUBS - 1:
                        one = from_slab1_ref[rows_of(g * levels, group), :]
                        two = from_slab2_ref[rows_of(g * levels, group), :]
                    if y == SUBS - 1:
                        north = jnp.where(lat_even, one, two)
                    else:
                        north = m_ref[rows_of((y + 1) * width + g * levels, group), :]
                    if y == 0:
                        south = jnp.where(lat_even, two, one)
                    else:
                        south = m_ref[rows_of((y - 1) * width + g * levels, group), :]
                    halo = turn_to_first(halos[2 * g + at % 2], at)
                    east = jnp.where(at_east, halo, pltpu.roll(m, LANES - 1, 1))
                    west = jnp.where(at_west, halo, pltpu.roll(m, 1, 1))
                    result = m
                    for f in range(fields):
                        result = result + mix[f][g] * planes[f]
                    result = result + (up_e * (east - m) + down_w * (m - west))
                    result = result + (up_n * (north - m) + down_s * (m - south))
                    if isinstance(group, int) and group == 0:
                        result = result + jnp.where(sub == 0, coupled[g][y : y + 1, :], 0.0)
                    if last:
                        out_ref[pl.ds(g * levels * SUBS + y + group * (SUBS * SUBS), SUBS, stride=SUBS), :] = result
                        continue
                    rows = rows_of(y * width + g * levels, group)
                    result = (result + f_ref[rows, :]) * mask_ref[y : y + 1, :]
                    out_ref[rows, :] = result
        if last:
            for f in range(fields):
                rows = pl.ds((f * levels + group0 * SUBS) * SUBS, batch * SUBS * SUBS)
                pltpu.make_async_copy(
                    out_ref.at[rows], sent_ref.at[rows], sems.at[f * levels // (batch * SUBS) + group0 // batch]
                ).start()
        return columns_turn(halos, batch)

    halos = columns_load(lon_even, from_column1_ref, from_column2_ref, fields)
    halos = batch_step(0, halos)

    def body(i, halos):
        return tuple(batch_step(i * batch, list(halos)))

    lax.fori_loop(1, levels // (SUBS * batch), body, tuple(halos))
    if last:
        for i in range(fields * levels // (batch * SUBS)):
            rows = pl.ds(i * batch * SUBS * SUBS, batch * SUBS * SUBS)
            pltpu.make_async_copy(out_ref.at[rows], sent_ref.at[rows], sems.at[i]).wait()
    else:
        columns_store(out_ref, rim_ref[(step - 1) * SUBS : step * SUBS, :], column_ref, fields, levels)
        slabs_store(lat_even, out_ref, slab1_ref, slab2_ref, width)
        low_store(out_ref, low_ref, fields, levels)


def params(limit=VMEM_LIMIT):
    return pltpu.CompilerParams(vmem_limit_bytes=limit)


def swaps(axis, start, closed):
    count = lax.axis_size(axis)
    pairs = []
    for i in range(start, count if closed else count - 1, 2):
        j = (i + 1) % count
        pairs += [(i, j), (j, i)]
    return pairs


def shards(innovations, obs_owner, obs_cell, velocity, diffusion, mixing, air_sea, sea_mask):
    lat_count = lax.axis_size("lat")
    lon_count = lax.axis_size("lon")
    owners = lat_count * lon_count
    steps, levels, lat_rows, lon_cols = (velocity.shape[i] for i in (1, 3, 4, 5))
    fields = mixing.shape[1]
    width = fields * levels
    count = innovations.shape[2]
    slots = 2
    assert (lat_rows, lon_cols, levels, count, owners, steps) == (SUBS, LANES, LANES, LANES, LANES, 3)
    f32 = functools.partial(jax.ShapeDtypeStruct, dtype=jnp.float32)
    stride = steps * slots * width // LANES + 1

    is_ocean = lax.axis_index("comp") == 1
    sea_float = sea_mask.astype(jnp.float32)
    mask = jnp.where(is_ocean, sea_float, jnp.ones_like(sea_float))
    opened = jnp.full((1, lon_cols), lax.axis_index("lat") < lat_count - 1, jnp.float32)
    smem = pl.BlockSpec(memory_space=pltpu.SMEM)
    vmem = pl.BlockSpec(memory_space=pltpu.VMEM)
    anywhere = pl.BlockSpec(memory_space=pltpu.HBM)
    speeds, diffuse = velocity[0], diffusion[0]

    north_rims = pl.pallas_call(
        rim_kernel,
        out_shape=f32((steps * levels, LANES)),
        in_specs=[anywhere] * 2,
        scratch_shapes=[pltpu.VMEM((steps, levels, LANES), jnp.float32)] * 2 + [pltpu.SemaphoreType.DMA((2,))],
        compiler_params=params(VMEM_WHOLE),
        name="rim",
    )(speeds, diffuse)
    north_rims = lax.ppermute(
        north_rims, "lat", [(i, i + 1) for i in range(lat_count - 1)]
    )

    sent = pl.pallas_call(
        functools.partial(pack_kernel, slots),
        out_shape=f32((owners * stride, LANES)),
        in_specs=[anywhere] * 3,
        scratch_shapes=[
            pltpu.VMEM((steps, count, width), jnp.float32),
            pltpu.VMEM((steps, 1, count), jnp.int32),
            pltpu.VMEM((steps, 1, count), jnp.int32),
            pltpu.SemaphoreType.DMA((steps + 2,)),
        ],
        compiler_params=params(VMEM_WHOLE),
        name="pack",
    )(
        innovations[0],
        obs_owner.reshape(steps, 1, count),
        obs_cell.reshape(steps, 1, count),
    )
    got = lax.all_to_all(
        sent.reshape(owners, 1, stride * LANES), ("lat", "lon"), split_axis=0, concat_axis=0, tiled=True
    ).reshape(owners * stride, LANES)

    table = f32((levels * SUBS, LANES))
    *tables, east_rims = pl.pallas_call(
        functools.partial(coefficient_kernel, steps, levels),
        out_shape=[table] * (4 * steps) + [f32((steps * SUBS, LANES))],
        compiler_params=params(),
        cost_estimate=pl.CostEstimate(flops=1 << 22, bytes_accessed=1 << 23, transcendentals=0),
        name="coefficients",
    )(
        speeds.reshape(steps * 2 * levels * SUBS, LANES),
        diffuse.reshape(steps * 2 * levels * SUBS, LANES),
        opened,
    )
    odd = jnp.stack([lax.axis_index("lat") % 2, lax.axis_index("lon") % 2]).astype(jnp.int32)
    edge_shapes = [
        f32((width * SUBS, LANES)),
        f32((width, LANES)),
        f32((width, LANES)),
        f32(((2 * fields + 1) * SUBS, LANES)),
        f32((fields * SUBS, LANES)),
    ]
    m, slab1, slab2, columns, low = pl.pallas_call(
        functools.partial(first_kernel, steps - 1, slots, fields, levels),
        out_shape=edge_shapes,
        in_specs=[smem] + [vmem] * 3,
        compiler_params=params(),
        name="first",
    )(odd, got, mask, east_rims)
    for step in reversed(range(steps)):
        last = step == 0
        operands = [
            mixing[0],
            air_sea,
            odd,
            m,
            *tables[4 * step : 4 * step + 4],
            north_rims,
            sea_float,
            mask,
            lax.ppermute(slab1, "lat", swaps("lat", 0, False)),
            lax.ppermute(slab2, "lat", swaps("lat", 1, False)),
            lax.ppermute(columns, "lon", swaps("lon", 1, True)),
            lax.ppermute(columns, "lon", swaps("lon", 0, True)),
            lax.ppermute(low, "comp", [(0, 1)]),
        ]
        if not last:
            operands.append(
                pl.pallas_call(
                    functools.partial(forcing_kernel, step - 1, slots, width),
                    out_shape=f32((width * SUBS, LANES)),
                    compiler_params=params(),
                    cost_estimate=pl.CostEstimate(
                        flops=2 * 3 * width * 2 * LANES * SUBS * LANES,
                        bytes_accessed=4 * (owners * stride * LANES + width * SUBS * LANES),
                        transcendentals=0,
                    ),
                    name="forcing",
                )(got)
            )
            operands.append(east_rims)
        result = pl.pallas_call(
            functools.partial(step_kernel, last, step, fields, levels),
            out_shape=edge_shapes[:1] if last else edge_shapes,
            in_specs=[smem] * 3 + [vmem] * (len(operands) - 3),
            out_specs=[anywhere] if last else [vmem] * len(edge_shapes),
            scratch_shapes=[
                pltpu.VMEM((width * SUBS, LANES), jnp.float32),
                pltpu.SemaphoreType.DMA((width // (BATCH * SUBS),)),
            ]
            if last
            else [],
            compiler_params=params(),
            name="step",
        )(*operands)
        if last:
            m = result[0]
        else:
            m, slab1, slab2, columns, low = result
    return m.reshape(1, fields, levels, lat_rows, lon_cols)


def solution(mesh):
    return jax.shard_map(
        shards,
        mesh=mesh,
        in_specs=(
            P("comp", None, ("lat", "lon"), None),
            P("comp", None, ("lat", "lon"), None),
            P("comp", None, ("lat", "lon")),
            P("comp", None, None, None, "lat", "lon"),
            P("comp", None, None, None, "lat", "lon"),
            P("comp", None, None),
            P(),
            P("lat", "lon"),
        ),
        out_specs=P("comp", None, None, "lat", "lon"),
        check_vma=False,
    )
```

```python
import functools

import jax
import jax.numpy as jnp
from jax import lax
from jax.experimental import pallas as pl
from jax.experimental.pallas import tpu as pltpu
from jax.sharding import PartitionSpec as P

LANES = 128
SUBS = 8
BATCH = 4
VMEM_LIMIT = 20 * 1024 * 1024
VMEM_WHOLE = 58 * 1024 * 1024


def split3(x):
    hi = x.astype(jnp.bfloat16)
    rest = x - hi.astype(jnp.float32)
    mid = rest.astype(jnp.bfloat16)
    low = (rest - mid.astype(jnp.float32)).astype(jnp.bfloat16)
    return [hi, mid, low]


def pack_kernel(slots, rows_hbm, owner_hbm, cell_hbm, out_ref, rows_ref, owner_ref, cell_ref, sems):
    steps, count, width = rows_ref.shape
    owners = count
    parts = width // LANES
    stride = out_ref.shape[0] // owners
    small = [
        pltpu.make_async_copy(owner_hbm, owner_ref, sems.at[steps]),
        pltpu.make_async_copy(cell_hbm, cell_ref, sems.at[steps + 1]),
    ]
    large = [
        pltpu.make_async_copy(rows_hbm.at[step], rows_ref.at[step], sems.at[step]) for step in range(steps)
    ]
    for copy in small + large:
        copy.start()
    dest = lax.broadcasted_iota(jnp.int32, (owners, count), 0)
    lane = lax.broadcasted_iota(jnp.int32, (owners, count), 1)
    before = (dest < lane).astype(jnp.bfloat16)
    cells = jnp.zeros((owners, LANES), jnp.float32)
    for copy in small:
        copy.wait()
    for step in range(steps):
        hits = owner_ref[step] == dest
        hits_f = hits.astype(jnp.float32)
        prior = jnp.dot(hits_f.astype(jnp.bfloat16), before, preferred_element_type=jnp.float32)
        large[step].wait()
        terms = jnp.concatenate(split3(rows_ref[step]), axis=0)
        marks = (cell_ref[step] + 1).astype(jnp.float32)
        for k in range(slots):
            slot = step * slots + k
            pick = jnp.where(prior == float(k), hits_f, 0.0)
            pick_b = pick.astype(jnp.bfloat16)
            out = jnp.dot(
                jnp.concatenate([pick_b] * 3, axis=1), terms, preferred_element_type=jnp.float32
            )
            for part in range(parts):
                out_ref[pl.ds(slot * parts + part, owners, stride=stride), :] = out[
                    :, part * LANES : (part + 1) * LANES
                ]
            mark = jnp.sum(pick * marks, axis=1, keepdims=True)
            cells = jnp.where(lane == slot, mark, cells)
    out_ref[pl.ds(stride - 1, owners, stride=stride), :] = cells


def spread_rows(step, slots, got_ref, width):
    parts = width // LANES
    stride = parts * slots * 3 + 1
    sources = got_ref.shape[0] // stride
    marks = got_ref[pl.ds(stride - 1, sources, stride=stride), :]
    where_to = lax.broadcasted_iota(jnp.int32, (sources, SUBS * LANES), 1)
    terms, onehots = [], []
    for k in range(slots):
        slot = step * slots + k
        cols = []
        for part in range(parts):
            block = got_ref[pl.ds(slot * parts + part, sources, stride=stride), :]
            cols.append(block.T)
        turned = jnp.concatenate(cols, axis=0)
        terms += split3(turned)
        cell = marks[:, slot : slot + 1].astype(jnp.int32) - 1
        onehot = (cell == where_to).astype(jnp.float32).astype(jnp.bfloat16)
        onehots += [onehot] * 3
    return jnp.dot(
        jnp.concatenate(terms, axis=1),
        jnp.concatenate(onehots, axis=0),
        preferred_element_type=jnp.float32,
    )


def column_halves(load, fields, groups, ys, halves):
    lane = lax.broadcasted_iota(jnp.int32, (SUBS, LANES), 1)
    for f in range(fields):
        for group in groups:
            for y in ys:
                at = group * SUBS + y
                plane = load(f, group, y)
                turned = plane if at == 0 else pltpu.roll(plane, at, 1)
                here = (lane == at) | (lane == (at - 1) % LANES)
                halves[2 * f + at % 2] = jnp.where(here, turned, halves[2 * f + at % 2])
    return halves


def columns_store(halves, rim, column_ref, fields):
    even = lax.broadcasted_iota(jnp.int32, (SUBS, LANES), 1) % 2 == 0
    for f in range(fields):
        a, b = halves[2 * f], halves[2 * f + 1]
        column_ref[f * SUBS : (f + 1) * SUBS, :] = jnp.where(even, a, b)
        column_ref[(fields + f) * SUBS : (fields + f + 1) * SUBS, :] = jnp.where(even, b, a)
    column_ref[2 * fields * SUBS :, :] = rim


def column_corrections(lon_even, first_ref, second_ref, own_ref, up_rim, fields):
    even = lax.broadcasted_iota(jnp.int32, (SUBS, LANES), 1) % 2 == 0

    def rows(i):
        one, two = first_ref[i * SUBS : (i + 1) * SUBS, :], second_ref[i * SUBS : (i + 1) * SUBS, :]
        return jnp.where(lon_even, one, two), jnp.where(lon_even, two, one)

    rim = pltpu.roll(rows(2 * fields)[0], 1, 1)
    halves = []
    for f in range(fields):
        from_west = pltpu.roll(rows(fields + f)[0], 1, 1)
        from_east = pltpu.roll(rows(f)[1], LANES - 1, 1)
        own_west = own_ref[f * SUBS : (f + 1) * SUBS, :]
        own_east = own_ref[(fields + f) * SUBS : (fields + f + 1) * SUBS, :]
        west = rim * (own_west - from_west)
        east = up_rim * (from_east - own_east)
        halves += [jnp.where(even, west, east), jnp.where(even, east, west)]
    return halves


def turn_to_first(col, at):
    return col if at == 0 else pltpu.roll(col, LANES - at, 1)


def rows_of(base, group):
    if isinstance(group, int):
        return pl.ds(base + group * SUBS, SUBS)
    return pl.ds(pl.multiple_of(base + group * SUBS, SUBS), SUBS)


def slabs_store(lat_even, m_ref, first_ref, second_ref, width):
    for i in range(width // SUBS):
        rows = slice(i * SUBS, (i + 1) * SUBS)
        south = m_ref[rows, :]
        north = m_ref[(SUBS - 1) * width + i * SUBS : (SUBS - 1) * width + (i + 1) * SUBS, :]
        first_ref[rows, :] = jnp.where(lat_even, north, south)
        second_ref[rows, :] = jnp.where(lat_even, south, north)


def parity(ref, i):
    return jnp.full((SUBS, LANES), ref[i], jnp.int32) == 0


def low_store(m_ref, low_ref, fields, levels):
    for f in range(fields):
        low_ref[f * SUBS : (f + 1) * SUBS, :] = m_ref[
            pl.ds(f * levels + levels - 1, SUBS, stride=fields * levels), :
        ]


def first_kernel(
    step, slots, fields, levels, odd_ref, got_ref, mask_ref, rim_ref, m_ref, slab1_ref, slab2_ref, column_ref, low_ref
):
    width = fields * levels
    out = spread_rows(step, slots, got_ref, width)
    for y in range(SUBS):
        m_ref[y * width : (y + 1) * width, :] = out[:, y * LANES : (y + 1) * LANES] * mask_ref[y : y + 1, :]
    slabs_store(parity(odd_ref, 0), m_ref, slab1_ref, slab2_ref, width)
    halves = column_halves(
        lambda f, group, y: m_ref[rows_of((y * fields + f) * levels, group), :],
        fields,
        range(levels // SUBS),
        range(SUBS),
        [jnp.zeros((SUBS, LANES), jnp.float32)] * (2 * fields),
    )
    columns_store(halves, rim_ref[step * SUBS : (step + 1) * SUBS, :], column_ref, fields)
    low_store(m_ref, low_ref, fields, levels)


def forcing_kernel(step, slots, width, got_ref, f_ref):
    out = spread_rows(step, slots, got_ref, width)
    for y in range(SUBS):
        f_ref[y * width : (y + 1) * width, :] = out[:, y * LANES : (y + 1) * LANES]


def rim_kernel(vel_ref, dif_ref, rim_ref, vel_row, dif_row, sems):
    copies = [
        pltpu.make_async_copy(src.at[:, 1, :, SUBS - 1, :], dst, sems.at[i])
        for i, (src, dst) in enumerate(((vel_ref, vel_row), (dif_ref, dif_row)))
    ]
    for copy in copies:
        copy.start()
    for copy in copies:
        copy.wait()
    steps, levels, lanes = vel_row.shape
    rim_ref[...] = (jnp.minimum(vel_row[...], 0.0) - dif_row[...]).reshape(steps * levels, lanes)


def coefficient_kernel(steps, levels, vel_ref, dif_ref, open_ref, mask_ref, *outs):
    tables, (rim_ref, up_rim_ref, mask_column_ref) = outs[:-3], outs[-3:]
    lane = lax.broadcasted_iota(jnp.int32, (SUBS, LANES), 1)
    tall = lax.broadcasted_iota(jnp.int32, (levels, LANES), 1)
    for step in range(steps):
        up_e_ref, down_w_ref, up_n_ref, down_n_ref = tables[4 * step : 4 * step + 4]
        east, north = 2 * step * levels * SUBS, (2 * step + 1) * levels * SUBS
        rim = jnp.zeros((SUBS, LANES), jnp.float32)
        up_rim = rim
        for y in range(SUBS):
            rows = slice(y * levels, (y + 1) * levels)
            w = vel_ref[pl.ds(east + y, levels, stride=SUBS), :]
            k = dif_ref[pl.ds(east + y, levels, stride=SUBS), :]
            up = jnp.maximum(w, 0.0) + k
            down = jnp.minimum(w, 0.0) - k
            for group in range(levels // SUBS):
                at = group * SUBS + y
                part = slice(group * SUBS, (group + 1) * SUBS)
                rim = jnp.where(lane == (at - 1) % LANES, pltpu.roll(down[part, :], at, 1) if at else down[part, :], rim)
                up_rim = jnp.where(lane == (at - 1) % LANES, pltpu.roll(up[part, :], at, 1) if at else up[part, :], up_rim)
            up_e_ref[rows, :] = jnp.where(tall == LANES - 1, 0.0, up)
            down_w_ref[rows, :] = jnp.where(tall == 0, 0.0, pltpu.roll(down, 1, 1))
            w = vel_ref[pl.ds(north + y, levels, stride=SUBS), :]
            k = dif_ref[pl.ds(north + y, levels, stride=SUBS), :]
            up = jnp.maximum(w, 0.0) + k
            up_n_ref[rows, :] = up * open_ref[...] if y == SUBS - 1 else up
            down_n_ref[rows, :] = jnp.minimum(w, 0.0) - k
        rim_ref[step * SUBS : (step + 1) * SUBS, :] = rim
        up_rim_ref[step * SUBS : (step + 1) * SUBS, :] = up_rim
    west, east = jnp.zeros((SUBS, LANES), jnp.float32), jnp.zeros((SUBS, LANES), jnp.float32)
    for group in range(levels // SUBS):
        for y in range(SUBS):
            at = group * SUBS + y
            row = jnp.broadcast_to(mask_ref[y : y + 1, :], (SUBS, LANES))
            turned = pltpu.roll(row, at, 1) if at else row
            west = jnp.where(lane == at, turned, west)
            east = jnp.where(lane == (at - 1) % LANES, turned, east)
    mask_column_ref[:SUBS, :] = west
    mask_column_ref[SUBS:, :] = east


def settled(f, group, y, at, p_ref, m_ref, halves, edge, coupled, up_n_ref, rim_row, from_south, from_north, fields, levels):
    rows = rows_of((y * fields + f) * levels, group)
    result = p_ref[rows, :] + jnp.where(edge, turn_to_first(halves[2 * f + at % 2], at), 0.0)
    if y == 0:
        result = result + rim_row(group) * (m_ref[rows, :] - from_south(f, group))
    if y == SUBS - 1:
        up = up_n_ref[rows_of(y * levels, group), :]
        result = result + up * (from_north(f, group) - m_ref[rows, :])
    if isinstance(group, int) and group == 0:
        sub = lax.broadcasted_iota(jnp.int32, (SUBS, LANES), 0)
        result = result + jnp.where(sub == 0, coupled(f, y), 0.0)
    return result


def slab_readers(lat_even, slab1_ref, slab2_ref, levels):
    def south(f, group):
        rows = rows_of(f * levels, group)
        return jnp.where(lat_even, slab2_ref[rows, :], slab1_ref[rows, :])

    def north(f, group):
        rows = rows_of(f * levels, group)
        return jnp.where(lat_even, slab1_ref[rows, :], slab2_ref[rows, :])

    return south, north


def coupling(air_ref, sea_ref, from_low_ref, fields):
    sea = sea_ref[...]
    planes = []
    for g in range(fields):
        total = jnp.zeros((SUBS, LANES), jnp.float32)
        for f in range(fields):
            total = total + air_ref[f, g] * from_low_ref[f * SUBS : (f + 1) * SUBS, :]
        planes.append(sea * total)
    return planes


def partial_kernel(settle, step, fields, levels, mix_ref, odd_ref, m_ref, tables, forcing_ref, before, outs):
    up_e_ref, down_w_ref, up_n_ref, down_n_ref = tables
    width = fields * levels
    lane = lax.broadcasted_iota(jnp.int32, (SUBS, LANES), 1)
    edge = (lane == 0) | (lane == LANES - 1)
    batches = levels // (SUBS * BATCH)
    if settle:
        old_p_ref, old_m_ref, old_up_n_ref, slab1_ref, slab2_ref, half_ref, couple_ref, rim_ref, mask_ref = before
        south, north = slab_readers(parity(odd_ref, 0), slab1_ref, slab2_ref, levels)

        def settle_batch(group0, halves):
            for u in range(BATCH):
                group = group0 + u
                for y in range(SUBS):
                    for f in range(fields):
                        plane = settled(
                            f,
                            group,
                            y,
                            u * SUBS + y,
                            old_p_ref,
                            old_m_ref,
                            halves,
                            edge,
                            lambda f, y: couple_ref[f * SUBS + y : f * SUBS + y + 1, :],
                            old_up_n_ref,
                            lambda group: rim_ref[rows_of((step + 1) * levels, group), :],
                            south,
                            north,
                            fields,
                            levels,
                        )
                        m_ref[rows_of((y * fields + f) * levels, group), :] = plane * mask_ref[y : y + 1, :]
            return tuple(pltpu.roll(h, LANES - BATCH * SUBS, 1) for h in halves)

        halves = settle_batch(0, [half_ref[i * SUBS : (i + 1) * SUBS, :] for i in range(2 * fields)])
        lax.fori_loop(1, batches, lambda i, halves: settle_batch(i * BATCH, halves), halves)
    p_ref = outs[0]
    mix = [[mix_ref[f, g] for g in range(fields)] for f in range(fields)]

    def body(i, carry):
        for u in range(BATCH):
            group = i * BATCH + u
            for y in range(SUBS):
                up_e = up_e_ref[rows_of(y * levels, group), :]
                down_w = down_w_ref[rows_of(y * levels, group), :]
                planes = [m_ref[rows_of(y * width + f * levels, group), :] for f in range(fields)]
                for g in range(fields):
                    m = planes[g]
                    rows = rows_of(y * width + g * levels, group)
                    result = m if forcing_ref is None else m + forcing_ref[rows, :]
                    for f in range(fields):
                        result = result + mix[f][g] * planes[f]
                    result = result + up_e * (pltpu.roll(m, LANES - 1, 1) - m)
                    result = result + down_w * (m - pltpu.roll(m, 1, 1))
                    if y < SUBS - 1:
                        up_n = up_n_ref[rows_of(y * levels, group), :]
                        result = result + up_n * (m_ref[rows_of((y + 1) * width + g * levels, group), :] - m)
                    if y > 0:
                        down_s = down_n_ref[rows_of((y - 1) * levels, group), :]
                        result = result + down_s * (m - m_ref[rows_of((y - 1) * width + g * levels, group), :])
                    p_ref[rows, :] = result
        return carry

    lax.fori_loop(0, batches, body, 0)
    if len(outs) > 1:
        halves = column_halves(
            lambda f, group, y: p_ref[rows_of((y * fields + f) * levels, group), :],
            fields,
            range(levels // SUBS),
            range(SUBS),
            [jnp.zeros((SUBS, LANES), jnp.float32)] * (2 * fields),
        )
        for i, half in enumerate(halves):
            outs[1][i * SUBS : (i + 1) * SUBS, :] = half


def start_kernel(step, fields, levels, mix_ref, odd_ref, m_ref, a_ref, b_ref, c_ref, d_ref, f_ref, *outs):
    partial_kernel(False, step, fields, levels, mix_ref, odd_ref, m_ref, (a_ref, b_ref, c_ref, d_ref), f_ref, None, outs)


def inner_kernel(last, step, fields, levels, mix_ref, odd_ref, a_ref, b_ref, c_ref, d_ref, *rest):
    tables = (a_ref, b_ref, c_ref, d_ref)
    before, rest = rest[:9], rest[9:]
    f_ref = None
    if not last:
        f_ref, rest = rest[0], rest[1:]
    partial_kernel(True, step, fields, levels, mix_ref, odd_ref, rest[0], tables, f_ref, before, rest[1:])


def edge_kernel(
    step,
    fields,
    levels,
    air_ref,
    odd_ref,
    p_ref,
    p_half_ref,
    m_ref,
    up_n_ref,
    own_column_ref,
    rim_ref,
    up_rim_ref,
    north_rim_ref,
    sea_ref,
    mask_ref,
    mask_column_ref,
    from_slab1_ref,
    from_slab2_ref,
    from_column1_ref,
    from_column2_ref,
    from_low_ref,
    slab1_ref,
    slab2_ref,
    column_ref,
    low_ref,
    half_ref,
    couple_ref,
):
    lane = lax.broadcasted_iota(jnp.int32, (SUBS, LANES), 1)
    edge = (lane == 0) | (lane == LANES - 1)
    even = lane % 2 == 0
    lat_even, lon_even = parity(odd_ref, 0), parity(odd_ref, 1)
    south, north = slab_readers(lat_even, from_slab1_ref, from_slab2_ref, levels)
    coupled = coupling(air_ref, sea_ref, from_low_ref, fields)
    for g in range(fields):
        couple_ref[g * SUBS : (g + 1) * SUBS, :] = coupled[g]
    halves = column_corrections(
        lon_even,
        from_column1_ref,
        from_column2_ref,
        own_column_ref,
        up_rim_ref[step * SUBS : (step + 1) * SUBS, :],
        fields,
    )
    for i, half in enumerate(halves):
        half_ref[i * SUBS : (i + 1) * SUBS, :] = half
    west, east = mask_column_ref[:SUBS, :], mask_column_ref[SUBS:, :]
    masks = [jnp.where(even, west, east), jnp.where(even, east, west)]
    following = [
        (p_half_ref[i * SUBS : (i + 1) * SUBS, :] + half) * masks[i % 2] for i, half in enumerate(halves)
    ]
    groups = levels // SUBS

    def plane(f, group, y):
        full = settled(
            f,
            group,
            y,
            group * SUBS + y,
            p_ref,
            m_ref,
            halves,
            edge,
            lambda f, y: coupled[f][y : y + 1, :],
            up_n_ref,
            lambda group: north_rim_ref[rows_of(step * levels, group), :],
            south,
            north,
            fields,
            levels,
        )
        return full * mask_ref[y : y + 1, :]

    for f in range(fields):
        for group in range(groups):
            ends = [plane(f, group, 0), plane(f, group, SUBS - 1)]
            rows = rows_of(f * levels, group)
            slab1_ref[rows, :] = jnp.where(lat_even, ends[1], ends[0])
            slab2_ref[rows, :] = jnp.where(lat_even, ends[0], ends[1])
            whole = {0: ends[0], SUBS - 1: ends[1]}
            if group == 0 or group == groups - 1:
                for y in range(1, SUBS - 1):
                    whole[y] = plane(f, group, y)
            if group == groups - 1:
                for y in range(SUBS):
                    low_ref[f * SUBS + y : f * SUBS + y + 1, :] = whole[y][SUBS - 1 :, :]
            ys = range(SUBS) if group == 0 else (0, SUBS - 1)
            part = column_halves(
                lambda _, group, y, whole=whole: whole[y], 1, (group,), ys, following[2 * f : 2 * f + 2]
            )
            following[2 * f : 2 * f + 2] = part
    columns_store(following, rim_ref[(step - 1) * SUBS : step * SUBS, :], column_ref, fields)


def last_kernel(
    fields,
    levels,
    air_ref,
    odd_ref,
    p_ref,
    m_ref,
    up_n_ref,
    own_column_ref,
    up_rim_ref,
    north_rim_ref,
    sea_ref,
    from_slab1_ref,
    from_slab2_ref,
    from_column1_ref,
    from_column2_ref,
    from_low_ref,
    sent_ref,
    out_ref,
    sems,
):
    lane = lax.broadcasted_iota(jnp.int32, (SUBS, LANES), 1)
    edge = (lane == 0) | (lane == LANES - 1)
    south, north = slab_readers(parity(odd_ref, 0), from_slab1_ref, from_slab2_ref, levels)
    coupled = coupling(air_ref, sea_ref, from_low_ref, fields)
    halves = column_corrections(
        parity(odd_ref, 1), from_column1_ref, from_column2_ref, own_column_ref, up_rim_ref[:SUBS, :], fields
    )
    batches = levels // (SUBS * BATCH)

    def pieces(i):
        for f in range(fields):
            rows = pl.ds((f * levels + i * BATCH * SUBS) * SUBS, BATCH * SUBS * SUBS)
            yield pltpu.make_async_copy(out_ref.at[rows], sent_ref.at[rows], sems.at[f * batches + i])

    def batch(i, halves):
        for u in range(BATCH):
            group = i * BATCH + u
            for y in range(SUBS):
                for f in range(fields):
                    out_ref[pl.ds(f * levels * SUBS + y + group * (SUBS * SUBS), SUBS, stride=SUBS), :] = settled(
                        f,
                        group,
                        y,
                        u * SUBS + y,
                        p_ref,
                        m_ref,
                        halves,
                        edge,
                        lambda f, y: coupled[f][y : y + 1, :],
                        up_n_ref,
                        lambda group: north_rim_ref[rows_of(0, group), :],
                        south,
                        north,
                        fields,
                        levels,
                    )
        for copy in pieces(i):
            copy.start()
        return tuple(pltpu.roll(h, LANES - BATCH * SUBS, 1) for h in halves)

    lax.fori_loop(1, batches, batch, batch(0, halves))
    for i in range(batches):
        for copy in pieces(i):
            copy.wait()


def params(limit=VMEM_LIMIT):
    return pltpu.CompilerParams(vmem_limit_bytes=limit)


def swaps(axis, start, closed):
    count = lax.axis_size(axis)
    pairs = []
    for i in range(start, count if closed else count - 1, 2):
        j = (i + 1) % count
        pairs += [(i, j), (j, i)]
    return pairs


def shards(innovations, obs_owner, obs_cell, velocity, diffusion, mixing, air_sea, sea_mask):
    lat_count = lax.axis_size("lat")
    lon_count = lax.axis_size("lon")
    owners = lat_count * lon_count
    steps, levels, lat_rows, lon_cols = (velocity.shape[i] for i in (1, 3, 4, 5))
    fields = mixing.shape[1]
    width = fields * levels
    count = innovations.shape[2]
    slots = 2
    assert (lat_rows, lon_cols, levels, count, owners, steps) == (SUBS, LANES, LANES, LANES, LANES, 3)
    f32 = functools.partial(jax.ShapeDtypeStruct, dtype=jnp.float32)
    stride = steps * slots * width // LANES + 1

    is_ocean = lax.axis_index("comp") == 1
    sea_float = sea_mask.astype(jnp.float32)
    mask = jnp.where(is_ocean, sea_float, jnp.ones_like(sea_float))
    opened = jnp.full((1, lon_cols), lax.axis_index("lat") < lat_count - 1, jnp.float32)
    smem = pl.BlockSpec(memory_space=pltpu.SMEM)
    vmem = pl.BlockSpec(memory_space=pltpu.VMEM)
    anywhere = pl.BlockSpec(memory_space=pltpu.HBM)
    speeds, diffuse = velocity[0], diffusion[0]

    north_rims = pl.pallas_call(
        rim_kernel,
        out_shape=f32((steps * levels, LANES)),
        in_specs=[anywhere] * 2,
        scratch_shapes=[pltpu.VMEM((steps, levels, LANES), jnp.float32)] * 2 + [pltpu.SemaphoreType.DMA((2,))],
        compiler_params=params(VMEM_WHOLE),
        name="rim",
    )(speeds, diffuse)
    north_rims = lax.ppermute(
        north_rims, "lat", [(i, i + 1) for i in range(lat_count - 1)]
    )

    sent = pl.pallas_call(
        functools.partial(pack_kernel, slots),
        out_shape=f32((owners * stride, LANES)),
        in_specs=[anywhere] * 3,
        scratch_shapes=[
            pltpu.VMEM((steps, count, width), jnp.float32),
            pltpu.VMEM((steps, 1, count), jnp.int32),
            pltpu.VMEM((steps, 1, count), jnp.int32),
            pltpu.SemaphoreType.DMA((steps + 2,)),
        ],
        compiler_params=params(VMEM_WHOLE),
        name="pack",
    )(
        innovations[0],
        obs_owner.reshape(steps, 1, count),
        obs_cell.reshape(steps, 1, count),
    )
    got = lax.all_to_all(
        sent.reshape(owners, 1, stride * LANES), ("lat", "lon"), split_axis=0, concat_axis=0, tiled=True
    ).reshape(owners * stride, LANES)

    table = f32((levels * SUBS, LANES))
    *tables, east_rims, up_rims, mask_columns = pl.pallas_call(
        functools.partial(coefficient_kernel, steps, levels),
        out_shape=[table] * (4 * steps) + [f32((steps * SUBS, LANES))] * 2 + [f32((2 * SUBS, LANES))],
        compiler_params=params(),
        cost_estimate=pl.CostEstimate(flops=1 << 22, bytes_accessed=1 << 23, transcendentals=0),
        name="coefficients",
    )(
        speeds.reshape(steps * 2 * levels * SUBS, LANES),
        diffuse.reshape(steps * 2 * levels * SUBS, LANES),
        opened,
        mask,
    )
    odd = jnp.stack([lax.axis_index("lat") % 2, lax.axis_index("lon") % 2]).astype(jnp.int32)
    whole = f32((width * SUBS, LANES))
    half = f32((2 * fields * SUBS, LANES))
    low_shape = f32((fields * SUBS, LANES))
    message = [f32((width, LANES)), f32((width, LANES)), f32(((2 * fields + 1) * SUBS, LANES)), low_shape]
    busy = pl.CostEstimate(flops=1 << 25, bytes_accessed=1 << 23, transcendentals=0)

    m, *edges = pl.pallas_call(
        functools.partial(first_kernel, steps - 1, slots, fields, levels),
        out_shape=[whole, *message],
        in_specs=[smem] + [vmem] * 3,
        compiler_params=params(),
        name="first",
    )(odd, got, mask, east_rims)
    before = None
    for step in reversed(range(steps)):
        slab1, slab2, columns, low = edges
        halos = [
            lax.ppermute(slab1, "lat", swaps("lat", 0, False)),
            lax.ppermute(slab2, "lat", swaps("lat", 1, False)),
            lax.ppermute(columns, "lon", swaps("lon", 1, True)),
            lax.ppermute(columns, "lon", swaps("lon", 0, True)),
            lax.ppermute(low, "comp", [(0, 1)]),
        ]
        last = step == 0
        forcing = []
        if not last:
            forcing.append(
                pl.pallas_call(
                    functools.partial(forcing_kernel, step - 1, slots, width),
                    out_shape=whole,
                    compiler_params=params(),
                    cost_estimate=busy,
                    name="forcing",
                )(got)
            )
        step_tables = tables[4 * step : 4 * step + 4]
        if before is None:
            p, p_half = pl.pallas_call(
                functools.partial(start_kernel, step, fields, levels),
                out_shape=[whole, half],
                in_specs=[smem] * 2 + [vmem] * 6,
                compiler_params=params(),
                cost_estimate=busy,
                name="start",
            )(mixing[0], odd, m, *step_tables, *forcing)
        else:
            operands = [mixing[0], odd, *step_tables, *before, *forcing]
            m, p, *rest = pl.pallas_call(
                functools.partial(inner_kernel, last, step, fields, levels),
                out_shape=[whole, whole] + [half] * (not last),
                in_specs=[smem] * 2 + [vmem] * (len(operands) - 2),
                compiler_params=params(),
                cost_estimate=busy,
                name="inner",
            )(*operands)
            if not last:
                (p_half,) = rest
        if last:
            break
        operands = [
            air_sea,
            odd,
            p,
            p_half,
            m,
            step_tables[2],
            columns,
            east_rims,
            up_rims,
            north_rims,
            sea_float,
            mask,
            mask_columns,
            *halos,
        ]
        *edges, halves, coupled = pl.pallas_call(
            functools.partial(edge_kernel, step, fields, levels),
            out_shape=[*message, half, low_shape],
            in_specs=[smem] * 2 + [vmem] * (len(operands) - 2),
            compiler_params=params(),
            name="edge",
        )(*operands)
        before = [p, m, step_tables[2], halos[0], halos[1], halves, coupled, north_rims, mask]
    operands = [air_sea, odd, p, m, tables[2], columns, up_rims, north_rims, sea_float, *halos]
    m = pl.pallas_call(
        functools.partial(last_kernel, fields, levels),
        out_shape=whole,
        in_specs=[smem] * 2 + [vmem] * (len(operands) - 2),
        out_specs=anywhere,
        scratch_shapes=[
            pltpu.VMEM((width * SUBS, LANES), jnp.float32),
            pltpu.SemaphoreType.DMA((width // (BATCH * SUBS),)),
        ],
        compiler_params=params(),
        name="last",
    )(*operands)
    return m.reshape(1, fields, levels, lat_rows, lon_cols)


def solution(mesh):
    return jax.shard_map(
        shards,
        mesh=mesh,
        in_specs=(
            P("comp", None, ("lat", "lon"), None),
            P("comp", None, ("lat", "lon"), None),
            P("comp", None, ("lat", "lon")),
            P("comp", None, None, None, "lat", "lon"),
            P("comp", None, None, None, "lat", "lon"),
            P("comp", None, None),
            P(),
            P("lat", "lon"),
        ),
        out_specs=P("comp", None, None, "lat", "lon"),
        check_vma=False,
    )
```

```python
import functools

import jax
import jax.numpy as jnp
from jax import lax
from jax.experimental import pallas as pl
from jax.experimental.pallas import tpu as pltpu
from jax.sharding import PartitionSpec as P

LANES = 128
SUBS = 8
BATCH = 4
VMEM_LIMIT = 12 * 1024 * 1024
VMEM_WHOLE = 58 * 1024 * 1024


def split3(x):
    hi = x.astype(jnp.bfloat16)
    rest = x - hi.astype(jnp.float32)
    mid = rest.astype(jnp.bfloat16)
    low = (rest - mid.astype(jnp.float32)).astype(jnp.bfloat16)
    return [hi, mid, low]


def pack_kernel(slots, rows_hbm, owner_hbm, cell_hbm, out_ref, rows_ref, owner_ref, cell_ref, sems):
    steps, count, width = rows_ref.shape
    owners = count
    parts = width // LANES
    stride = out_ref.shape[0] // owners
    small = [
        pltpu.make_async_copy(owner_hbm, owner_ref, sems.at[steps]),
        pltpu.make_async_copy(cell_hbm, cell_ref, sems.at[steps + 1]),
    ]
    large = [
        pltpu.make_async_copy(rows_hbm.at[step], rows_ref.at[step], sems.at[step]) for step in range(steps)
    ]
    for copy in small + large:
        copy.start()
    dest = lax.broadcasted_iota(jnp.int32, (owners, count), 0)
    lane = lax.broadcasted_iota(jnp.int32, (owners, count), 1)
    before = (dest < lane).astype(jnp.bfloat16)
    cells = jnp.zeros((owners, LANES), jnp.float32)
    for copy in small:
        copy.wait()
    for step in range(steps):
        hits = owner_ref[step] == dest
        hits_f = hits.astype(jnp.float32)
        prior = jnp.dot(hits_f.astype(jnp.bfloat16), before, preferred_element_type=jnp.float32)
        large[step].wait()
        terms = jnp.concatenate(split3(rows_ref[step]), axis=0)
        marks = (cell_ref[step] + 1).astype(jnp.float32)
        for k in range(slots):
            slot = step * slots + k
            pick = jnp.where(prior == float(k), hits_f, 0.0)
            pick_b = pick.astype(jnp.bfloat16)
            out = jnp.dot(
                jnp.concatenate([pick_b] * 3, axis=1), terms, preferred_element_type=jnp.float32
            )
            for part in range(parts):
                out_ref[pl.ds(slot * parts + part, owners, stride=stride), :] = out[
                    :, part * LANES : (part + 1) * LANES
                ]
            mark = jnp.sum(pick * marks, axis=1, keepdims=True)
            cells = jnp.where(lane == slot, mark, cells)
    out_ref[pl.ds(stride - 1, owners, stride=stride), :] = cells


def spread_rows(step, slots, got_ref, width):
    parts = width // LANES
    stride = parts * slots * 3 + 1
    sources = got_ref.shape[0] // stride
    marks = got_ref[pl.ds(stride - 1, sources, stride=stride), :]
    where_to = lax.broadcasted_iota(jnp.int32, (sources, SUBS * LANES), 1)
    terms, onehots = [], []
    for k in range(slots):
        slot = step * slots + k
        cols = []
        for part in range(parts):
            block = got_ref[pl.ds(slot * parts + part, sources, stride=stride), :]
            cols.append(block.T)
        turned = jnp.concatenate(cols, axis=0)
        terms += split3(turned)
        cell = marks[:, slot : slot + 1].astype(jnp.int32) - 1
        onehot = (cell == where_to).astype(jnp.float32).astype(jnp.bfloat16)
        onehots += [onehot] * 3
    return jnp.dot(
        jnp.concatenate(terms, axis=1),
        jnp.concatenate(onehots, axis=0),
        preferred_element_type=jnp.float32,
    )


def column_halves(load, fields, groups, ys, halves):
    lane = lax.broadcasted_iota(jnp.int32, (SUBS, LANES), 1)
    for f in range(fields):
        for group in groups:
            for y in ys:
                at = group * SUBS + y
                plane = load(f, group, y)
                turned = plane if at == 0 else pltpu.roll(plane, at, 1)
                here = (lane == at) | (lane == (at - 1) % LANES)
                halves[2 * f + at % 2] = jnp.where(here, turned, halves[2 * f + at % 2])
    return halves


def columns_store(halves, rim, column_ref, fields):
    even = lax.broadcasted_iota(jnp.int32, (SUBS, LANES), 1) % 2 == 0
    for f in range(fields):
        a, b = halves[2 * f], halves[2 * f + 1]
        column_ref[f * SUBS : (f + 1) * SUBS, :] = jnp.where(even, a, b)
        column_ref[(fields + f) * SUBS : (fields + f + 1) * SUBS, :] = jnp.where(even, b, a)
    column_ref[2 * fields * SUBS :, :] = rim


def column_corrections(lon_even, first_ref, second_ref, own_ref, up_rim, fields):
    even = lax.broadcasted_iota(jnp.int32, (SUBS, LANES), 1) % 2 == 0

    def rows(i):
        one, two = first_ref[i * SUBS : (i + 1) * SUBS, :], second_ref[i * SUBS : (i + 1) * SUBS, :]
        return jnp.where(lon_even, one, two), jnp.where(lon_even, two, one)

    rim = pltpu.roll(rows(2 * fields)[0], 1, 1)
    halves = []
    for f in range(fields):
        from_west = pltpu.roll(rows(fields + f)[0], 1, 1)
        from_east = pltpu.roll(rows(f)[1], LANES - 1, 1)
        own_west = own_ref[f * SUBS : (f + 1) * SUBS, :]
        own_east = own_ref[(fields + f) * SUBS : (fields + f + 1) * SUBS, :]
        west = rim * (own_west - from_west)
        east = up_rim * (from_east - own_east)
        halves += [jnp.where(even, west, east), jnp.where(even, east, west)]
    return halves


def turn_to_first(col, at):
    return col if at == 0 else pltpu.roll(col, LANES - at, 1)


def rows_of(base, group):
    if isinstance(group, int):
        return pl.ds(base + group * SUBS, SUBS)
    return pl.ds(pl.multiple_of(base + group * SUBS, SUBS), SUBS)


def slabs_store(lat_even, m_ref, first_ref, second_ref, width):
    for i in range(width // SUBS):
        rows = slice(i * SUBS, (i + 1) * SUBS)
        south = m_ref[rows, :]
        north = m_ref[(SUBS - 1) * width + i * SUBS : (SUBS - 1) * width + (i + 1) * SUBS, :]
        first_ref[rows, :] = jnp.where(lat_even, north, south)
        second_ref[rows, :] = jnp.where(lat_even, south, north)


def parity(ref, i):
    return jnp.full((SUBS, LANES), ref[i], jnp.int32) == 0


def low_store(m_ref, low_ref, fields, levels):
    for f in range(fields):
        low_ref[f * SUBS : (f + 1) * SUBS, :] = m_ref[
            pl.ds(f * levels + levels - 1, SUBS, stride=fields * levels), :
        ]


def first_kernel(
    step, slots, fields, levels, odd_ref, got_ref, mask_ref, rim_ref, _, m_ref, slab1_ref, slab2_ref, column_ref, low_ref
):
    width = fields * levels
    out = spread_rows(step, slots, got_ref, width)
    for y in range(SUBS):
        m_ref[y * width : (y + 1) * width, :] = out[:, y * LANES : (y + 1) * LANES] * mask_ref[y : y + 1, :]
    slabs_store(parity(odd_ref, 0), m_ref, slab1_ref, slab2_ref, width)
    halves = column_halves(
        lambda f, group, y: m_ref[rows_of((y * fields + f) * levels, group), :],
        fields,
        range(levels // SUBS),
        range(SUBS),
        [jnp.zeros((SUBS, LANES), jnp.float32)] * (2 * fields),
    )
    columns_store(halves, rim_ref[step * SUBS : (step + 1) * SUBS, :], column_ref, fields)
    low_store(m_ref, low_ref, fields, levels)


def forcing_kernel(step, slots, width, got_ref, f_ref):
    out = spread_rows(step, slots, got_ref, width)
    for y in range(SUBS):
        f_ref[y * width : (y + 1) * width, :] = out[:, y * LANES : (y + 1) * LANES]


def rim_kernel(vel_ref, dif_ref, rim_ref, vel_row, dif_row, sems):
    copies = [
        pltpu.make_async_copy(src.at[:, 1, :, SUBS - 1, :], dst, sems.at[i])
        for i, (src, dst) in enumerate(((vel_ref, vel_row), (dif_ref, dif_row)))
    ]
    for copy in copies:
        copy.start()
    for copy in copies:
        copy.wait()
    steps, levels, lanes = vel_row.shape
    rim_ref[...] = (jnp.minimum(vel_row[...], 0.0) - dif_row[...]).reshape(steps * levels, lanes)


def coefficient_kernel(steps, levels, vel_ref, dif_ref, open_ref, mask_ref, *outs):
    tables, (rim_ref, up_rim_ref, mask_column_ref) = outs[:-3], outs[-3:]
    lane = lax.broadcasted_iota(jnp.int32, (SUBS, LANES), 1)
    tall = lax.broadcasted_iota(jnp.int32, (levels, LANES), 1)
    for step in range(steps):
        up_e_ref, down_w_ref, up_n_ref, down_n_ref = tables[4 * step : 4 * step + 4]
        east, north = 2 * step * levels * SUBS, (2 * step + 1) * levels * SUBS
        rim = jnp.zeros((SUBS, LANES), jnp.float32)
        up_rim = rim
        for y in range(SUBS):
            rows = slice(y * levels, (y + 1) * levels)
            w = vel_ref[pl.ds(east + y, levels, stride=SUBS), :]
            k = dif_ref[pl.ds(east + y, levels, stride=SUBS), :]
            up = jnp.maximum(w, 0.0) + k
            down = jnp.minimum(w, 0.0) - k
            for group in range(levels // SUBS):
                at = group * SUBS + y
                part = slice(group * SUBS, (group + 1) * SUBS)
                rim = jnp.where(lane == (at - 1) % LANES, pltpu.roll(down[part, :], at, 1) if at else down[part, :], rim)
                up_rim = jnp.where(lane == (at - 1) % LANES, pltpu.roll(up[part, :], at, 1) if at else up[part, :], up_rim)
            up_e_ref[rows, :] = jnp.where(tall == LANES - 1, 0.0, up)
            down_w_ref[rows, :] = jnp.where(tall == 0, 0.0, pltpu.roll(down, 1, 1))
            w = vel_ref[pl.ds(north + y, levels, stride=SUBS), :]
            k = dif_ref[pl.ds(north + y, levels, stride=SUBS), :]
            up = jnp.maximum(w, 0.0) + k
            up_n_ref[rows, :] = up * open_ref[...] if y == SUBS - 1 else up
            down_n_ref[rows, :] = jnp.minimum(w, 0.0) - k
        rim_ref[step * SUBS : (step + 1) * SUBS, :] = rim
        up_rim_ref[step * SUBS : (step + 1) * SUBS, :] = up_rim
    west, east = jnp.zeros((SUBS, LANES), jnp.float32), jnp.zeros((SUBS, LANES), jnp.float32)
    for group in range(levels // SUBS):
        for y in range(SUBS):
            at = group * SUBS + y
            row = jnp.broadcast_to(mask_ref[y : y + 1, :], (SUBS, LANES))
            turned = pltpu.roll(row, at, 1) if at else row
            west = jnp.where(lane == at, turned, west)
            east = jnp.where(lane == (at - 1) % LANES, turned, east)
    mask_column_ref[:SUBS, :] = west
    mask_column_ref[SUBS:, :] = east


def settled(f, group, y, at, p_ref, m_ref, halves, edge, coupled, up_n_ref, rim_row, from_south, from_north, fields, levels):
    rows = rows_of((y * fields + f) * levels, group)
    result = p_ref[rows, :] + jnp.where(edge, turn_to_first(halves[2 * f + at % 2], at), 0.0)
    if y == 0:
        result = result + rim_row(group) * (m_ref[rows, :] - from_south(f, group))
    if y == SUBS - 1:
        up = up_n_ref[rows_of(y * levels, group), :]
        result = result + up * (from_north(f, group) - m_ref[rows, :])
    if isinstance(group, int) and group == 0:
        sub = lax.broadcasted_iota(jnp.int32, (SUBS, LANES), 0)
        result = result + jnp.where(sub == 0, coupled(f, y), 0.0)
    return result


def slab_readers(lat_even, slab1_ref, slab2_ref, levels):
    def south(f, group):
        rows = rows_of(f * levels, group)
        return jnp.where(lat_even, slab2_ref[rows, :], slab1_ref[rows, :])

    def north(f, group):
        rows = rows_of(f * levels, group)
        return jnp.where(lat_even, slab1_ref[rows, :], slab2_ref[rows, :])

    return south, north


def coupling(air_ref, sea_ref, from_low_ref, fields):
    sea = sea_ref[...]
    planes = []
    for g in range(fields):
        total = jnp.zeros((SUBS, LANES), jnp.float32)
        for f in range(fields):
            total = total + air_ref[f, g] * from_low_ref[f * SUBS : (f + 1) * SUBS, :]
        planes.append(sea * total)
    return planes


def partial_kernel(settle, step, fields, levels, mix_ref, odd_ref, m_ref, tables, forcing_ref, before, outs):
    up_e_ref, down_w_ref, up_n_ref, down_n_ref = tables
    width = fields * levels
    lane = lax.broadcasted_iota(jnp.int32, (SUBS, LANES), 1)
    edge = (lane == 0) | (lane == LANES - 1)
    batches = levels // (SUBS * BATCH)
    if settle:
        old_p_ref, old_m_ref, old_up_n_ref, slab1_ref, slab2_ref, half_ref, couple_ref, rim_ref, mask_ref = before
        south, north = slab_readers(parity(odd_ref, 0), slab1_ref, slab2_ref, levels)

        def settle_batch(group0, halves):
            for u in range(BATCH):
                group = group0 + u
                for y in range(SUBS):
                    for f in range(fields):
                        plane = settled(
                            f,
                            group,
                            y,
                            u * SUBS + y,
                            old_p_ref,
                            old_m_ref,
                            halves,
                            edge,
                            lambda f, y: couple_ref[f * SUBS + y : f * SUBS + y + 1, :],
                            old_up_n_ref,
                            lambda group: rim_ref[rows_of((step + 1) * levels, group), :],
                            south,
                            north,
                            fields,
                            levels,
                        )
                        m_ref[rows_of((y * fields + f) * levels, group), :] = plane * mask_ref[y : y + 1, :]
            return tuple(pltpu.roll(h, LANES - BATCH * SUBS, 1) for h in halves)

        halves = settle_batch(0, [half_ref[i * SUBS : (i + 1) * SUBS, :] for i in range(2 * fields)])
        lax.fori_loop(1, batches, lambda i, halves: settle_batch(i * BATCH, halves), halves)
    p_ref = outs[0]
    mix = [[mix_ref[f, g] for g in range(fields)] for f in range(fields)]

    def body(i, carry):
        for u in range(BATCH):
            group = i * BATCH + u
            for y in range(SUBS):
                up_e = up_e_ref[rows_of(y * levels, group), :]
                down_w = down_w_ref[rows_of(y * levels, group), :]
                planes = [m_ref[rows_of(y * width + f * levels, group), :] for f in range(fields)]
                for g in range(fields):
                    m = planes[g]
                    rows = rows_of(y * width + g * levels, group)
                    result = m if forcing_ref is None else m + forcing_ref[rows, :]
                    for f in range(fields):
                        result = result + mix[f][g] * planes[f]
                    result = result + up_e * (pltpu.roll(m, LANES - 1, 1) - m)
                    result = result + down_w * (m - pltpu.roll(m, 1, 1))
                    if y < SUBS - 1:
                        up_n = up_n_ref[rows_of(y * levels, group), :]
                        result = result + up_n * (m_ref[rows_of((y + 1) * width + g * levels, group), :] - m)
                    if y > 0:
                        down_s = down_n_ref[rows_of((y - 1) * levels, group), :]
                        result = result + down_s * (m - m_ref[rows_of((y - 1) * width + g * levels, group), :])
                    p_ref[rows, :] = result
        return carry

    lax.fori_loop(0, batches, body, 0)
    if len(outs) > 1:
        halves = column_halves(
            lambda f, group, y: p_ref[rows_of((y * fields + f) * levels, group), :],
            fields,
            range(levels // SUBS),
            range(SUBS),
            [jnp.zeros((SUBS, LANES), jnp.float32)] * (2 * fields),
        )
        for i, half in enumerate(halves):
            outs[1][i * SUBS : (i + 1) * SUBS, :] = half


def start_kernel(step, fields, levels, mix_ref, odd_ref, m_ref, a_ref, b_ref, c_ref, d_ref, f_ref, *outs):
    partial_kernel(False, step, fields, levels, mix_ref, odd_ref, m_ref, (a_ref, b_ref, c_ref, d_ref), f_ref, None, outs)


def inner_kernel(last, step, fields, levels, mix_ref, odd_ref, a_ref, b_ref, c_ref, d_ref, *rest):
    tables = (a_ref, b_ref, c_ref, d_ref)
    before, rest = rest[:9], rest[9:]
    f_ref = None
    if not last:
        f_ref, rest = rest[0], rest[1:]
    partial_kernel(True, step, fields, levels, mix_ref, odd_ref, rest[0], tables, f_ref, before, rest[1:])


def edge_kernel(
    step,
    fields,
    levels,
    air_ref,
    odd_ref,
    p_ref,
    p_half_ref,
    m_ref,
    up_n_ref,
    own_column_ref,
    rim_ref,
    up_rim_ref,
    north_rim_ref,
    sea_ref,
    mask_ref,
    mask_column_ref,
    from_slab1_ref,
    from_slab2_ref,
    from_column1_ref,
    from_column2_ref,
    from_low_ref,
    slab1_ref,
    slab2_ref,
    column_ref,
    low_ref,
    half_ref,
    couple_ref,
    next_ref,
):
    lane = lax.broadcasted_iota(jnp.int32, (SUBS, LANES), 1)
    edge = (lane == 0) | (lane == LANES - 1)
    even = lane % 2 == 0
    lat_even, lon_even = parity(odd_ref, 0), parity(odd_ref, 1)
    south, north = slab_readers(lat_even, from_slab1_ref, from_slab2_ref, levels)
    coupled = coupling(air_ref, sea_ref, from_low_ref, fields)
    for g in range(fields):
        couple_ref[g * SUBS : (g + 1) * SUBS, :] = coupled[g]
    halves = column_corrections(
        lon_even,
        from_column1_ref,
        from_column2_ref,
        own_column_ref,
        up_rim_ref[step * SUBS : (step + 1) * SUBS, :],
        fields,
    )
    for i, half in enumerate(halves):
        half_ref[i * SUBS : (i + 1) * SUBS, :] = half
    west, east = mask_column_ref[:SUBS, :], mask_column_ref[SUBS:, :]
    masks = [jnp.where(even, west, east), jnp.where(even, east, west)]
    following = [
        (p_half_ref[i * SUBS : (i + 1) * SUBS, :] + half) * masks[i % 2] for i, half in enumerate(halves)
    ]
    groups = levels // SUBS

    def plane(f, group, y):
        full = settled(
            f,
            group,
            y,
            group * SUBS + y,
            p_ref,
            m_ref,
            halves,
            edge,
            lambda f, y: coupled[f][y : y + 1, :],
            up_n_ref,
            lambda group: north_rim_ref[rows_of(step * levels, group), :],
            south,
            north,
            fields,
            levels,
        )
        return full * mask_ref[y : y + 1, :]

    for f in range(fields):
        for group in range(groups):
            for y in range(SUBS) if group in (0, groups - 1) else (0, SUBS - 1):
                next_ref[rows_of((y * fields + f) * levels, group), :] = plane(f, group, y)
    slabs_store(lat_even, next_ref, slab1_ref, slab2_ref, fields * levels)
    low_store(next_ref, low_ref, fields, levels)

    def load(f, group, y):
        return next_ref[rows_of((y * fields + f) * levels, group), :]

    following = column_halves(load, fields, range(groups), (0, SUBS - 1), following)
    following = column_halves(load, fields, (0,), range(1, SUBS - 1), following)
    columns_store(following, rim_ref[(step - 1) * SUBS : step * SUBS, :], column_ref, fields)


def last_kernel(
    fields,
    levels,
    air_ref,
    odd_ref,
    p_ref,
    m_ref,
    up_n_ref,
    own_column_ref,
    up_rim_ref,
    north_rim_ref,
    sea_ref,
    from_slab1_ref,
    from_slab2_ref,
    from_column1_ref,
    from_column2_ref,
    from_low_ref,
    sent_ref,
    out_ref,
    sems,
):
    lane = lax.broadcasted_iota(jnp.int32, (SUBS, LANES), 1)
    edge = (lane == 0) | (lane == LANES - 1)
    south, north = slab_readers(parity(odd_ref, 0), from_slab1_ref, from_slab2_ref, levels)
    coupled = coupling(air_ref, sea_ref, from_low_ref, fields)
    halves = column_corrections(
        parity(odd_ref, 1), from_column1_ref, from_column2_ref, own_column_ref, up_rim_ref[:SUBS, :], fields
    )
    batches = levels // (SUBS * BATCH)

    def pieces(i):
        for f in range(fields):
            rows = pl.ds((f * levels + i * BATCH * SUBS) * SUBS, BATCH * SUBS * SUBS)
            yield pltpu.make_async_copy(out_ref.at[rows], sent_ref.at[rows], sems.at[f * batches + i])

    def batch(i, halves):
        for u in range(BATCH):
            group = i * BATCH + u
            for y in range(SUBS):
                for f in range(fields):
                    out_ref[pl.ds(f * levels * SUBS + y + group * (SUBS * SUBS), SUBS, stride=SUBS), :] = settled(
                        f,
                        group,
                        y,
                        u * SUBS + y,
                        p_ref,
                        m_ref,
                        halves,
                        edge,
                        lambda f, y: coupled[f][y : y + 1, :],
                        up_n_ref,
                        lambda group: north_rim_ref[rows_of(0, group), :],
                        south,
                        north,
                        fields,
                        levels,
                    )
        for copy in pieces(i):
            copy.start()
        return tuple(pltpu.roll(h, LANES - BATCH * SUBS, 1) for h in halves)

    lax.fori_loop(1, batches, batch, batch(0, halves))
    for i in range(batches):
        for copy in pieces(i):
            copy.wait()


def params(limit=VMEM_LIMIT):
    return pltpu.CompilerParams(vmem_limit_bytes=limit)


def swaps(axis, start, closed):
    count = lax.axis_size(axis)
    pairs = []
    for i in range(start, count if closed else count - 1, 2):
        j = (i + 1) % count
        pairs += [(i, j), (j, i)]
    return pairs


def shards(innovations, obs_owner, obs_cell, velocity, diffusion, mixing, air_sea, sea_mask):
    lat_count = lax.axis_size("lat")
    lon_count = lax.axis_size("lon")
    owners = lat_count * lon_count
    steps, levels, lat_rows, lon_cols = (velocity.shape[i] for i in (1, 3, 4, 5))
    fields = mixing.shape[1]
    width = fields * levels
    count = innovations.shape[2]
    slots = 2
    assert (lat_rows, lon_cols, levels, count, owners, steps) == (SUBS, LANES, LANES, LANES, LANES, 3)
    f32 = functools.partial(jax.ShapeDtypeStruct, dtype=jnp.float32)
    stride = steps * slots * width // LANES + 1

    is_ocean = lax.axis_index("comp") == 1
    sea_float = sea_mask.astype(jnp.float32)
    mask = jnp.where(is_ocean, sea_float, jnp.ones_like(sea_float))
    opened = jnp.full((1, lon_cols), lax.axis_index("lat") < lat_count - 1, jnp.float32)
    smem = pl.BlockSpec(memory_space=pltpu.SMEM)
    vmem = pl.BlockSpec(memory_space=pltpu.VMEM)
    anywhere = pl.BlockSpec(memory_space=pltpu.HBM)
    speeds, diffuse = velocity[0], diffusion[0]

    north_rims = pl.pallas_call(
        rim_kernel,
        out_shape=f32((steps * levels, LANES)),
        in_specs=[anywhere] * 2,
        scratch_shapes=[pltpu.VMEM((steps, levels, LANES), jnp.float32)] * 2 + [pltpu.SemaphoreType.DMA((2,))],
        compiler_params=params(VMEM_WHOLE),
        name="rim",
    )(speeds, diffuse)
    north_rims = lax.ppermute(
        north_rims, "lat", [(i, i + 1) for i in range(lat_count - 1)]
    )

    sent = pl.pallas_call(
        functools.partial(pack_kernel, slots),
        out_shape=f32((owners * stride, LANES)),
        in_specs=[anywhere] * 3,
        scratch_shapes=[
            pltpu.VMEM((steps, count, width), jnp.float32),
            pltpu.VMEM((steps, 1, count), jnp.int32),
            pltpu.VMEM((steps, 1, count), jnp.int32),
            pltpu.SemaphoreType.DMA((steps + 2,)),
        ],
        compiler_params=params(VMEM_WHOLE),
        name="pack",
    )(
        innovations[0],
        obs_owner.reshape(steps, 1, count),
        obs_cell.reshape(steps, 1, count),
    )
    got = lax.all_to_all(
        sent.reshape(owners, 1, stride * LANES), ("lat", "lon"), split_axis=0, concat_axis=0, tiled=True
    ).reshape(owners * stride, LANES)

    table = f32((levels * SUBS, LANES))
    *tables, east_rims, up_rims, mask_columns = pl.pallas_call(
        functools.partial(coefficient_kernel, steps, levels),
        out_shape=[table] * (4 * steps) + [f32((steps * SUBS, LANES))] * 2 + [f32((2 * SUBS, LANES))],
        compiler_params=params(),
        cost_estimate=pl.CostEstimate(flops=1 << 22, bytes_accessed=1 << 23, transcendentals=0),
        name="coefficients",
    )(
        speeds.reshape(steps * 2 * levels * SUBS, LANES),
        diffuse.reshape(steps * 2 * levels * SUBS, LANES),
        opened,
        mask,
    )
    odd = jnp.stack([lax.axis_index("lat") % 2, lax.axis_index("lon") % 2]).astype(jnp.int32)
    whole = f32((width * SUBS, LANES))
    half = f32((2 * fields * SUBS, LANES))
    low_shape = f32((fields * SUBS, LANES))
    message = [f32((width, LANES)), f32((width, LANES)), f32(((2 * fields + 1) * SUBS, LANES)), low_shape]
    busy = pl.CostEstimate(flops=1 << 25, bytes_accessed=1 << 23, transcendentals=0)

    m, *edges = pl.pallas_call(
        functools.partial(first_kernel, steps - 1, slots, fields, levels),
        out_shape=[whole, *message],
        in_specs=[smem] + [vmem] * 3 + [anywhere],
        compiler_params=params(),
        name="first",
    )(odd, got, mask, east_rims, north_rims)
    before = None
    for step in reversed(range(steps)):
        slab1, slab2, columns, low = edges
        halos = [
            lax.ppermute(slab1, "lat", swaps("lat", 0, False)),
            lax.ppermute(slab2, "lat", swaps("lat", 1, False)),
            lax.ppermute(columns, "lon", swaps("lon", 1, True)),
            lax.ppermute(columns, "lon", swaps("lon", 0, True)),
            lax.ppermute(low, "comp", [(0, 1)]),
        ]
        last = step == 0
        forcing = []
        if not last:
            forcing.append(
                pl.pallas_call(
                    functools.partial(forcing_kernel, step - 1, slots, width),
                    out_shape=whole,
                    compiler_params=params(),
                    cost_estimate=busy,
                    name="forcing",
                )(got)
            )
        step_tables = tables[4 * step : 4 * step + 4]
        if before is None:
            p, p_half = pl.pallas_call(
                functools.partial(start_kernel, step, fields, levels),
                out_shape=[whole, half],
                in_specs=[smem] * 2 + [vmem] * 6,
                compiler_params=params(),
                cost_estimate=busy,
                name="start",
            )(mixing[0], odd, m, *step_tables, *forcing)
        else:
            operands = [mixing[0], odd, *step_tables, *before, *forcing]
            m, p, *rest = pl.pallas_call(
                functools.partial(inner_kernel, last, step, fields, levels),
                out_shape=[whole, whole] + [half] * (not last),
                in_specs=[smem] * 2 + [vmem] * (len(operands) - 2),
                compiler_params=params(),
                cost_estimate=busy,
                name="inner",
            )(*operands)
            if not last:
                (p_half,) = rest
        if last:
            break
        operands = [
            air_sea,
            odd,
            p,
            p_half,
            m,
            step_tables[2],
            columns,
            east_rims,
            up_rims,
            north_rims,
            sea_float,
            mask,
            mask_columns,
            *halos,
        ]
        *edges, halves, coupled = pl.pallas_call(
            functools.partial(edge_kernel, step, fields, levels),
            out_shape=[*message, half, low_shape],
            in_specs=[smem] * 2 + [vmem] * (len(operands) - 2),
            scratch_shapes=[pltpu.VMEM((width * SUBS, LANES), jnp.float32)],
            compiler_params=params(),
            name="edge",
        )(*operands)
        before = [p, m, step_tables[2], halos[0], halos[1], halves, coupled, north_rims, mask]
    operands = [air_sea, odd, p, m, tables[2], columns, up_rims, north_rims, sea_float, *halos]
    m = pl.pallas_call(
        functools.partial(last_kernel, fields, levels),
        out_shape=whole,
        in_specs=[smem] * 2 + [vmem] * (len(operands) - 2),
        out_specs=anywhere,
        scratch_shapes=[
            pltpu.VMEM((width * SUBS, LANES), jnp.float32),
            pltpu.SemaphoreType.DMA((width // (BATCH * SUBS),)),
        ],
        compiler_params=params(),
        name="last",
    )(*operands)
    return m.reshape(1, fields, levels, lat_rows, lon_cols)


def solution(mesh):
    return jax.shard_map(
        shards,
        mesh=mesh,
        in_specs=(
            P("comp", None, ("lat", "lon"), None),
            P("comp", None, ("lat", "lon"), None),
            P("comp", None, ("lat", "lon")),
            P("comp", None, None, None, "lat", "lon"),
            P("comp", None, None, None, "lat", "lon"),
            P("comp", None, None),
            P(),
            P("lat", "lon"),
        ),
        out_specs=P("comp", None, None, "lat", "lon"),
        check_vma=False,
    )
```

```python
import functools

import jax
import jax.numpy as jnp
from jax import lax
from jax.experimental import pallas as pl
from jax.experimental.pallas import tpu as pltpu
from jax.sharding import PartitionSpec as P

LANES = 128
SUBS = 8
BATCH = 4
VMEM_LIMIT = 12 * 1024 * 1024
VMEM_WHOLE = 58 * 1024 * 1024


def split(x):
    high = x.astype(jnp.bfloat16)
    return [high, (x - high.astype(jnp.float32)).astype(jnp.bfloat16)]


def pack_kernel(slots, rows_hbm, owner_hbm, cell_hbm, out_ref, rows_ref, owner_ref, cell_ref, sems):
    steps, count, width = rows_ref.shape
    owners = count
    parts = width // LANES
    stride = out_ref.shape[0] // owners
    small = [
        pltpu.make_async_copy(owner_hbm, owner_ref, sems.at[steps]),
        pltpu.make_async_copy(cell_hbm, cell_ref, sems.at[steps + 1]),
    ]
    large = [
        pltpu.make_async_copy(rows_hbm.at[step], rows_ref.at[step], sems.at[step]) for step in range(steps)
    ]
    for copy in small + large:
        copy.start()
    dest = lax.broadcasted_iota(jnp.int32, (owners, count), 0)
    lane = lax.broadcasted_iota(jnp.int32, (owners, count), 1)
    before = (dest < lane).astype(jnp.bfloat16)
    cells = jnp.zeros((owners, LANES), jnp.float32)
    for copy in small:
        copy.wait()
    for step in range(steps):
        hits = owner_ref[step] == dest
        hits_f = hits.astype(jnp.float32)
        prior = jnp.dot(hits_f.astype(jnp.bfloat16), before, preferred_element_type=jnp.float32)
        large[step].wait()
        terms = jnp.concatenate(split(rows_ref[step]), axis=0)
        marks = (cell_ref[step] + 1).astype(jnp.float32)
        for k in range(slots):
            slot = step * slots + k
            pick = jnp.where(prior == float(k), hits_f, 0.0)
            pick_b = pick.astype(jnp.bfloat16)
            out = jnp.dot(
                jnp.concatenate([pick_b] * 2, axis=1), terms, preferred_element_type=jnp.float32
            )
            for part in range(parts):
                out_ref[pl.ds(slot * parts + part, owners, stride=stride), :] = out[
                    :, part * LANES : (part + 1) * LANES
                ]
            mark = jnp.sum(pick * marks, axis=1, keepdims=True)
            cells = jnp.where(lane == slot, mark, cells)
    out_ref[pl.ds(stride - 1, owners, stride=stride), :] = cells


def spread_rows(step, slots, got_ref, width):
    parts = width // LANES
    stride = parts * slots * 3 + 1
    sources = got_ref.shape[0] // stride
    marks = got_ref[pl.ds(stride - 1, sources, stride=stride), :]
    where_to = lax.broadcasted_iota(jnp.int32, (sources, SUBS * LANES), 1)
    terms, onehots = [], []
    for k in range(slots):
        slot = step * slots + k
        cols = []
        for part in range(parts):
            block = got_ref[pl.ds(slot * parts + part, sources, stride=stride), :]
            cols.append(block.T)
        turned = jnp.concatenate(cols, axis=0)
        terms += split(turned)
        cell = marks[:, slot : slot + 1].astype(jnp.int32) - 1
        onehot = (cell == where_to).astype(jnp.float32).astype(jnp.bfloat16)
        onehots += [onehot] * 2
    return jnp.dot(
        jnp.concatenate(terms, axis=1),
        jnp.concatenate(onehots, axis=0),
        preferred_element_type=jnp.float32,
    )


def column_halves(load, fields, groups, ys, halves):
    lane = lax.broadcasted_iota(jnp.int32, (SUBS, LANES), 1)
    for f in range(fields):
        for group in groups:
            for y in ys:
                at = group * SUBS + y
                plane = load(f, group, y)
                turned = plane if at == 0 else pltpu.roll(plane, at, 1)
                here = (lane == at) | (lane == (at - 1) % LANES)
                halves[2 * f + at % 2] = jnp.where(here, turned, halves[2 * f + at % 2])
    return halves


def columns_store(halves, rim, column_ref, fields):
    even = lax.broadcasted_iota(jnp.int32, (SUBS, LANES), 1) % 2 == 0
    for f in range(fields):
        a, b = halves[2 * f], halves[2 * f + 1]
        column_ref[f * SUBS : (f + 1) * SUBS, :] = jnp.where(even, a, b)
        column_ref[(fields + f) * SUBS : (fields + f + 1) * SUBS, :] = jnp.where(even, b, a)
    column_ref[2 * fields * SUBS :, :] = rim


def column_corrections(lon_even, first_ref, second_ref, own_ref, up_rim, fields):
    even = lax.broadcasted_iota(jnp.int32, (SUBS, LANES), 1) % 2 == 0

    def rows(i):
        one, two = first_ref[i * SUBS : (i + 1) * SUBS, :], second_ref[i * SUBS : (i + 1) * SUBS, :]
        return jnp.where(lon_even, one, two), jnp.where(lon_even, two, one)

    rim = pltpu.roll(rows(2 * fields)[0], 1, 1)
    halves = []
    for f in range(fields):
        from_west = pltpu.roll(rows(fields + f)[0], 1, 1)
        from_east = pltpu.roll(rows(f)[1], LANES - 1, 1)
        own_west = own_ref[f * SUBS : (f + 1) * SUBS, :]
        own_east = own_ref[(fields + f) * SUBS : (fields + f + 1) * SUBS, :]
        west = rim * (own_west - from_west)
        east = up_rim * (from_east - own_east)
        halves += [jnp.where(even, west, east), jnp.where(even, east, west)]
    return halves


def turn_to_first(col, at):
    return col if at == 0 else pltpu.roll(col, LANES - at, 1)


def rows_of(base, group):
    if isinstance(group, int):
        return pl.ds(base + group * SUBS, SUBS)
    return pl.ds(pl.multiple_of(base + group * SUBS, SUBS), SUBS)


def slabs_store(lat_even, m_ref, first_ref, second_ref, width):
    for i in range(width // SUBS):
        rows = slice(i * SUBS, (i + 1) * SUBS)
        south = m_ref[rows, :]
        north = m_ref[(SUBS - 1) * width + i * SUBS : (SUBS - 1) * width + (i + 1) * SUBS, :]
        first_ref[rows, :] = jnp.where(lat_even, north, south)
        second_ref[rows, :] = jnp.where(lat_even, south, north)


def parity(ref, i):
    return jnp.full((SUBS, LANES), ref[i], jnp.int32) == 0


def low_store(m_ref, low_ref, fields, levels):
    for f in range(fields):
        low_ref[f * SUBS : (f + 1) * SUBS, :] = m_ref[
            pl.ds(f * levels + levels - 1, SUBS, stride=fields * levels), :
        ]


def first_kernel(
    step, slots, fields, levels, odd_ref, got_ref, mask_ref, rim_ref, m_ref, slab1_ref, slab2_ref, column_ref, low_ref
):
    width = fields * levels
    out = spread_rows(step, slots, got_ref, width)
    for y in range(SUBS):
        m_ref[y * width : (y + 1) * width, :] = out[:, y * LANES : (y + 1) * LANES] * mask_ref[y : y + 1, :]
    slabs_store(parity(odd_ref, 0), m_ref, slab1_ref, slab2_ref, width)
    halves = column_halves(
        lambda f, group, y: m_ref[rows_of((y * fields + f) * levels, group), :],
        fields,
        range(levels // SUBS),
        range(SUBS),
        [jnp.zeros((SUBS, LANES), jnp.float32)] * (2 * fields),
    )
    columns_store(halves, rim_ref[step * SUBS : (step + 1) * SUBS, :], column_ref, fields)
    low_store(m_ref, low_ref, fields, levels)


def forcing_kernel(step, slots, width, got_ref, f_ref):
    out = spread_rows(step, slots, got_ref, width)
    for y in range(SUBS):
        f_ref[y * width : (y + 1) * width, :] = out[:, y * LANES : (y + 1) * LANES]


def copy_kernel(from_ref, to_ref):
    to_ref[...] = from_ref[...]


def rim_kernel(vel_ref, dif_ref, rim_ref, vel_row, dif_row, sems):
    copies = [
        pltpu.make_async_copy(src.at[:, 1, :, SUBS - 1, :], dst, sems.at[i])
        for i, (src, dst) in enumerate(((vel_ref, vel_row), (dif_ref, dif_row)))
    ]
    for copy in copies:
        copy.start()
    for copy in copies:
        copy.wait()
    steps, levels, lanes = vel_row.shape
    rim_ref[...] = (jnp.minimum(vel_row[...], 0.0) - dif_row[...]).reshape(steps * levels, lanes)


def coefficient_kernel(steps, levels, vel_ref, dif_ref, open_ref, mask_ref, *outs):
    tables, (rim_ref, up_rim_ref, mask_column_ref) = outs[:-3], outs[-3:]
    lane = lax.broadcasted_iota(jnp.int32, (SUBS, LANES), 1)
    tall = lax.broadcasted_iota(jnp.int32, (levels, LANES), 1)
    for step in range(steps):
        up_e_ref, down_w_ref, up_n_ref, down_n_ref = tables[4 * step : 4 * step + 4]
        east, north = 2 * step * levels * SUBS, (2 * step + 1) * levels * SUBS
        rim = jnp.zeros((SUBS, LANES), jnp.float32)
        up_rim = rim
        for y in range(SUBS):
            rows = slice(y * levels, (y + 1) * levels)
            w = vel_ref[pl.ds(east + y, levels, stride=SUBS), :]
            k = dif_ref[pl.ds(east + y, levels, stride=SUBS), :]
            up = jnp.maximum(w, 0.0) + k
            down = jnp.minimum(w, 0.0) - k
            for group in range(levels // SUBS):
                at = group * SUBS + y
                part = slice(group * SUBS, (group + 1) * SUBS)
                rim = jnp.where(lane == (at - 1) % LANES, pltpu.roll(down[part, :], at, 1) if at else down[part, :], rim)
                up_rim = jnp.where(lane == (at - 1) % LANES, pltpu.roll(up[part, :], at, 1) if at else up[part, :], up_rim)
            up_e_ref[rows, :] = jnp.where(tall == LANES - 1, 0.0, up)
            down_w_ref[rows, :] = jnp.where(tall == 0, 0.0, pltpu.roll(down, 1, 1))
            w = vel_ref[pl.ds(north + y, levels, stride=SUBS), :]
            k = dif_ref[pl.ds(north + y, levels, stride=SUBS), :]
            up = jnp.maximum(w, 0.0) + k
            up_n_ref[rows, :] = up * open_ref[...] if y == SUBS - 1 else up
            down_n_ref[rows, :] = jnp.minimum(w, 0.0) - k
        rim_ref[step * SUBS : (step + 1) * SUBS, :] = rim
        up_rim_ref[step * SUBS : (step + 1) * SUBS, :] = up_rim
    west, east = jnp.zeros((SUBS, LANES), jnp.float32), jnp.zeros((SUBS, LANES), jnp.float32)
    for group in range(levels // SUBS):
        for y in range(SUBS):
            at = group * SUBS + y
            row = jnp.broadcast_to(mask_ref[y : y + 1, :], (SUBS, LANES))
            turned = pltpu.roll(row, at, 1) if at else row
            west = jnp.where(lane == at, turned, west)
            east = jnp.where(lane == (at - 1) % LANES, turned, east)
    mask_column_ref[:SUBS, :] = west
    mask_column_ref[SUBS:, :] = east


def settled(f, group, y, at, p_ref, m_ref, halves, edge, coupled, up_n_ref, rim_row, from_south, from_north, fields, levels):
    rows = rows_of((y * fields + f) * levels, group)
    result = p_ref[rows, :] + jnp.where(edge, turn_to_first(halves[2 * f + at % 2], at), 0.0)
    if y == 0:
        result = result + rim_row(group) * (m_ref[rows, :] - from_south(f, group))
    if y == SUBS - 1:
        up = up_n_ref[rows_of(y * levels, group), :]
        result = result + up * (from_north(f, group) - m_ref[rows, :])
    if isinstance(group, int) and group == 0:
        sub = lax.broadcasted_iota(jnp.int32, (SUBS, LANES), 0)
        result = result + jnp.where(sub == 0, coupled(f, y), 0.0)
    return result


def slab_readers(lat_even, slab1_ref, slab2_ref, levels):
    def south(f, group):
        rows = rows_of(f * levels, group)
        return jnp.where(lat_even, slab2_ref[rows, :], slab1_ref[rows, :])

    def north(f, group):
        rows = rows_of(f * levels, group)
        return jnp.where(lat_even, slab1_ref[rows, :], slab2_ref[rows, :])

    return south, north


def coupling(air_ref, sea_ref, from_low_ref, fields):
    sea = sea_ref[...]
    planes = []
    for g in range(fields):
        total = jnp.zeros((SUBS, LANES), jnp.float32)
        for f in range(fields):
            total = total + air_ref[f, g] * from_low_ref[f * SUBS : (f + 1) * SUBS, :]
        planes.append(sea * total)
    return planes


def partial_kernel(settle, step, fields, levels, mix_ref, odd_ref, m_ref, tables, forcing_ref, before, outs):
    up_e_ref, down_w_ref, up_n_ref, down_n_ref = tables
    width = fields * levels
    lane = lax.broadcasted_iota(jnp.int32, (SUBS, LANES), 1)
    edge = (lane == 0) | (lane == LANES - 1)
    batches = levels // (SUBS * BATCH)
    if settle:
        old_p_ref, old_m_ref, old_up_n_ref, slab1_ref, slab2_ref, half_ref, couple_ref, rim_ref, mask_ref = before
        south, north = slab_readers(parity(odd_ref, 0), slab1_ref, slab2_ref, levels)

        def settle_batch(group0, halves):
            for u in range(BATCH):
                group = group0 + u
                for y in range(SUBS):
                    for f in range(fields):
                        plane = settled(
                            f,
                            group,
                            y,
                            u * SUBS + y,
                            old_p_ref,
                            old_m_ref,
                            halves,
                            edge,
                            lambda f, y: couple_ref[f * SUBS + y : f * SUBS + y + 1, :],
                            old_up_n_ref,
                            lambda group: rim_ref[rows_of((step + 1) * levels, group), :],
                            south,
                            north,
                            fields,
                            levels,
                        )
                        m_ref[rows_of((y * fields + f) * levels, group), :] = plane * mask_ref[y : y + 1, :]
            return tuple(pltpu.roll(h, LANES - BATCH * SUBS, 1) for h in halves)

        halves = settle_batch(0, [half_ref[i * SUBS : (i + 1) * SUBS, :] for i in range(2 * fields)])
        lax.fori_loop(1, batches, lambda i, halves: settle_batch(i * BATCH, halves), halves)
    p_ref = outs[0]
    mix = [[mix_ref[f, g] for g in range(fields)] for f in range(fields)]

    def body(i, carry):
        for u in range(BATCH):
            group = i * BATCH + u
            for y in range(SUBS):
                up_e = up_e_ref[rows_of(y * levels, group), :]
                down_w = down_w_ref[rows_of(y * levels, group), :]
                planes = [m_ref[rows_of(y * width + f * levels, group), :] for f in range(fields)]
                for g in range(fields):
                    m = planes[g]
                    rows = rows_of(y * width + g * levels, group)
                    result = m if forcing_ref is None else m + forcing_ref[rows, :]
                    for f in range(fields):
                        result = result + mix[f][g] * planes[f]
                    result = result + up_e * (pltpu.roll(m, LANES - 1, 1) - m)
                    result = result + down_w * (m - pltpu.roll(m, 1, 1))
                    if y < SUBS - 1:
                        up_n = up_n_ref[rows_of(y * levels, group), :]
                        result = result + up_n * (m_ref[rows_of((y + 1) * width + g * levels, group), :] - m)
                    if y > 0:
                        down_s = down_n_ref[rows_of((y - 1) * levels, group), :]
                        result = result + down_s * (m - m_ref[rows_of((y - 1) * width + g * levels, group), :])
                    p_ref[rows, :] = result
        return carry

    lax.fori_loop(0, batches, body, 0)
    if len(outs) > 1:
        halves = column_halves(
            lambda f, group, y: p_ref[rows_of((y * fields + f) * levels, group), :],
            fields,
            range(levels // SUBS),
            range(SUBS),
            [jnp.zeros((SUBS, LANES), jnp.float32)] * (2 * fields),
        )
        for i, half in enumerate(halves):
            outs[1][i * SUBS : (i + 1) * SUBS, :] = half


def start_kernel(step, fields, levels, mix_ref, odd_ref, m_ref, a_ref, b_ref, c_ref, d_ref, f_ref, *outs):
    partial_kernel(False, step, fields, levels, mix_ref, odd_ref, m_ref, (a_ref, b_ref, c_ref, d_ref), f_ref, None, outs)


def inner_kernel(last, step, fields, levels, mix_ref, odd_ref, a_ref, b_ref, c_ref, d_ref, *rest):
    tables = (a_ref, b_ref, c_ref, d_ref)
    before, rest = rest[:9], rest[9:]
    f_ref = None
    if not last:
        f_ref, rest = rest[0], rest[1:]
    partial_kernel(True, step, fields, levels, mix_ref, odd_ref, rest[0], tables, f_ref, before, rest[1:])


def edge_kernel(
    step,
    fields,
    levels,
    air_ref,
    odd_ref,
    p_ref,
    p_half_ref,
    m_ref,
    up_n_ref,
    own_column_ref,
    rim_ref,
    up_rim_ref,
    north_rim_ref,
    sea_ref,
    mask_ref,
    mask_column_ref,
    from_slab1_ref,
    from_slab2_ref,
    from_column1_ref,
    from_column2_ref,
    from_low_ref,
    slab1_ref,
    slab2_ref,
    column_ref,
    low_ref,
    half_ref,
    couple_ref,
    next_ref,
):
    lane = lax.broadcasted_iota(jnp.int32, (SUBS, LANES), 1)
    edge = (lane == 0) | (lane == LANES - 1)
    even = lane % 2 == 0
    lat_even, lon_even = parity(odd_ref, 0), parity(odd_ref, 1)
    south, north = slab_readers(lat_even, from_slab1_ref, from_slab2_ref, levels)
    coupled = coupling(air_ref, sea_ref, from_low_ref, fields)
    for g in range(fields):
        couple_ref[g * SUBS : (g + 1) * SUBS, :] = coupled[g]
    halves = column_corrections(
        lon_even,
        from_column1_ref,
        from_column2_ref,
        own_column_ref,
        up_rim_ref[step * SUBS : (step + 1) * SUBS, :],
        fields,
    )
    for i, half in enumerate(halves):
        half_ref[i * SUBS : (i + 1) * SUBS, :] = half
    west, east = mask_column_ref[:SUBS, :], mask_column_ref[SUBS:, :]
    masks = [jnp.where(even, west, east), jnp.where(even, east, west)]
    following = [
        (p_half_ref[i * SUBS : (i + 1) * SUBS, :] + half) * masks[i % 2] for i, half in enumerate(halves)
    ]
    groups = levels // SUBS

    def plane(f, group, y):
        full = settled(
            f,
            group,
            y,
            group * SUBS + y,
            p_ref,
            m_ref,
            halves,
            edge,
            lambda f, y: coupled[f][y : y + 1, :],
            up_n_ref,
            lambda group: north_rim_ref[rows_of(step * levels, group), :],
            south,
            north,
            fields,
            levels,
        )
        return full * mask_ref[y : y + 1, :]

    for f in range(fields):
        for group in range(groups):
            for y in range(SUBS) if group in (0, groups - 1) else (0, SUBS - 1):
                next_ref[rows_of((y * fields + f) * levels, group), :] = plane(f, group, y)
    slabs_store(lat_even, next_ref, slab1_ref, slab2_ref, fields * levels)
    low_store(next_ref, low_ref, fields, levels)

    def load(f, group, y):
        return next_ref[rows_of((y * fields + f) * levels, group), :]

    following = column_halves(load, fields, range(groups), (0, SUBS - 1), following)
    following = column_halves(load, fields, (0,), range(1, SUBS - 1), following)
    columns_store(following, rim_ref[(step - 1) * SUBS : step * SUBS, :], column_ref, fields)


def last_kernel(
    fields,
    levels,
    air_ref,
    odd_ref,
    p_ref,
    m_ref,
    up_n_ref,
    own_column_ref,
    up_rim_ref,
    north_rim_ref,
    sea_ref,
    from_slab1_ref,
    from_slab2_ref,
    from_column1_ref,
    from_column2_ref,
    from_low_ref,
    sent_ref,
    out_ref,
    sems,
):
    lane = lax.broadcasted_iota(jnp.int32, (SUBS, LANES), 1)
    edge = (lane == 0) | (lane == LANES - 1)
    south, north = slab_readers(parity(odd_ref, 0), from_slab1_ref, from_slab2_ref, levels)
    coupled = coupling(air_ref, sea_ref, from_low_ref, fields)
    halves = column_corrections(
        parity(odd_ref, 1), from_column1_ref, from_column2_ref, own_column_ref, up_rim_ref[:SUBS, :], fields
    )
    batches = levels // (SUBS * BATCH)

    def pieces(i):
        for f in range(fields):
            rows = pl.ds((f * levels + i * BATCH * SUBS) * SUBS, BATCH * SUBS * SUBS)
            yield pltpu.make_async_copy(out_ref.at[rows], sent_ref.at[rows], sems.at[f * batches + i])

    def batch(i, halves):
        for u in range(BATCH):
            group = i * BATCH + u
            for y in range(SUBS):
                for f in range(fields):
                    out_ref[pl.ds(f * levels * SUBS + y + group * (SUBS * SUBS), SUBS, stride=SUBS), :] = settled(
                        f,
                        group,
                        y,
                        u * SUBS + y,
                        p_ref,
                        m_ref,
                        halves,
                        edge,
                        lambda f, y: coupled[f][y : y + 1, :],
                        up_n_ref,
                        lambda group: north_rim_ref[rows_of(0, group), :],
                        south,
                        north,
                        fields,
                        levels,
                    )
        for copy in pieces(i):
            copy.start()
        return tuple(pltpu.roll(h, LANES - BATCH * SUBS, 1) for h in halves)

    lax.fori_loop(1, batches, batch, batch(0, halves))
    for i in range(batches):
        for copy in pieces(i):
            copy.wait()


def params(limit=VMEM_LIMIT):
    return pltpu.CompilerParams(vmem_limit_bytes=limit)


def swaps(axis, start, closed):
    count = lax.axis_size(axis)
    pairs = []
    for i in range(start, count if closed else count - 1, 2):
        j = (i + 1) % count
        pairs += [(i, j), (j, i)]
    return pairs


def shards(innovations, obs_owner, obs_cell, velocity, diffusion, mixing, air_sea, sea_mask):
    lat_count = lax.axis_size("lat")
    lon_count = lax.axis_size("lon")
    owners = lat_count * lon_count
    steps, levels, lat_rows, lon_cols = (velocity.shape[i] for i in (1, 3, 4, 5))
    fields = mixing.shape[1]
    width = fields * levels
    count = innovations.shape[2]
    slots = 2
    assert (lat_rows, lon_cols, levels, count, owners, steps) == (SUBS, LANES, LANES, LANES, LANES, 3)
    f32 = functools.partial(jax.ShapeDtypeStruct, dtype=jnp.float32)
    stride = steps * slots * width // LANES + 1

    is_ocean = lax.axis_index("comp") == 1
    sea_float = sea_mask.astype(jnp.float32)
    mask = jnp.where(is_ocean, sea_float, jnp.ones_like(sea_float))
    opened = jnp.full((1, lon_cols), lax.axis_index("lat") < lat_count - 1, jnp.float32)
    smem = pl.BlockSpec(memory_space=pltpu.SMEM)
    vmem = pl.BlockSpec(memory_space=pltpu.VMEM)
    anywhere = pl.BlockSpec(memory_space=pltpu.HBM)
    speeds, diffuse = velocity[0], diffusion[0]

    north_rims = pl.pallas_call(
        rim_kernel,
        out_shape=f32((steps * levels, LANES)),
        in_specs=[anywhere] * 2,
        scratch_shapes=[pltpu.VMEM((steps, levels, LANES), jnp.float32)] * 2 + [pltpu.SemaphoreType.DMA((2,))],
        compiler_params=params(VMEM_WHOLE),
        name="rim",
    )(speeds, diffuse)
    north_rims = lax.ppermute(
        north_rims, "lat", [(i, i + 1) for i in range(lat_count - 1)]
    )

    north_rims = pl.pallas_call(
        copy_kernel,
        out_shape=f32((steps * levels, LANES)),
        compiler_params=params(),
        cost_estimate=pl.CostEstimate(flops=int(2e9), bytes_accessed=1 << 19, transcendentals=0),
        name="rims",
    )(north_rims)
    sent = pl.pallas_call(
        functools.partial(pack_kernel, slots),
        out_shape=f32((owners * stride, LANES)),
        in_specs=[anywhere] * 3,
        scratch_shapes=[
            pltpu.VMEM((steps, count, width), jnp.float32),
            pltpu.VMEM((steps, 1, count), jnp.int32),
            pltpu.VMEM((steps, 1, count), jnp.int32),
            pltpu.SemaphoreType.DMA((steps + 2,)),
        ],
        compiler_params=params(VMEM_WHOLE),
        name="pack",
    )(
        innovations[0],
        obs_owner.reshape(steps, 1, count),
        obs_cell.reshape(steps, 1, count),
    )
    got = lax.all_to_all(
        sent.reshape(owners, 1, stride * LANES), ("lat", "lon"), split_axis=0, concat_axis=0, tiled=True
    ).reshape(owners * stride, LANES)

    table = f32((levels * SUBS, LANES))
    *tables, east_rims, up_rims, mask_columns = pl.pallas_call(
        functools.partial(coefficient_kernel, steps, levels),
        out_shape=[table] * (4 * steps) + [f32((steps * SUBS, LANES))] * 2 + [f32((2 * SUBS, LANES))],
        compiler_params=params(),
        cost_estimate=pl.CostEstimate(flops=1 << 22, bytes_accessed=1 << 23, transcendentals=0),
        name="coefficients",
    )(
        speeds.reshape(steps * 2 * levels * SUBS, LANES),
        diffuse.reshape(steps * 2 * levels * SUBS, LANES),
        opened,
        mask,
    )
    odd = jnp.stack([lax.axis_index("lat") % 2, lax.axis_index("lon") % 2]).astype(jnp.int32)
    whole = f32((width * SUBS, LANES))
    half = f32((2 * fields * SUBS, LANES))
    low_shape = f32((fields * SUBS, LANES))
    message = [f32((width, LANES)), f32((width, LANES)), f32(((2 * fields + 1) * SUBS, LANES)), low_shape]
    busy = pl.CostEstimate(flops=1 << 25, bytes_accessed=1 << 23, transcendentals=0)

    m, *edges = pl.pallas_call(
        functools.partial(first_kernel, steps - 1, slots, fields, levels),
        out_shape=[whole, *message],
        in_specs=[smem] + [vmem] * 3,
        compiler_params=params(),
        name="first",
    )(odd, got, mask, east_rims)
    before = None
    for step in reversed(range(steps)):
        slab1, slab2, columns, low = edges
        halos = [
            lax.ppermute(slab1, "lat", swaps("lat", 0, False)),
            lax.ppermute(slab2, "lat", swaps("lat", 1, False)),
            lax.ppermute(columns, "lon", swaps("lon", 1, True)),
            lax.ppermute(columns, "lon", swaps("lon", 0, True)),
            lax.ppermute(low, "comp", [(0, 1)]),
        ]
        last = step == 0
        forcing = []
        if not last:
            forcing.append(
                pl.pallas_call(
                    functools.partial(forcing_kernel, step - 1, slots, width),
                    out_shape=whole,
                    compiler_params=params(),
                    cost_estimate=busy,
                    name="forcing",
                )(got)
            )
        step_tables = tables[4 * step : 4 * step + 4]
        if before is None:
            p, p_half = pl.pallas_call(
                functools.partial(start_kernel, step, fields, levels),
                out_shape=[whole, half],
                in_specs=[smem] * 2 + [vmem] * 6,
                compiler_params=params(),
                cost_estimate=busy,
                name="start",
            )(mixing[0], odd, m, *step_tables, *forcing)
        else:
            operands = [mixing[0], odd, *step_tables, *before, *forcing]
            m, p, *rest = pl.pallas_call(
                functools.partial(inner_kernel, last, step, fields, levels),
                out_shape=[whole, whole] + [half] * (not last),
                in_specs=[smem] * 2 + [vmem] * (len(operands) - 2),
                compiler_params=params(),
                cost_estimate=busy,
                name="inner",
            )(*operands)
            if not last:
                (p_half,) = rest
        if last:
            break
        operands = [
            air_sea,
            odd,
            p,
            p_half,
            m,
            step_tables[2],
            columns,
            east_rims,
            up_rims,
            north_rims,
            sea_float,
            mask,
            mask_columns,
            *halos,
        ]
        *edges, halves, coupled = pl.pallas_call(
            functools.partial(edge_kernel, step, fields, levels),
            out_shape=[*message, half, low_shape],
            in_specs=[smem] * 2 + [vmem] * (len(operands) - 2),
            scratch_shapes=[pltpu.VMEM((width * SUBS, LANES), jnp.float32)],
            compiler_params=params(),
            name="edge",
        )(*operands)
        before = [p, m, step_tables[2], halos[0], halos[1], halves, coupled, north_rims, mask]
    operands = [air_sea, odd, p, m, tables[2], columns, up_rims, north_rims, sea_float, *halos]
    m = pl.pallas_call(
        functools.partial(last_kernel, fields, levels),
        out_shape=whole,
        in_specs=[smem] * 2 + [vmem] * (len(operands) - 2),
        out_specs=anywhere,
        scratch_shapes=[
            pltpu.VMEM((width * SUBS, LANES), jnp.float32),
            pltpu.SemaphoreType.DMA((width // (BATCH * SUBS),)),
        ],
        compiler_params=params(),
        name="last",
    )(*operands)
    return m.reshape(1, fields, levels, lat_rows, lon_cols)


def solution(mesh):
    return jax.shard_map(
        shards,
        mesh=mesh,
        in_specs=(
            P("comp", None, ("lat", "lon"), None),
            P("comp", None, ("lat", "lon"), None),
            P("comp", None, ("lat", "lon")),
            P("comp", None, None, None, "lat", "lon"),
            P("comp", None, None, None, "lat", "lon"),
            P("comp", None, None),
            P(),
            P("lat", "lon"),
        ),
        out_specs=P("comp", None, None, "lat", "lon"),
        check_vma=False,
    )
```

```python
import functools

import jax
import jax.numpy as jnp
from jax import lax
from jax.experimental import pallas as pl
from jax.experimental.pallas import tpu as pltpu
from jax.sharding import PartitionSpec as P

LANES = 128
SUBS = 8
BATCH = 16
VMEM_LIMIT = 12 * 1024 * 1024
VMEM_WHOLE = 58 * 1024 * 1024


def split(x):
    high = x.astype(jnp.bfloat16)
    return [high, (x - high.astype(jnp.float32)).astype(jnp.bfloat16)]


def pack_kernel(slots, rows_hbm, owner_hbm, cell_hbm, out_ref, rows_ref, owner_ref, cell_ref, sems):
    steps, count, width = rows_ref.shape
    owners = count
    parts = width // LANES
    stride = out_ref.shape[0] // owners
    small = [
        pltpu.make_async_copy(owner_hbm, owner_ref, sems.at[steps]),
        pltpu.make_async_copy(cell_hbm, cell_ref, sems.at[steps + 1]),
    ]
    large = [
        pltpu.make_async_copy(rows_hbm.at[step], rows_ref.at[step], sems.at[step]) for step in range(steps)
    ]
    for copy in small + large:
        copy.start()
    dest = lax.broadcasted_iota(jnp.int32, (owners, count), 0)
    lane = lax.broadcasted_iota(jnp.int32, (owners, count), 1)
    before = (dest < lane).astype(jnp.bfloat16)
    cells = jnp.zeros((owners, LANES), jnp.float32)
    for copy in small:
        copy.wait()
    for step in range(steps):
        hits = owner_ref[step] == dest
        hits_f = hits.astype(jnp.float32)
        prior = jnp.dot(hits_f.astype(jnp.bfloat16), before, preferred_element_type=jnp.float32)
        large[step].wait()
        terms = jnp.concatenate(split(rows_ref[step]), axis=0)
        marks = (cell_ref[step] + 1).astype(jnp.float32)
        for k in range(slots):
            slot = step * slots + k
            pick = jnp.where(prior == float(k), hits_f, 0.0)
            pick_b = pick.astype(jnp.bfloat16)
            out = jnp.dot(
                jnp.concatenate([pick_b] * 2, axis=1), terms, preferred_element_type=jnp.float32
            )
            for part in range(parts):
                out_ref[pl.ds(slot * parts + part, owners, stride=stride), :] = out[
                    :, part * LANES : (part + 1) * LANES
                ]
            mark = jnp.sum(pick * marks, axis=1, keepdims=True)
            cells = jnp.where(lane == slot, mark, cells)
    out_ref[pl.ds(stride - 1, owners, stride=stride), :] = cells


def spread_rows(step, slots, got_ref, width):
    parts = width // LANES
    stride = parts * slots * 3 + 1
    sources = got_ref.shape[0] // stride
    marks = got_ref[pl.ds(stride - 1, sources, stride=stride), :]
    where_to = lax.broadcasted_iota(jnp.int32, (sources, SUBS * LANES), 1)
    terms, onehots = [], []
    for k in range(slots):
        slot = step * slots + k
        cols = []
        for part in range(parts):
            block = got_ref[pl.ds(slot * parts + part, sources, stride=stride), :]
            cols.append(block.T)
        turned = jnp.concatenate(cols, axis=0)
        terms += split(turned)
        cell = marks[:, slot : slot + 1].astype(jnp.int32) - 1
        onehot = (cell == where_to).astype(jnp.float32).astype(jnp.bfloat16)
        onehots += [onehot] * 2
    return jnp.dot(
        jnp.concatenate(terms, axis=1),
        jnp.concatenate(onehots, axis=0),
        preferred_element_type=jnp.float32,
    )


def column_halves(load, fields, groups, ys, halves):
    lane = lax.broadcasted_iota(jnp.int32, (SUBS, LANES), 1)
    for f in range(fields):
        for group in groups:
            for y in ys:
                at = group * SUBS + y
                plane = load(f, group, y)
                turned = plane if at == 0 else pltpu.roll(plane, at, 1)
                here = (lane == at) | (lane == (at - 1) % LANES)
                halves[2 * f + at % 2] = jnp.where(here, turned, halves[2 * f + at % 2])
    return halves


def columns_store(halves, rim, column_ref, fields):
    even = lax.broadcasted_iota(jnp.int32, (SUBS, LANES), 1) % 2 == 0
    for f in range(fields):
        a, b = halves[2 * f], halves[2 * f + 1]
        column_ref[f * SUBS : (f + 1) * SUBS, :] = jnp.where(even, a, b)
        column_ref[(fields + f) * SUBS : (fields + f + 1) * SUBS, :] = jnp.where(even, b, a)
    column_ref[2 * fields * SUBS :, :] = rim


def column_corrections(lon_even, first_ref, second_ref, own_ref, up_rim, fields):
    even = lax.broadcasted_iota(jnp.int32, (SUBS, LANES), 1) % 2 == 0

    def rows(i):
        one, two = first_ref[i * SUBS : (i + 1) * SUBS, :], second_ref[i * SUBS : (i + 1) * SUBS, :]
        return jnp.where(lon_even, one, two), jnp.where(lon_even, two, one)

    rim = pltpu.roll(rows(2 * fields)[0], 1, 1)
    halves = []
    for f in range(fields):
        from_west = pltpu.roll(rows(fields + f)[0], 1, 1)
        from_east = pltpu.roll(rows(f)[1], LANES - 1, 1)
        own_west = own_ref[f * SUBS : (f + 1) * SUBS, :]
        own_east = own_ref[(fields + f) * SUBS : (fields + f + 1) * SUBS, :]
        west = rim * (own_west - from_west)
        east = up_rim * (from_east - own_east)
        halves += [jnp.where(even, west, east), jnp.where(even, east, west)]
    return halves


def turn_to_first(col, at):
    return col if at == 0 else pltpu.roll(col, LANES - at, 1)


def rows_of(base, group):
    if isinstance(group, int):
        return pl.ds(base + group * SUBS, SUBS)
    return pl.ds(pl.multiple_of(base + group * SUBS, SUBS), SUBS)


def slabs_store(lat_even, m_ref, first_ref, second_ref, width):
    for i in range(width // SUBS):
        rows = slice(i * SUBS, (i + 1) * SUBS)
        south = m_ref[rows, :]
        north = m_ref[(SUBS - 1) * width + i * SUBS : (SUBS - 1) * width + (i + 1) * SUBS, :]
        first_ref[rows, :] = jnp.where(lat_even, north, south)
        second_ref[rows, :] = jnp.where(lat_even, south, north)


def parity(ref, i):
    return jnp.full((SUBS, LANES), ref[i], jnp.int32) == 0


def low_store(m_ref, low_ref, fields, levels):
    for f in range(fields):
        low_ref[f * SUBS : (f + 1) * SUBS, :] = m_ref[
            pl.ds(f * levels + levels - 1, SUBS, stride=fields * levels), :
        ]


def first_kernel(
    step, slots, fields, levels, odd_ref, got_ref, mask_ref, rim_ref, m_ref, slab1_ref, slab2_ref, column_ref, low_ref
):
    width = fields * levels
    out = spread_rows(step, slots, got_ref, width)
    for y in range(SUBS):
        m_ref[y * width : (y + 1) * width, :] = out[:, y * LANES : (y + 1) * LANES] * mask_ref[y : y + 1, :]
    slabs_store(parity(odd_ref, 0), m_ref, slab1_ref, slab2_ref, width)
    halves = column_halves(
        lambda f, group, y: m_ref[rows_of((y * fields + f) * levels, group), :],
        fields,
        range(levels // SUBS),
        range(SUBS),
        [jnp.zeros((SUBS, LANES), jnp.float32)] * (2 * fields),
    )
    columns_store(halves, rim_ref[step * SUBS : (step + 1) * SUBS, :], column_ref, fields)
    low_store(m_ref, low_ref, fields, levels)


def forcing_kernel(step, slots, width, got_ref, f_ref):
    out = spread_rows(step, slots, got_ref, width)
    for y in range(SUBS):
        f_ref[y * width : (y + 1) * width, :] = out[:, y * LANES : (y + 1) * LANES]


def copy_kernel(from_ref, to_ref):
    to_ref[...] = from_ref[...]


def rim_kernel(vel_ref, dif_ref, rim_ref, vel_row, dif_row, sems):
    copies = [
        pltpu.make_async_copy(src.at[:, 1, :, SUBS - 1, :], dst, sems.at[i])
        for i, (src, dst) in enumerate(((vel_ref, vel_row), (dif_ref, dif_row)))
    ]
    for copy in copies:
        copy.start()
    for copy in copies:
        copy.wait()
    steps, levels, lanes = vel_row.shape
    rim_ref[...] = (jnp.minimum(vel_row[...], 0.0) - dif_row[...]).reshape(steps * levels, lanes)


def coefficient_kernel(steps, levels, vel_ref, dif_ref, open_ref, mask_ref, *outs):
    tables, (rim_ref, up_rim_ref, mask_column_ref) = outs[:-3], outs[-3:]
    lane = lax.broadcasted_iota(jnp.int32, (SUBS, LANES), 1)
    tall = lax.broadcasted_iota(jnp.int32, (levels, LANES), 1)
    for step in range(steps):
        up_e_ref, down_w_ref, up_n_ref, down_n_ref = tables[4 * step : 4 * step + 4]
        east, north = 2 * step * levels * SUBS, (2 * step + 1) * levels * SUBS
        rim = jnp.zeros((SUBS, LANES), jnp.float32)
        up_rim = rim
        for y in range(SUBS):
            rows = slice(y * levels, (y + 1) * levels)
            w = vel_ref[pl.ds(east + y, levels, stride=SUBS), :]
            k = dif_ref[pl.ds(east + y, levels, stride=SUBS), :]
            up = jnp.maximum(w, 0.0) + k
            down = jnp.minimum(w, 0.0) - k
            for group in range(levels // SUBS):
                at = group * SUBS + y
                part = slice(group * SUBS, (group + 1) * SUBS)
                rim = jnp.where(lane == (at - 1) % LANES, pltpu.roll(down[part, :], at, 1) if at else down[part, :], rim)
                up_rim = jnp.where(lane == (at - 1) % LANES, pltpu.roll(up[part, :], at, 1) if at else up[part, :], up_rim)
            up_e_ref[rows, :] = jnp.where(tall == LANES - 1, 0.0, up)
            down_w_ref[rows, :] = jnp.where(tall == 0, 0.0, pltpu.roll(down, 1, 1))
            w = vel_ref[pl.ds(north + y, levels, stride=SUBS), :]
            k = dif_ref[pl.ds(north + y, levels, stride=SUBS), :]
            up = jnp.maximum(w, 0.0) + k
            up_n_ref[rows, :] = up * open_ref[...] if y == SUBS - 1 else up
            down_n_ref[rows, :] = jnp.minimum(w, 0.0) - k
        rim_ref[step * SUBS : (step + 1) * SUBS, :] = rim
        up_rim_ref[step * SUBS : (step + 1) * SUBS, :] = up_rim
    west, east = jnp.zeros((SUBS, LANES), jnp.float32), jnp.zeros((SUBS, LANES), jnp.float32)
    for group in range(levels // SUBS):
        for y in range(SUBS):
            at = group * SUBS + y
            row = jnp.broadcast_to(mask_ref[y : y + 1, :], (SUBS, LANES))
            turned = pltpu.roll(row, at, 1) if at else row
            west = jnp.where(lane == at, turned, west)
            east = jnp.where(lane == (at - 1) % LANES, turned, east)
    mask_column_ref[:SUBS, :] = west
    mask_column_ref[SUBS:, :] = east


def settled(f, group, y, at, p_ref, m_ref, halves, edge, coupled, up_n_ref, rim_row, from_south, from_north, fields, levels):
    rows = rows_of((y * fields + f) * levels, group)
    result = p_ref[rows, :] + jnp.where(edge, turn_to_first(halves[2 * f + at % 2], at), 0.0)
    if y == 0:
        result = result + rim_row(group) * (m_ref[rows, :] - from_south(f, group))
    if y == SUBS - 1:
        up = up_n_ref[rows_of(y * levels, group), :]
        result = result + up * (from_north(f, group) - m_ref[rows, :])
    if isinstance(group, int) and group == 0:
        sub = lax.broadcasted_iota(jnp.int32, (SUBS, LANES), 0)
        result = result + jnp.where(sub == 0, coupled(f, y), 0.0)
    return result


def slab_readers(lat_even, slab1_ref, slab2_ref, levels):
    def south(f, group):
        rows = rows_of(f * levels, group)
        return jnp.where(lat_even, slab2_ref[rows, :], slab1_ref[rows, :])

    def north(f, group):
        rows = rows_of(f * levels, group)
        return jnp.where(lat_even, slab1_ref[rows, :], slab2_ref[rows, :])

    return south, north


def coupling(air_ref, sea_ref, from_low_ref, fields):
    sea = sea_ref[...]
    planes = []
    for g in range(fields):
        total = jnp.zeros((SUBS, LANES), jnp.float32)
        for f in range(fields):
            total = total + air_ref[f, g] * from_low_ref[f * SUBS : (f + 1) * SUBS, :]
        planes.append(sea * total)
    return planes


def partial_kernel(settle, step, fields, levels, mix_ref, odd_ref, m_ref, tables, forcing_ref, before, outs):
    up_e_ref, down_w_ref, up_n_ref, down_n_ref = tables
    width = fields * levels
    lane = lax.broadcasted_iota(jnp.int32, (SUBS, LANES), 1)
    edge = (lane == 0) | (lane == LANES - 1)
    batches = levels // (SUBS * BATCH)
    if settle:
        old_p_ref, old_m_ref, old_up_n_ref, slab1_ref, slab2_ref, half_ref, couple_ref, rim_ref, mask_ref = before
        south, north = slab_readers(parity(odd_ref, 0), slab1_ref, slab2_ref, levels)

        def settle_batch(group0, halves):
            for u in range(BATCH):
                group = group0 + u
                for y in range(SUBS):
                    for f in range(fields):
                        plane = settled(
                            f,
                            group,
                            y,
                            u * SUBS + y,
                            old_p_ref,
                            old_m_ref,
                            halves,
                            edge,
                            lambda f, y: couple_ref[f * SUBS + y : f * SUBS + y + 1, :],
                            old_up_n_ref,
                            lambda group: rim_ref[rows_of((step + 1) * levels, group), :],
                            south,
                            north,
                            fields,
                            levels,
                        )
                        m_ref[rows_of((y * fields + f) * levels, group), :] = plane * mask_ref[y : y + 1, :]
            return tuple(pltpu.roll(h, LANES - BATCH * SUBS, 1) for h in halves)

        halves = settle_batch(0, [half_ref[i * SUBS : (i + 1) * SUBS, :] for i in range(2 * fields)])
        lax.fori_loop(1, batches, lambda i, halves: settle_batch(i * BATCH, halves), halves)
    p_ref = outs[0]
    mix = [[mix_ref[f, g] for g in range(fields)] for f in range(fields)]

    def body(i, carry):
        for u in range(BATCH):
            group = i * BATCH + u
            for y in range(SUBS):
                up_e = up_e_ref[rows_of(y * levels, group), :]
                down_w = down_w_ref[rows_of(y * levels, group), :]
                planes = [m_ref[rows_of(y * width + f * levels, group), :] for f in range(fields)]
                for g in range(fields):
                    m = planes[g]
                    rows = rows_of(y * width + g * levels, group)
                    result = m if forcing_ref is None else m + forcing_ref[rows, :]
                    for f in range(fields):
                        result = result + mix[f][g] * planes[f]
                    result = result + up_e * (pltpu.roll(m, LANES - 1, 1) - m)
                    result = result + down_w * (m - pltpu.roll(m, 1, 1))
                    if y < SUBS - 1:
                        up_n = up_n_ref[rows_of(y * levels, group), :]
                        result = result + up_n * (m_ref[rows_of((y + 1) * width + g * levels, group), :] - m)
                    if y > 0:
                        down_s = down_n_ref[rows_of((y - 1) * levels, group), :]
                        result = result + down_s * (m - m_ref[rows_of((y - 1) * width + g * levels, group), :])
                    p_ref[rows, :] = result
        return carry

    lax.fori_loop(0, batches, body, 0)
    if len(outs) > 1:
        halves = column_halves(
            lambda f, group, y: p_ref[rows_of((y * fields + f) * levels, group), :],
            fields,
            range(levels // SUBS),
            range(1, SUBS - 1),
            [jnp.zeros((SUBS, LANES), jnp.float32)] * (2 * fields),
        )
        for i, half in enumerate(halves):
            outs[1][i * SUBS : (i + 1) * SUBS, :] = half


def start_kernel(step, fields, levels, mix_ref, odd_ref, m_ref, a_ref, b_ref, c_ref, d_ref, f_ref, *outs):
    partial_kernel(False, step, fields, levels, mix_ref, odd_ref, m_ref, (a_ref, b_ref, c_ref, d_ref), f_ref, None, outs)


def inner_kernel(last, step, fields, levels, mix_ref, odd_ref, a_ref, b_ref, c_ref, d_ref, *rest):
    tables = (a_ref, b_ref, c_ref, d_ref)
    before, rest = rest[:9], rest[9:]
    f_ref = None
    if not last:
        f_ref, rest = rest[0], rest[1:]
    partial_kernel(True, step, fields, levels, mix_ref, odd_ref, rest[0], tables, f_ref, before, rest[1:])


def edge_kernel(
    step,
    fields,
    levels,
    air_ref,
    odd_ref,
    p_ref,
    p_half_ref,
    m_ref,
    up_n_ref,
    own_column_ref,
    rim_ref,
    up_rim_ref,
    north_rim_ref,
    sea_ref,
    mask_ref,
    mask_column_ref,
    from_slab1_ref,
    from_slab2_ref,
    from_column1_ref,
    from_column2_ref,
    from_low_ref,
    slab1_ref,
    slab2_ref,
    column_ref,
    low_ref,
    half_ref,
    couple_ref,
    next_ref,
):
    lane = lax.broadcasted_iota(jnp.int32, (SUBS, LANES), 1)
    edge = (lane == 0) | (lane == LANES - 1)
    even = lane % 2 == 0
    lat_even, lon_even = parity(odd_ref, 0), parity(odd_ref, 1)
    south, north = slab_readers(lat_even, from_slab1_ref, from_slab2_ref, levels)
    coupled = coupling(air_ref, sea_ref, from_low_ref, fields)
    for g in range(fields):
        couple_ref[g * SUBS : (g + 1) * SUBS, :] = coupled[g]
    halves = column_corrections(
        lon_even,
        from_column1_ref,
        from_column2_ref,
        own_column_ref,
        up_rim_ref[step * SUBS : (step + 1) * SUBS, :],
        fields,
    )
    for i, half in enumerate(halves):
        half_ref[i * SUBS : (i + 1) * SUBS, :] = half
    west, east = mask_column_ref[:SUBS, :], mask_column_ref[SUBS:, :]
    masks = [jnp.where(even, west, east), jnp.where(even, east, west)]
    following = [
        (p_half_ref[i * SUBS : (i + 1) * SUBS, :] + half) * masks[i % 2] for i, half in enumerate(halves)
    ]
    groups = levels // SUBS

    def plane(f, group, y):
        full = settled(
            f,
            group,
            y,
            group * SUBS + y,
            p_ref,
            m_ref,
            halves,
            edge,
            lambda f, y: coupled[f][y : y + 1, :],
            up_n_ref,
            lambda group: north_rim_ref[rows_of(step * levels, group), :],
            south,
            north,
            fields,
            levels,
        )
        return full * mask_ref[y : y + 1, :]

    for f in range(fields):
        for group in range(groups):
            for y in range(SUBS) if group in (0, groups - 1) else (0, SUBS - 1):
                next_ref[rows_of((y * fields + f) * levels, group), :] = plane(f, group, y)
    slabs_store(lat_even, next_ref, slab1_ref, slab2_ref, fields * levels)
    low_store(next_ref, low_ref, fields, levels)

    def load(f, group, y):
        return next_ref[rows_of((y * fields + f) * levels, group), :]

    following = column_halves(load, fields, range(groups), (0, SUBS - 1), following)
    following = column_halves(load, fields, (0,), range(1, SUBS - 1), following)
    columns_store(following, rim_ref[(step - 1) * SUBS : step * SUBS, :], column_ref, fields)


def last_kernel(
    fields,
    levels,
    air_ref,
    odd_ref,
    p_ref,
    m_ref,
    up_n_ref,
    own_column_ref,
    up_rim_ref,
    north_rim_ref,
    sea_ref,
    from_slab1_ref,
    from_slab2_ref,
    from_column1_ref,
    from_column2_ref,
    from_low_ref,
    sent_ref,
    out_ref,
    sems,
):
    lane = lax.broadcasted_iota(jnp.int32, (SUBS, LANES), 1)
    edge = (lane == 0) | (lane == LANES - 1)
    south, north = slab_readers(parity(odd_ref, 0), from_slab1_ref, from_slab2_ref, levels)
    coupled = coupling(air_ref, sea_ref, from_low_ref, fields)
    halves = column_corrections(
        parity(odd_ref, 1), from_column1_ref, from_column2_ref, own_column_ref, up_rim_ref[:SUBS, :], fields
    )
    batches = levels // (SUBS * BATCH)

    def pieces(i):
        for f in range(fields):
            rows = pl.ds((f * levels + i * BATCH * SUBS) * SUBS, BATCH * SUBS * SUBS)
            yield pltpu.make_async_copy(out_ref.at[rows], sent_ref.at[rows], sems.at[f * batches + i])

    def batch(i, halves):
        for u in range(BATCH):
            group = i * BATCH + u
            for y in range(SUBS):
                for f in range(fields):
                    out_ref[pl.ds(f * levels * SUBS + y + group * (SUBS * SUBS), SUBS, stride=SUBS), :] = settled(
                        f,
                        group,
                        y,
                        u * SUBS + y,
                        p_ref,
                        m_ref,
                        halves,
                        edge,
                        lambda f, y: coupled[f][y : y + 1, :],
                        up_n_ref,
                        lambda group: north_rim_ref[rows_of(0, group), :],
                        south,
                        north,
                        fields,
                        levels,
                    )
        for copy in pieces(i):
            copy.start()
        return tuple(pltpu.roll(h, LANES - BATCH * SUBS, 1) for h in halves)

    lax.fori_loop(1, batches, batch, batch(0, halves))
    for i in range(batches):
        for copy in pieces(i):
            copy.wait()


def params(limit=VMEM_LIMIT):
    return pltpu.CompilerParams(vmem_limit_bytes=limit)


def swaps(axis, start, closed):
    count = lax.axis_size(axis)
    pairs = []
    for i in range(start, count if closed else count - 1, 2):
        j = (i + 1) % count
        pairs += [(i, j), (j, i)]
    return pairs


def shards(innovations, obs_owner, obs_cell, velocity, diffusion, mixing, air_sea, sea_mask):
    lat_count = lax.axis_size("lat")
    lon_count = lax.axis_size("lon")
    owners = lat_count * lon_count
    steps, levels, lat_rows, lon_cols = (velocity.shape[i] for i in (1, 3, 4, 5))
    fields = mixing.shape[1]
    width = fields * levels
    count = innovations.shape[2]
    slots = 2
    assert (lat_rows, lon_cols, levels, count, owners, steps) == (SUBS, LANES, LANES, LANES, LANES, 3)
    f32 = functools.partial(jax.ShapeDtypeStruct, dtype=jnp.float32)
    stride = steps * slots * width // LANES + 1

    is_ocean = lax.axis_index("comp") == 1
    sea_float = sea_mask.astype(jnp.float32)
    mask = jnp.where(is_ocean, sea_float, jnp.ones_like(sea_float))
    opened = jnp.full((1, lon_cols), lax.axis_index("lat") < lat_count - 1, jnp.float32)
    smem = pl.BlockSpec(memory_space=pltpu.SMEM)
    vmem = pl.BlockSpec(memory_space=pltpu.VMEM)
    anywhere = pl.BlockSpec(memory_space=pltpu.HBM)
    speeds, diffuse = velocity[0], diffusion[0]

    north_rims = pl.pallas_call(
        rim_kernel,
        out_shape=f32((steps * levels, LANES)),
        in_specs=[anywhere] * 2,
        scratch_shapes=[pltpu.VMEM((steps, levels, LANES), jnp.float32)] * 2 + [pltpu.SemaphoreType.DMA((2,))],
        compiler_params=params(VMEM_WHOLE),
        name="rim",
    )(speeds, diffuse)
    north_rims = lax.ppermute(
        north_rims, "lat", [(i, i + 1) for i in range(lat_count - 1)]
    )

    north_rims = pl.pallas_call(
        copy_kernel,
        out_shape=f32((steps * levels, LANES)),
        compiler_params=params(),
        cost_estimate=pl.CostEstimate(flops=int(2e9), bytes_accessed=1 << 19, transcendentals=0),
        name="rims",
    )(north_rims)
    sent = pl.pallas_call(
        functools.partial(pack_kernel, slots),
        out_shape=f32((owners * stride, LANES)),
        in_specs=[anywhere] * 3,
        scratch_shapes=[
            pltpu.VMEM((steps, count, width), jnp.float32),
            pltpu.VMEM((steps, 1, count), jnp.int32),
            pltpu.VMEM((steps, 1, count), jnp.int32),
            pltpu.SemaphoreType.DMA((steps + 2,)),
        ],
        compiler_params=params(VMEM_WHOLE),
        name="pack",
    )(
        innovations[0],
        obs_owner.reshape(steps, 1, count),
        obs_cell.reshape(steps, 1, count),
    )
    got = lax.all_to_all(
        sent.reshape(owners, 1, stride * LANES), ("lat", "lon"), split_axis=0, concat_axis=0, tiled=True
    ).reshape(owners * stride, LANES)

    table = f32((levels * SUBS, LANES))
    *tables, east_rims, up_rims, mask_columns = pl.pallas_call(
        functools.partial(coefficient_kernel, steps, levels),
        out_shape=[table] * (4 * steps) + [f32((steps * SUBS, LANES))] * 2 + [f32((2 * SUBS, LANES))],
        compiler_params=params(),
        cost_estimate=pl.CostEstimate(flops=1 << 22, bytes_accessed=1 << 23, transcendentals=0),
        name="coefficients",
    )(
        speeds.reshape(steps * 2 * levels * SUBS, LANES),
        diffuse.reshape(steps * 2 * levels * SUBS, LANES),
        opened,
        mask,
    )
    odd = jnp.stack([lax.axis_index("lat") % 2, lax.axis_index("lon") % 2]).astype(jnp.int32)
    whole = f32((width * SUBS, LANES))
    half = f32((2 * fields * SUBS, LANES))
    low_shape = f32((fields * SUBS, LANES))
    message = [f32((width, LANES)), f32((width, LANES)), f32(((2 * fields + 1) * SUBS, LANES)), low_shape]
    busy = pl.CostEstimate(flops=1 << 25, bytes_accessed=1 << 23, transcendentals=0)

    m, *edges = pl.pallas_call(
        functools.partial(first_kernel, steps - 1, slots, fields, levels),
        out_shape=[whole, *message],
        in_specs=[smem] + [vmem] * 3,
        compiler_params=params(),
        name="first",
    )(odd, got, mask, east_rims)
    before = None
    for step in reversed(range(steps)):
        slab1, slab2, columns, low = edges
        halos = [
            lax.ppermute(slab1, "lat", swaps("lat", 0, False)),
            lax.ppermute(slab2, "lat", swaps("lat", 1, False)),
            lax.ppermute(columns, "lon", swaps("lon", 1, True)),
            lax.ppermute(columns, "lon", swaps("lon", 0, True)),
            lax.ppermute(low, "comp", [(0, 1)]),
        ]
        last = step == 0
        forcing = []
        if not last:
            forcing.append(
                pl.pallas_call(
                    functools.partial(forcing_kernel, step - 1, slots, width),
                    out_shape=whole,
                    compiler_params=params(),
                    cost_estimate=busy,
                    name="forcing",
                )(got)
            )
        step_tables = tables[4 * step : 4 * step + 4]
        if before is None:
            p, p_half = pl.pallas_call(
                functools.partial(start_kernel, step, fields, levels),
                out_shape=[whole, half],
                in_specs=[smem] * 2 + [vmem] * 6,
                compiler_params=params(),
                cost_estimate=busy,
                name="start",
            )(mixing[0], odd, m, *step_tables, *forcing)
        else:
            operands = [mixing[0], odd, *step_tables, *before, *forcing]
            m, p, *rest = pl.pallas_call(
                functools.partial(inner_kernel, last, step, fields, levels),
                out_shape=[whole, whole] + [half] * (not last),
                in_specs=[smem] * 2 + [vmem] * (len(operands) - 2),
                compiler_params=params(),
                cost_estimate=busy,
                name="inner",
            )(*operands)
            if not last:
                (p_half,) = rest
        if last:
            break
        operands = [
            air_sea,
            odd,
            p,
            p_half,
            m,
            step_tables[2],
            columns,
            east_rims,
            up_rims,
            north_rims,
            sea_float,
            mask,
            mask_columns,
            *halos,
        ]
        *edges, halves, coupled = pl.pallas_call(
            functools.partial(edge_kernel, step, fields, levels),
            out_shape=[*message, half, low_shape],
            in_specs=[smem] * 2 + [vmem] * (len(operands) - 2),
            scratch_shapes=[pltpu.VMEM((width * SUBS, LANES), jnp.float32)],
            compiler_params=params(),
            name="edge",
        )(*operands)
        before = [p, m, step_tables[2], halos[0], halos[1], halves, coupled, north_rims, mask]
    operands = [air_sea, odd, p, m, tables[2], columns, up_rims, north_rims, sea_float, *halos]
    m = pl.pallas_call(
        functools.partial(last_kernel, fields, levels),
        out_shape=whole,
        in_specs=[smem] * 2 + [vmem] * (len(operands) - 2),
        out_specs=anywhere,
        scratch_shapes=[
            pltpu.VMEM((width * SUBS, LANES), jnp.float32),
            pltpu.SemaphoreType.DMA((width // (BATCH * SUBS),)),
        ],
        compiler_params=params(),
        name="last",
    )(*operands)
    return m.reshape(1, fields, levels, lat_rows, lon_cols)


def solution(mesh):
    return jax.shard_map(
        shards,
        mesh=mesh,
        in_specs=(
            P("comp", None, ("lat", "lon"), None),
            P("comp", None, ("lat", "lon"), None),
            P("comp", None, ("lat", "lon")),
            P("comp", None, None, None, "lat", "lon"),
            P("comp", None, None, None, "lat", "lon"),
            P("comp", None, None),
            P(),
            P("lat", "lon"),
        ),
        out_specs=P("comp", None, None, "lat", "lon"),
        check_vma=False,
    )
```
